32 devices in a mesh: ctx: 8 (over z, y), grp: 4 (over x, core).
Axes of the slice: x: 2, y: 2, z: 4, core: 2. Of those that a mesh axis runs over, the one named last changes fastest.
Arguments:
- query_gate: bfloat16 [1024, 4096], P('ctx', 'grp'), may hold values from -6 to 6
- key_gate: bfloat16 [1024, 4096], P('ctx', 'grp'), may hold values from -6 to 6
- values: bfloat16 [1024, 4096], P('ctx', 'grp'), may hold values from -6 to 6
- upstream: bfloat16 [1024, 4096], P('ctx', 'grp'), may hold values from -6 to 6
- skip_weight: float32 [4096], P('grp'), may hold values from -3 to 3
- residues: float32 [256, 16], replicated, may hold values from -3 to 3
- log_rates: float32 [256, 16], replicated, as said below
Outputs:
- query_grad: bfloat16 [1024, 4096], P('ctx', 'grp')
- key_grad: bfloat16 [1024, 4096], P('ctx', 'grp')
- value_grad: bfloat16 [1024, 4096], P('ctx', 'grp')
- skip_grad: float32 [4096], P('grp')
- residue_grad: float32 [256, 16], replicated
- log_rate_grad: float32 [256, 16], replicated
The draws below stay inside these ranges and needn't reach their ends.
Inputs may be any that keep to these rules, and one draw needn't show every extreme that they name: `log_rates`: each entry is the natural logarithm of a rate between 1/4 and 1024/30.
All inputs are finite; a program needn't handle non-finite values.
Results may differ from the reference program's by a relative error of at most 0.0013.
Values sent between devices are 32-bit elements; how exact they have to be, the bound alone decides.
No kernel may reach another device: no remote copies, remote signals or barrier semaphores. Data moves between devices by JAX's collectives and lax.ppermute only.
A program may use at most 64 MiB of HBM per device.

```python
import math
import jax
import jax.numpy as jnp
from jax import lax

CH = 4096
GROUP_CH = 16
MODES = 16
FILTERS = 256
TOKENS = 1024


def draw_log_rates(key, part):
    pick_key, low_key, high_key = jax.random.split(key, 3)
    extent = (FILTERS, MODES)
    slow_share = 0.5
    chooser = jax.random.uniform(pick_key, extent, dtype=jnp.float32)
    slow_logs = jax.random.uniform(low_key, extent, dtype=jnp.float32, minval=math.log(0.25), maxval=math.log(2.3))
    fast_logs = jax.random.uniform(high_key, extent, dtype=jnp.float32, minval=math.log(2.3), maxval=math.log(TOKENS / 30.0))
    return jnp.where(chooser < slow_share, slow_logs, fast_logs).astype(jnp.float32)


def levels(rng, shape, cuts, least, largest):
    level = 1.0
    for position, shards_of in cuts:
        draws = jax.random.uniform(jax.random.fold_in(jax.random.fold_in(rng, 6), position), (shards_of,), jnp.float32, least / len(cuts), largest / len(cuts))
        level = level * jnp.repeat(jnp.exp(draws), shape[position] // shards_of).reshape((-1,) + (1,) * (len(shape) - 1 - position))
    return level


def centred(stream_key, shape, width, limit, pieces=(), kind=jnp.bfloat16):
    values = jax.random.normal(stream_key, shape, jnp.float32) * width
    if len(pieces) > 0:
        values = levels(stream_key, shape, pieces, -0.22, 0.18) * values
    return jnp.clip(values, min=-limit, max=limit).astype(kind)


def setup_inputs(seed: int = 0) -> dict:
    seeds = jax.random.split(jax.random.key(seed), 8)
    query_gate = centred(seeds[0], (TOKENS, CH), 1.0, 6.0, ((0, 8), (1, 4)))
    key_gate = centred(seeds[1], (TOKENS, CH), 1.0, 6.0, ((0, 8), (1, 4)))
    values = centred(seeds[2], (TOKENS, CH), 1.0, 6.0, ((0, 8), (1, 4)))
    upstream = centred(seeds[3], (TOKENS, CH), 1.0, 6.0, ((0, 8), (1, 4)))
    skip_weight = centred(seeds[4], (CH,), 0.5, 3.0, ((0, 4),), jnp.float32)
    residues = centred(seeds[5], (FILTERS, MODES), 0.5, 3.0, (), jnp.float32)
    log_rates = draw_log_rates(jax.random.fold_in(seeds[7], 71), 0)
    return {"query_gate": query_gate, "key_gate": key_gate, "values": values, "upstream": upstream, "skip_weight": skip_weight, "residues": residues, "log_rates": log_rates}


def reference(query_gate, key_gate, values, upstream, skip_weight, residues, log_rates):
    rates = jnp.exp(log_rates)
    scaled = residues * jnp.sqrt(rates / TOKENS)
    lag_steps = jnp.arange(TOKENS).astype(jnp.float32)
    decays = jnp.exp(-rates[None, :, :] * lag_steps[:, None, None] / TOKENS)
    filter_taps = jnp.einsum('fm,kfm->kf', scaled, decays)
    mixed = key_gate.astype(jnp.float32) * values.astype(jnp.float32)
    carried = upstream.astype(jnp.float32) * query_gate.astype(jnp.float32)
    period = 2 * TOKENS
    spec_taps = jnp.fft.rfft(filter_taps, n=period, axis=0)
    spec_channels = jnp.repeat(spec_taps, GROUP_CH, axis=1)
    spec_mixed = jnp.fft.rfft(mixed, n=period, axis=0)
    spec_carried = jnp.fft.rfft(carried, n=period, axis=0)
    convolved = jnp.fft.irfft(spec_mixed * spec_channels, n=period, axis=0)[:TOKENS]
    correlated = jnp.fft.irfft(spec_carried * jnp.conj(spec_channels), n=period, axis=0)[:TOKENS]
    cross_spec = (spec_carried * jnp.conj(spec_mixed)).reshape(-1, FILTERS, GROUP_CH).sum(axis=2)
    lag_grad = jnp.fft.irfft(cross_spec, n=period, axis=0)[:TOKENS]
    first_sum = jnp.einsum('kf,kfm->fm', lag_grad, decays)
    second_sum = jnp.einsum('kf,kfm->fm', lag_grad, decays * (lag_steps[:, None, None] / TOKENS))
    scale_root = jnp.sqrt(jnp.asarray(TOKENS, dtype=jnp.float32))
    query_grad = (upstream.astype(jnp.float32) * (convolved + skip_weight[None, :] * mixed)).astype(jnp.bfloat16)
    mixed_grad = correlated + skip_weight[None, :] * carried
    key_grad = (mixed_grad * values.astype(jnp.float32)).astype(jnp.bfloat16)
    value_grad = (mixed_grad * key_gate.astype(jnp.float32)).astype(jnp.bfloat16)
    skip_grad = lax.optimization_barrier(jnp.sum(carried * mixed, axis=0)) / scale_root
    residue_grad = jnp.sqrt(rates / TOKENS) * first_sum / scale_root
    log_rate_grad = scaled * (0.5 * first_sum - rates * second_sum) / scale_root
    return (query_grad, key_grad, value_grad, skip_grad, residue_grad, log_rate_grad)
```

```python
import functools

import jax
import jax.numpy as jnp
from jax import lax
from jax.experimental import pallas as pl
from jax.experimental.pallas import tpu as pltpu
from jax.sharding import PartitionSpec as P

GROUP_CH = 16
LANES = 128
SUB = 8
HIGHEST = lax.Precision.HIGHEST


def group_mask(filters, channels):
    row = lax.broadcasted_iota(jnp.int32, (filters, channels), 0)
    col = lax.broadcasted_iota(jnp.int32, (filters, channels), 1)
    return jnp.where(row == lax.div(col, GROUP_CH), 1.0, 0.0).astype(jnp.float32)


def per_channel(table, mask):
    return lax.dot_general(
        table, mask, (((0,), (0,)), ((), ())), precision=HIGHEST, preferred_element_type=jnp.float32
    )


def tile_rows(ref, ct):
    return ref[:, pl.ds(pl.multiple_of(ct * LANES, LANES), LANES)].astype(jnp.float32)


def spread(row):
    return jnp.broadcast_to(row, (SUB, LANES))


def sub_ends(x_ref, decay, steps, modes, reverse):
    order = range(steps - 1, -1, -1) if reverse else range(steps)
    state = None
    for i in order:
        x = x_ref[pl.ds(i, SUB, stride=steps), :]
        state = [x] * modes if state is None else [decay[m] * state[m] + x for m in range(modes)]
    return state


def states_kernel(full, log_rates, key, values, upstream, query, send, mixed_s, carried_s, rate_s):
    rows, channels = key.shape
    tiles = channels // LANES
    filters = channels // GROUP_CH
    modes = log_rates.shape[1]
    steps = rows // SUB
    parts = send.shape[0]
    position = lax.axis_index("ctx")
    group = lax.axis_index("grp")
    rates = jnp.exp(log_rates[pl.ds(pl.multiple_of(group * filters, filters), filters), :])
    scaled_rates = per_channel(rates, group_mask(filters, channels)) * (1.0 / full)
    for ct in range(tiles):
        rate_s[ct] = scaled_rates[:, ct * LANES : (ct + 1) * LANES]
    sub_index = lax.broadcasted_iota(jnp.int32, (SUB, LANES), 0).astype(jnp.float32)
    ahead = (SUB - 1 - sub_index) * float(steps)
    behind = sub_index * float(steps)

    def tile(ct, _):
        mixed = tile_rows(key, ct) * tile_rows(values, ct)
        carried = tile_rows(upstream, ct) * tile_rows(query, ct)
        mixed_s[...] = mixed
        carried_s[...] = carried
        rate = rate_s[ct]
        rate_rows = [spread(rate[m : m + 1, :]) for m in range(modes)]
        decay = [jnp.exp(-r) for r in rate_rows]
        ends = sub_ends(mixed_s, decay, steps, modes, False)
        forward = [
            jnp.sum(ends[m] * jnp.exp(-rate_rows[m] * ahead), axis=0, keepdims=True)
            for m in range(modes)
        ]
        starts = sub_ends(carried_s, decay, steps, modes, True)
        backward = [
            jnp.sum(starts[m] * jnp.exp(-rate_rows[m] * behind), axis=0, keepdims=True)
            for m in range(modes)
        ]
        forward = jnp.concatenate(forward, axis=0)
        backward = jnp.concatenate(backward, axis=0)
        skip = jnp.sum(mixed * carried, axis=0, keepdims=True)
        base = pl.multiple_of(ct * modes, modes)

        def place(part, _):
            send[part, pl.ds(base, modes), :] = jnp.where(part > position, forward, backward)
            send[part, pl.ds(tiles * modes + ct, 1), :] = skip
            return 0

        lax.fori_loop(0, parts, place, 0)
        return 0

    lax.fori_loop(0, tiles, tile, 0)


def grads_kernel(
    full,
    log_rates,
    residues,
    skip_weight,
    key,
    values,
    upstream,
    query,
    received,
    query_grad,
    key_grad,
    value_grad,
    skip_grad,
    sums,
    mixed_s,
    carried_s,
    conv_s,
    back_s,
    after_s,
    rate_s,
    scale_s,
    first_s,
    second_s,
):
    rows, channels = key.shape
    tiles = channels // LANES
    filters = channels // GROUP_CH
    modes = log_rates.shape[1]
    steps = rows // SUB
    parts = received.shape[0]
    position = lax.axis_index("ctx")
    group = lax.axis_index("grp")
    own = pl.ds(pl.multiple_of(group * filters, filters), filters)
    rates = jnp.exp(log_rates[own, :])
    mask = group_mask(filters, channels)
    scaled_rates = per_channel(rates, mask) * (1.0 / full)
    scaled = per_channel(residues[own, :] * jnp.sqrt(rates / full), mask)
    for ct in range(tiles):
        rate_s[ct] = scaled_rates[:, ct * LANES : (ct + 1) * LANES]
        scale_s[ct] = scaled[:, ct * LANES : (ct + 1) * LANES]
    sub_index = lax.broadcasted_iota(jnp.int32, (SUB, LANES), 0)

    skip_rows = pl.ds(tiles * modes, tiles)
    skip_total = lax.fori_loop(
        0, parts, lambda p, a: a + received[p, skip_rows, :], jnp.zeros((tiles, LANES), jnp.float32)
    )
    skip_grad[...] = skip_total / jnp.sqrt(jnp.float32(full))

    def tile(ct, _):
        mixed_s[...] = tile_rows(key, ct) * tile_rows(values, ct)
        carried_s[...] = tile_rows(upstream, ct) * tile_rows(query, ct)
        rate = rate_s[ct]
        scale = scale_s[ct]
        block_decay = jnp.exp(-rate * float(rows))
        base = pl.multiple_of(ct * modes, modes)

        def gather_in(j, acc):
            return jnp.where(j < position, acc * block_decay + received[j, pl.ds(base, modes), :], acc)

        def gather_back(n, acc):
            j = parts - 1 - n
            return jnp.where(j > position, acc * block_decay + received[j, pl.ds(base, modes), :], acc)

        zero = jnp.zeros((modes, LANES), jnp.float32)
        incoming = lax.fori_loop(0, parts, gather_in, zero)
        outgoing = lax.fori_loop(0, parts, gather_back, zero)

        half = modes // 2
        for lo in range(0, modes, half):
            rate_rows = [spread(rate[m : m + 1, :]) for m in range(lo, lo + half)]
            decay = [jnp.exp(-r) for r in rate_rows]
            scales = [spread(scale[m : m + 1, :]) for m in range(lo, lo + half)]
            ends = sub_ends(mixed_s, decay, steps, half, False)
            starts = sub_ends(carried_s, decay, steps, half, True)
            forward, backward = [], []
            for m in range(half):
                jump = jnp.exp(-rate_rows[m] * float(steps))
                jump2 = jump * jump
                jump4 = jump2 * jump2
                x = jnp.where(sub_index == 0, spread(incoming[lo + m : lo + m + 1, :]), pltpu.roll(ends[m], 1, 0))
                x = x + jnp.where(sub_index >= 1, jump, 0.0) * pltpu.roll(x, 1, 0)
                x = x + jnp.where(sub_index >= 2, jump2, 0.0) * pltpu.roll(x, 2, 0)
                x = x + jnp.where(sub_index >= 4, jump4, 0.0) * pltpu.roll(x, 4, 0)
                forward.append(x)
                y = jnp.where(
                    sub_index == SUB - 1, spread(outgoing[lo + m : lo + m + 1, :]), pltpu.roll(starts[m], SUB - 1, 0)
                )
                y = y + jnp.where(sub_index < SUB - 1, jump, 0.0) * pltpu.roll(y, SUB - 1, 0)
                y = y + jnp.where(sub_index < SUB - 2, jump2, 0.0) * pltpu.roll(y, SUB - 2, 0)
                y = y + jnp.where(sub_index < SUB - 4, jump4, 0.0) * pltpu.roll(y, SUB - 4, 0)
                backward.append(y)
            for i in range(steps - 1, -1, -1):
                c = carried_s[pl.ds(i, SUB, stride=steps), :]
                total = None
                for m in range(half):
                    after = decay[m] * backward[m]
                    after_s[i, m] = after
                    backward[m] = after + c
                    term = scales[m] * backward[m]
                    total = term if total is None else total + term
                if lo > 0:
                    total = total + back_s[pl.ds(i, SUB, stride=steps), :]
                back_s[pl.ds(i, SUB, stride=steps), :] = total
            first = [jnp.zeros((SUB, LANES), jnp.float32) for _ in range(half)]
            second = [jnp.zeros((SUB, LANES), jnp.float32) for _ in range(half)]
            for i in range(steps):
                x = mixed_s[pl.ds(i, SUB, stride=steps), :]
                c = carried_s[pl.ds(i, SUB, stride=steps), :]
                total = None
                for m in range(half):
                    forward[m] = decay[m] * forward[m] + x
                    term = scales[m] * forward[m]
                    total = term if total is None else total + term
                    first[m] = first[m] + c * forward[m]
                    second[m] = second[m] + after_s[i, m] * forward[m]
                if lo > 0:
                    total = total + conv_s[pl.ds(i, SUB, stride=steps), :]
                conv_s[pl.ds(i, SUB, stride=steps), :] = total
            first_s[ct, lo : lo + half, :] = jnp.concatenate(
                [jnp.sum(v, axis=0, keepdims=True) for v in first], axis=0
            )
            second_s[ct, lo : lo + half, :] = jnp.concatenate(
                [jnp.sum(v, axis=0, keepdims=True) for v in second], axis=0
            )
        lanes = pl.ds(pl.multiple_of(ct * LANES, LANES), LANES)
        weight = skip_weight[pl.ds(ct, 1), :]
        query_grad[:, lanes] = (
            tile_rows(upstream, ct) * (conv_s[...] + weight * mixed_s[...])
        ).astype(query_grad.dtype)
        mixed_grad = back_s[...] + weight * carried_s[...]
        key_grad[:, lanes] = (mixed_grad * tile_rows(values, ct)).astype(key_grad.dtype)
        value_grad[:, lanes] = (mixed_grad * tile_rows(key, ct)).astype(value_grad.dtype)
        return 0

    lax.fori_loop(0, tiles, tile, 0)

    def by_filter(ref):
        whole = jnp.concatenate([ref[ct] for ct in range(tiles)], axis=1)
        return lax.dot_general(
            whole, mask, (((1,), (1,)), ((), ())), precision=HIGHEST, preferred_element_type=jnp.float32
        )

    both = jnp.concatenate([by_filter(first_s), by_filter(second_s) * (1.0 / full)], axis=1)

    def place(p, _):
        sums[p] = both
        return 0

    lax.fori_loop(0, sums.shape[0], place, 0)


def local(query_gate, key_gate, values, upstream, skip_weight, residues, log_rates):
    context = lax.axis_size("ctx")
    groups = lax.axis_size("grp")
    rows, channels = query_gate.shape
    total_filters, modes = residues.shape
    filters = channels // GROUP_CH
    tiles = channels // LANES
    full = rows * context
    vmem = pl.BlockSpec(memory_space=pltpu.VMEM)
    f32 = jnp.float32
    chunk = tiles * modes + tiles
    params = pltpu.CompilerParams(vmem_limit_bytes=48 * 1024 * 1024)

    send = pl.pallas_call(
        functools.partial(states_kernel, full),
        out_shape=jax.ShapeDtypeStruct((context, chunk, LANES), f32),
        in_specs=[vmem] * 5,
        out_specs=vmem,
        scratch_shapes=[
            pltpu.VMEM((rows, LANES), f32),
            pltpu.VMEM((rows, LANES), f32),
            pltpu.VMEM((tiles, modes, LANES), f32),
        ],
        compiler_params=params,
        name="states",
    )(log_rates, key_gate, values, upstream, query_gate)
    received = lax.all_to_all(send, "ctx", split_axis=0, concat_axis=0, tiled=True)

    bf16 = jnp.bfloat16
    query_grad, key_grad, value_grad, skip_grad, sums = pl.pallas_call(
        functools.partial(grads_kernel, full),
        out_shape=(
            jax.ShapeDtypeStruct((rows, channels), bf16),
            jax.ShapeDtypeStruct((rows, channels), bf16),
            jax.ShapeDtypeStruct((rows, channels), bf16),
            jax.ShapeDtypeStruct((tiles, LANES), f32),
            jax.ShapeDtypeStruct((context * groups, modes, 2 * filters), f32),
        ),
        in_specs=[vmem] * 8,
        out_specs=(vmem,) * 5,
        scratch_shapes=[
            pltpu.VMEM((rows, LANES), f32),
            pltpu.VMEM((rows, LANES), f32),
            pltpu.VMEM((rows, LANES), f32),
            pltpu.VMEM((rows, LANES), f32),
            pltpu.VMEM((rows // SUB, modes // 2, SUB, LANES), f32),
            pltpu.VMEM((tiles, modes, LANES), f32),
            pltpu.VMEM((tiles, modes, LANES), f32),
            pltpu.VMEM((tiles, modes, LANES), f32),
            pltpu.VMEM((tiles, modes, LANES), f32),
        ],
        compiler_params=params,
        name="grads",
    )(
        log_rates,
        residues,
        skip_weight.reshape(tiles, LANES),
        key_gate,
        values,
        upstream,
        query_gate,
        received,
    )
    everyone = lax.all_to_all(sums, ("ctx", "grp"), split_axis=0, concat_axis=0, tiled=True)
    totals = everyone.reshape(context, groups, modes, 2, filters).sum(axis=0)
    first_sum = totals[:, :, 0].transpose(0, 2, 1).reshape(total_filters, modes)
    second_sum = totals[:, :, 1].transpose(0, 2, 1).reshape(total_filters, modes)
    rates = jnp.exp(log_rates)
    root = jnp.sqrt(rates / full)
    scale_root = jnp.sqrt(jnp.float32(full))
    residue_grad = root * first_sum / scale_root
    log_rate_grad = residues * root * (0.5 * first_sum - rates * second_sum) / scale_root
    return (query_grad, key_grad, value_grad, skip_grad.reshape(channels), residue_grad, log_rate_grad)


def solution(mesh):
    placed = (
        P("ctx", "grp"),
        P("ctx", "grp"),
        P("ctx", "grp"),
        P("ctx", "grp"),
        P("grp"),
        P(),
        P(),
    )
    return jax.shard_map(
        local,
        mesh=mesh,
        in_specs=placed,
        out_specs=(P("ctx", "grp"), P("ctx", "grp"), P("ctx", "grp"), P("grp"), P(), P()),
        check_vma=False,
    )
```

```python
import functools

import jax
import jax.numpy as jnp
from jax import lax
from jax.experimental import pallas as pl
from jax.experimental.pallas import tpu as pltpu
from jax.sharding import PartitionSpec as P

GROUP_CH = 16
LANES = 128
SUB = 8
TILE_FILTERS = LANES // GROUP_CH
HIGHEST = lax.Precision.HIGHEST
F32 = jnp.float32
BF16 = jnp.bfloat16


def own_columns(table, filters):
    total = table.shape[1]
    start = lax.axis_index("grp") * filters
    return pltpu.roll(table, lax.rem(total - start, total), 1)[:, :filters]


def group_mask(filters, channels):
    row = lax.broadcasted_iota(jnp.int32, (filters, channels), 0)
    col = lax.broadcasted_iota(jnp.int32, (filters, channels), 1)
    return jnp.where(row == lax.div(col, GROUP_CH), 1.0, 0.0).astype(F32)


def per_channel(table, mask):
    return jnp.dot(table, mask, precision=HIGHEST, preferred_element_type=F32)


def split(x):
    high = x.astype(BF16)
    return high, (x - high.astype(F32)).astype(BF16)


def wide_dot(a_high, a_low, b_high, b_low):
    dot = functools.partial(jnp.dot, preferred_element_type=F32)
    return dot(a_high, b_high) + (dot(a_high, b_low) + dot(a_low, b_high))


def spread(row):
    return jnp.broadcast_to(row, (SUB, LANES))


def states_kernel(
    full,
    log_rates_h,
    key_h,
    values_h,
    upstream_h,
    query_h,
    states,
    decays,
    rate_out,
    mixed_out,
    carried_out,
    rates_s,
    key,
    values,
    upstream,
    query,
    weight_s,
    sems,
):
    rows, channels = key.shape
    tiles = channels // LANES
    filters = channels // GROUP_CH
    modes = log_rates_h.shape[0]
    copies = [
        pltpu.make_async_copy(src, dst, sems.at[n])
        for n, (src, dst) in enumerate(
            (
                (log_rates_h, rates_s),
                (key_h, key),
                (values_h, values),
                (upstream_h, upstream),
                (query_h, query),
            )
        )
    ]
    for copy in copies:
        copy.start()
    copies[0].wait()
    step_rates = own_columns(jnp.exp(rates_s[...]), filters) * (1.0 / full)
    channel_rates = per_channel(step_rates, group_mask(filters, channels))
    time = lax.broadcasted_iota(jnp.int32, (modes, rows), 1).astype(F32)
    back_time = float(rows - 1) - time
    for f in range(filters):
        rate = jnp.broadcast_to(step_rates[:, f : f + 1], (modes, rows))
        ct, place = f // TILE_FILTERS, pl.ds((f % TILE_FILTERS) * modes, modes)
        for n, high_low in enumerate((split(jnp.exp(-rate * back_time)), split(jnp.exp(-rate * time)))):
            weight_s[ct, 2 * n, place, :] = high_low[0]
            weight_s[ct, 2 * n + 1, place, :] = high_low[1]
    for ct in range(tiles):
        rate = channel_rates[:, ct * LANES : (ct + 1) * LANES]
        rate_out[ct] = rate
        decay = jnp.exp(-rate * float(rows))
        decays[ct * modes : (ct + 1) * modes, :] = decay
        decays[(tiles + ct) * modes : (tiles + ct + 1) * modes, :] = decay
    decays[2 * tiles * modes :, :] = jnp.ones((tiles, LANES), F32)
    lane_filter = lax.div(lax.broadcasted_iota(jnp.int32, (modes, LANES), 1), GROUP_CH)

    def fold(products):
        parts = [
            jnp.where(lane_filter == f, products[f * modes : (f + 1) * modes, :], 0.0)
            for f in range(TILE_FILTERS)
        ]
        while len(parts) > 1:
            parts = [a + b for a, b in zip(parts[::2], parts[1::2])]
        return parts[0]

    for copy in copies[1:]:
        copy.wait()
    for ct in range(tiles):
        lanes = slice(ct * LANES, (ct + 1) * LANES)
        mixed = key[:, lanes].astype(F32) * values[:, lanes].astype(F32)
        carried = upstream[:, lanes].astype(F32) * query[:, lanes].astype(F32)
        mixed_out[ct] = mixed
        carried_out[ct] = carried
        ahead = wide_dot(weight_s[ct, 0], weight_s[ct, 1], *split(mixed))
        behind = wide_dot(weight_s[ct, 2], weight_s[ct, 3], *split(carried))
        states[ct * modes : (ct + 1) * modes, :] = fold(ahead)
        states[(tiles + ct) * modes : (tiles + ct + 1) * modes, :] = fold(behind)
        states[2 * tiles * modes + ct : 2 * tiles * modes + ct + 1, :] = jnp.sum(
            mixed * carried, axis=0, keepdims=True
        )


def sub_ends(x_ref, ct, decay, steps, reverse):
    order = range(steps - 1, -1, -1) if reverse else range(steps)
    state = None
    for i in order:
        x = x_ref[ct, pl.ds(i, SUB, stride=steps), :]
        state = [x] * len(decay) if state is None else [d * s + x for d, s in zip(decay, state)]
    return state


def sub_starts(first, ends, jumps, reverse):
    index = lax.broadcasted_iota(jnp.int32, (SUB, LANES), 0)
    if reverse:
        index = SUB - 1 - index
    shift = lambda v, n: pltpu.roll(v, SUB - n if reverse else n, 0)
    out = []
    for m, (end, jump) in enumerate(zip(ends, jumps)):
        x = jnp.where(index == 0, 0.0 if first is None else spread(first[m : m + 1, :]), shift(end, 1))
        for n in (1, 2, 4):
            x = x + jnp.where(index >= n, jump, 0.0) * shift(x, n)
            jump = jump * jump
        out.append(x)
    return out


def local_kernel(begin, rate_ref, mixed_ref, carried_ref, sums, after_s):
    rows = mixed_ref.shape[1]
    modes = rate_ref.shape[1]
    steps = rows // SUB
    half = modes // 2
    index = lax.broadcasted_iota(jnp.int32, (SUB, LANES), 0).astype(F32)

    def tile(n, _):
        ct = begin + n
        rate = rate_ref[ct]
        for lo in range(0, modes, half):
            rate_rows = [spread(rate[m : m + 1, :]) for m in range(lo, lo + half)]
            decay = [jnp.exp(-r) for r in rate_rows]
            jumps = [jnp.exp(-r * float(steps)) for r in rate_rows]
            state = sub_starts(None, sub_ends(carried_ref, ct, decay, steps, True), jumps, True)
            tally = None
            for i in range(steps - 1, -1, -1):
                c = carried_ref[ct, pl.ds(i, SUB, stride=steps), :]
                after = [d * s for d, s in zip(decay, state)]
                for m in range(half):
                    after_s[i, m] = after[m]
                tally = after if tally is None else [d * t + a for d, t, a in zip(decay, tally, after)]
                state = [a + c for a in after]
            sums[n, 2 * modes + lo : 2 * modes + lo + half, :] = jnp.concatenate(
                [
                    jnp.sum(t * (d * jnp.exp(-r * (index * float(steps)))), axis=0, keepdims=True)
                    for t, d, r in zip(tally, decay, rate_rows)
                ],
                axis=0,
            )
            state = sub_starts(None, sub_ends(mixed_ref, ct, decay, steps, False), jumps, False)
            first = [jnp.zeros((SUB, LANES), F32)] * half
            second = [jnp.zeros((SUB, LANES), F32)] * half
            tally = None
            for i in range(steps):
                x = mixed_ref[ct, pl.ds(i, SUB, stride=steps), :]
                c = carried_ref[ct, pl.ds(i, SUB, stride=steps), :]
                state = [d * s + x for d, s in zip(decay, state)]
                first = [f + c * s for f, s in zip(first, state)]
                second = [f + after_s[i, m] * state[m] for m, f in enumerate(second)]
                tally = state if tally is None else [d * t + s for d, t, s in zip(decay, tally, state)]
            left = [jnp.exp(-r * ((SUB - 1 - index) * float(steps))) for r in rate_rows]
            for place, values in (
                (0, first),
                (modes, second),
                (3 * modes, [t * (d * e) for t, d, e in zip(tally, decay, left)]),
            ):
                sums[n, place + lo : place + lo + half, :] = jnp.concatenate(
                    [jnp.sum(v, axis=0, keepdims=True) for v in values], axis=0
                )
        return 0

    lax.fori_loop(0, sums.shape[0], tile, 0)


def cross_kernel(full, rows, skip_rows, rate_ref, own, edges, skip_total, *refs):
    *locals_, sums, skip_grad = refs
    tiles, modes, _ = rate_ref.shape
    half = tiles * modes
    filters = tiles * TILE_FILTERS
    skip_grad[...] = skip_total[pl.ds(skip_rows, tiles), :] / jnp.sqrt(jnp.float32(full))
    firsts, seconds = [], []
    done = 0
    for ref in locals_:
        for n in range(ref.shape[0]):
            ct = done + n
            rate = rate_ref[ct]
            at = slice(ct * modes, (ct + 1) * modes)
            far = slice(half + ct * modes, half + (ct + 1) * modes)
            incoming, outgoing = edges[at, :], edges[far, :]
            firsts.append(ref[n, 0:modes, :] + jnp.exp(-rate) * own[far, :] * incoming)
            seconds.append(
                ref[n, modes : 2 * modes, :]
                + incoming * ref[n, 2 * modes : 3 * modes, :]
                + outgoing * ref[n, 3 * modes : 4 * modes, :]
                + (float(rows) * jnp.exp(-rate * float(rows + 1))) * (incoming * outgoing)
            )
        done += ref.shape[0]
    mask = group_mask(filters, tiles * LANES)
    both = jnp.concatenate([jnp.concatenate(v, axis=1) for v in (firsts, seconds)], axis=0)
    summed = lax.dot_general(
        both, mask, (((1,), (1,)), ((), ())), precision=HIGHEST, preferred_element_type=F32
    )
    packed = jnp.concatenate([summed[:modes], summed[modes:] * (1.0 / full)], axis=1)

    def place(p, _):
        sums[p] = packed
        return 0

    lax.fori_loop(0, sums.shape[0], place, 0)


def grads_kernel(
    full,
    log_rates,
    residues,
    skip_weight,
    rate_ref,
    edges,
    mixed_ref,
    carried_ref,
    key,
    values,
    upstream,
    query_grad,
    key_grad,
    value_grad,
    conv_s,
    back_s,
    scale_s,
):
    tiles, rows, _ = mixed_ref.shape
    modes = rate_ref.shape[1]
    channels = tiles * LANES
    filters = channels // GROUP_CH
    steps = rows // SUB
    half = modes // 2
    rates = jnp.exp(own_columns(log_rates[...], filters))
    scaled = own_columns(residues[...], filters) * jnp.sqrt(rates / full)
    scaled = per_channel(scaled, group_mask(filters, channels))
    for ct in range(tiles):
        scale_s[ct] = scaled[:, ct * LANES : (ct + 1) * LANES]

    def tile(ct, _):
        rate = rate_ref[ct]
        scale = scale_s[ct]
        base = pl.multiple_of(ct * modes, modes)
        incoming = edges[pl.ds(base, modes), :]
        outgoing = edges[pl.ds(tiles * modes + base, modes), :]
        for lo in range(0, modes, half):
            rate_rows = [spread(rate[m : m + 1, :]) for m in range(lo, lo + half)]
            decay = [jnp.exp(-r) for r in rate_rows]
            jumps = [jnp.exp(-r * float(steps)) for r in rate_rows]
            scales = [spread(scale[m : m + 1, :]) for m in range(lo, lo + half)]
            for x_ref, edge, result, reverse in (
                (mixed_ref, incoming, conv_s, False),
                (carried_ref, outgoing, back_s, True),
            ):
                ends = sub_ends(x_ref, ct, decay, steps, reverse)
                state = sub_starts(edge[lo : lo + half, :], ends, jumps, reverse)
                for i in range(steps - 1, -1, -1) if reverse else range(steps):
                    x = x_ref[ct, pl.ds(i, SUB, stride=steps), :]
                    state = [d * s + x for d, s in zip(decay, state)]
                    terms = [g * s for g, s in zip(scales, state)]
                    if lo > 0:
                        terms.append(result[pl.ds(i, SUB, stride=steps), :])
                    result[pl.ds(i, SUB, stride=steps), :] = functools.reduce(jnp.add, terms)
        lanes = pl.ds(pl.multiple_of(ct * LANES, LANES), LANES)
        weight = skip_weight[pl.ds(ct, 1), :]
        query_grad[:, lanes] = (
            upstream[:, lanes].astype(F32) * (conv_s[...] + weight * mixed_ref[ct])
        ).astype(query_grad.dtype)
        mixed_grad = back_s[...] + weight * carried_ref[ct]
        key_grad[:, lanes] = (mixed_grad * values[:, lanes].astype(F32)).astype(key_grad.dtype)
        value_grad[:, lanes] = (mixed_grad * key[:, lanes].astype(F32)).astype(value_grad.dtype)
        return 0

    lax.fori_loop(0, tiles, tile, 0)


def final_kernel(full, groups, log_rates, residues, sums, residue_grad, log_rate_grad):
    modes = log_rates.shape[0]
    filters = sums.shape[2] // 2
    totals = []
    for g in range(groups):
        parts = [sums[p] for p in range(g, sums.shape[0], groups)]
        totals.append(functools.reduce(jnp.add, parts))
    first_sum = jnp.concatenate([t[:, :filters] for t in totals], axis=1)
    second_sum = jnp.concatenate([t[:, filters:] for t in totals], axis=1)
    rates = jnp.exp(log_rates[...])
    root = jnp.sqrt(rates / full)
    scale_root = jnp.sqrt(jnp.float32(full))
    residue_grad[...] = root * first_sum / scale_root
    log_rate_grad[...] = residues[...] * root * (0.5 * first_sum - rates * second_sum) / scale_root


def exchange(states, decays, rows_state):
    context = lax.axis_size("ctx")
    position = lax.axis_index("ctx")
    is_forward = lax.broadcasted_iota(jnp.int32, states.shape, 0) < rows_state
    edge_rows = 2 * rows_state
    edges = reach = None
    step = 1
    while step < context:
        upper = (position & step) != 0
        pairs = [(i, i ^ step) for i in range(context)]
        takes = (is_forward == upper)[:edge_rows]
        if 2 * step < context:
            other = lax.ppermute(states, "ctx", pairs)
            summed = jnp.where(is_forward == upper, states + decays * other, decays * states + other)
            skip = summed[edge_rows:]
        else:
            half = jnp.where(upper, states[rows_state:edge_rows], states[:rows_state])
            other = lax.ppermute(
                jnp.concatenate([half, states[edge_rows:]], axis=0), "ctx", pairs
            )
            skip = states[edge_rows:] + other[rows_state:]
            other = jnp.concatenate([other[:rows_state]] * 2, axis=0)
            summed = None
        other = other[:edge_rows]
        if edges is None:
            edges = jnp.where(takes, other, 0.0)
            reach = jnp.where(takes, decays[:edge_rows], 1.0)
        else:
            edges = edges + jnp.where(takes, reach * other, 0.0)
            reach = jnp.where(takes, reach * decays[:edge_rows], reach)
        decays = decays * decays
        states = summed
        step *= 2
    return edges, skip


def local(query_gate, key_gate, values, upstream, skip_weight, residues, log_rates):
    context = lax.axis_size("ctx")
    groups = lax.axis_size("grp")
    rows, channels = query_gate.shape
    total_filters, modes = residues.shape
    filters = channels // GROUP_CH
    tiles = channels // LANES
    full = rows * context
    rows_state = tiles * modes
    chunk = 2 * rows_state + tiles
    vmem = pl.BlockSpec(memory_space=pltpu.VMEM)
    anywhere = pl.BlockSpec(memory_space=pltpu.HBM)
    shape = jax.ShapeDtypeStruct
    params = pltpu.CompilerParams(vmem_limit_bytes=16 * 1024 * 1024)
    log_rates_t, residues_t = log_rates.T, residues.T

    states, decays, rate, mixed, carried = pl.pallas_call(
        functools.partial(states_kernel, full),
        out_shape=(
            shape((chunk, LANES), F32),
            shape((chunk, LANES), F32),
            shape((tiles, modes, LANES), F32),
            shape((tiles, rows, LANES), F32),
            shape((tiles, rows, LANES), F32),
        ),
        in_specs=[anywhere] * 5,
        out_specs=(vmem,) * 5,
        scratch_shapes=[
            pltpu.VMEM((modes, total_filters), F32),
            pltpu.VMEM((rows, channels), BF16),
            pltpu.VMEM((rows, channels), BF16),
            pltpu.VMEM((rows, channels), BF16),
            pltpu.VMEM((rows, channels), BF16),
            pltpu.VMEM((tiles, 4, TILE_FILTERS * modes, rows), BF16),
            pltpu.SemaphoreType.DMA((5,)),
        ],
        compiler_params=params,
        name="states",
    )(*(pltpu.with_memory_space_constraint(x, pltpu.HBM) for x in (log_rates_t, key_gate, values, upstream, query_gate)))

    edges, skip_total = exchange(states, decays, rows_state)

    pieces = 2
    share = tiles // pieces
    work = rows * channels * modes // pieces
    local_sums = [
        pl.pallas_call(
            functools.partial(local_kernel, n * share),
            out_shape=shape((share, 4 * modes, LANES), F32),
            in_specs=[vmem] * 3,
            out_specs=vmem,
            scratch_shapes=[pltpu.VMEM((rows // SUB, modes // 2, SUB, LANES), F32)],
            compiler_params=params,
            cost_estimate=pl.CostEstimate(
                flops=16 * work, transcendentals=0, bytes_accessed=8 * rows * channels // pieces
            ),
            name="within",
        )(rate, mixed, carried)
        for n in range(pieces)
    ]

    sums, skip_grad = pl.pallas_call(
        functools.partial(cross_kernel, full, rows, 0),
        out_shape=(shape((context * groups, modes, 2 * filters), F32), shape((tiles, LANES), F32)),
        in_specs=[vmem] * (4 + pieces),
        out_specs=(vmem,) * 2,
        compiler_params=params,
        name="across",
    )(rate, states, edges, skip_total, *local_sums)

    everyone = lax.all_to_all(sums, ("ctx", "grp"), split_axis=0, concat_axis=0, tiled=True)

    query_grad, key_grad, value_grad = pl.pallas_call(
        functools.partial(grads_kernel, full),
        out_shape=(shape((rows, channels), BF16),) * 3,
        in_specs=[vmem] * 10,
        out_specs=(vmem,) * 3,
        scratch_shapes=[
            pltpu.VMEM((rows, LANES), F32),
            pltpu.VMEM((rows, LANES), F32),
            pltpu.VMEM((tiles, modes, LANES), F32),
        ],
        compiler_params=params,
        cost_estimate=pl.CostEstimate(
            flops=12 * rows * channels * modes, transcendentals=0, bytes_accessed=20 * rows * channels
        ),
        name="grads",
    )(
        log_rates_t,
        residues_t,
        skip_weight.reshape(tiles, LANES),
        rate,
        edges,
        mixed,
        carried,
        key_gate,
        values,
        upstream,
    )

    residue_grad, log_rate_grad = pl.pallas_call(
        functools.partial(final_kernel, full, groups),
        out_shape=(shape((modes, total_filters), F32),) * 2,
        in_specs=[vmem] * 3,
        out_specs=(vmem,) * 2,
        compiler_params=params,
        name="final",
    )(log_rates_t, residues_t, everyone)
    return (
        query_grad,
        key_grad,
        value_grad,
        skip_grad.reshape(channels),
        residue_grad.T,
        log_rate_grad.T,
    )


def solution(mesh):
    placed = (
        P("ctx", "grp"),
        P("ctx", "grp"),
        P("ctx", "grp"),
        P("ctx", "grp"),
        P("grp"),
        P(),
        P(),
    )
    return jax.shard_map(
        local,
        mesh=mesh,
        in_specs=placed,
        out_specs=(P("ctx", "grp"), P("ctx", "grp"), P("ctx", "grp"), P("grp"), P(), P()),
        check_vma=False,
    )
```

```python
import functools

import jax
import jax.numpy as jnp
from jax import lax
from jax.experimental import pallas as pl
from jax.experimental.pallas import tpu as pltpu
from jax.sharding import PartitionSpec as P

GROUP_CH = 16
LANES = 128
SUB = 8
TILE_FILTERS = LANES // GROUP_CH
HIGHEST = lax.Precision.HIGHEST
F32 = jnp.float32
BF16 = jnp.bfloat16


def own_columns(table, filters):
    total = table.shape[1]
    start = lax.axis_index("grp") * filters
    return pltpu.roll(table, lax.rem(total - start, total), 1)[:, :filters]


def group_mask(filters, channels):
    row = lax.broadcasted_iota(jnp.int32, (filters, channels), 0)
    col = lax.broadcasted_iota(jnp.int32, (filters, channels), 1)
    return jnp.where(row == lax.div(col, GROUP_CH), 1.0, 0.0).astype(F32)


def per_channel(table, mask):
    return jnp.dot(table, mask, precision=HIGHEST, preferred_element_type=F32)


def split(x):
    high = x.astype(BF16)
    return high, (x - high.astype(F32)).astype(BF16)


def wide_dot(a_high, a_low, b_high, b_low):
    dot = functools.partial(jnp.dot, preferred_element_type=F32)
    return dot(a_high, b_high) + (dot(a_high, b_low) + dot(a_low, b_high))


def spread(row):
    return jnp.broadcast_to(row, (SUB, LANES))


def states_kernel(
    full,
    log_rates_h,
    key_h,
    values_h,
    upstream_h,
    query_h,
    states,
    decays,
    rate_out,
    mixed_out,
    carried_out,
    rates_s,
    key,
    values,
    upstream,
    query,
    weight_s,
    sems,
):
    rows, channels = key.shape
    tiles = channels // LANES
    filters = channels // GROUP_CH
    modes = log_rates_h.shape[0]
    copies = [
        pltpu.make_async_copy(src, dst, sems.at[n])
        for n, (src, dst) in enumerate(
            (
                (log_rates_h, rates_s),
                (key_h, key),
                (values_h, values),
                (upstream_h, upstream),
                (query_h, query),
            )
        )
    ]
    for copy in copies:
        copy.start()
    copies[0].wait()
    step_rates = own_columns(jnp.exp(rates_s[...]), filters) * (1.0 / full)
    channel_rates = per_channel(step_rates, group_mask(filters, channels))
    time = lax.broadcasted_iota(jnp.int32, (modes, rows), 1).astype(F32)
    back_time = float(rows - 1) - time
    for f in range(filters):
        rate = jnp.broadcast_to(step_rates[:, f : f + 1], (modes, rows))
        ct, place = f // TILE_FILTERS, pl.ds((f % TILE_FILTERS) * modes, modes)
        for n, high_low in enumerate((split(jnp.exp(-rate * back_time)), split(jnp.exp(-rate * time)))):
            weight_s[ct, 2 * n, place, :] = high_low[0]
            weight_s[ct, 2 * n + 1, place, :] = high_low[1]
    for ct in range(tiles):
        rate = channel_rates[:, ct * LANES : (ct + 1) * LANES]
        rate_out[ct] = rate
        decay = jnp.exp(-rate * float(rows))
        decays[ct * modes : (ct + 1) * modes, :] = decay
        decays[(tiles + ct) * modes : (tiles + ct + 1) * modes, :] = decay
    decays[2 * tiles * modes :, :] = jnp.ones((tiles, LANES), F32)
    lane_filter = lax.div(lax.broadcasted_iota(jnp.int32, (modes, LANES), 1), GROUP_CH)

    def fold(products):
        parts = [
            jnp.where(lane_filter == f, products[f * modes : (f + 1) * modes, :], 0.0)
            for f in range(TILE_FILTERS)
        ]
        while len(parts) > 1:
            parts = [a + b for a, b in zip(parts[::2], parts[1::2])]
        return parts[0]

    for copy in copies[1:]:
        copy.wait()
    for ct in range(tiles):
        lanes = slice(ct * LANES, (ct + 1) * LANES)
        mixed = key[:, lanes].astype(F32) * values[:, lanes].astype(F32)
        carried = upstream[:, lanes].astype(F32) * query[:, lanes].astype(F32)
        mixed_out[ct] = mixed
        carried_out[ct] = carried
        ahead = wide_dot(weight_s[ct, 0], weight_s[ct, 1], *split(mixed))
        behind = wide_dot(weight_s[ct, 2], weight_s[ct, 3], *split(carried))
        states[ct * modes : (ct + 1) * modes, :] = fold(ahead)
        states[(tiles + ct) * modes : (tiles + ct + 1) * modes, :] = fold(behind)
        states[2 * tiles * modes + ct : 2 * tiles * modes + ct + 1, :] = jnp.sum(
            mixed * carried, axis=0, keepdims=True
        )


def sub_ends(x_ref, ct, decay, steps, reverse):
    order = range(steps - 1, -1, -1) if reverse else range(steps)
    state = None
    for i in order:
        x = x_ref[ct, pl.ds(i, SUB, stride=steps), :]
        state = [x] * len(decay) if state is None else [d * s + x for d, s in zip(decay, state)]
    return state


def sub_starts(ends, jumps, reverse):
    index = lax.broadcasted_iota(jnp.int32, (SUB, LANES), 0)
    if reverse:
        index = SUB - 1 - index
    shift = lambda v, n: pltpu.roll(v, SUB - n if reverse else n, 0)
    out = []
    for end, jump in zip(ends, jumps):
        x = jnp.where(index == 0, 0.0, shift(end, 1))
        for n in (1, 2, 4):
            x = x + jnp.where(index >= n, jump, 0.0) * shift(x, n)
            jump = jump * jump
        out.append(x)
    return out


def local_kernel(begin, rate_ref, states, mixed_ref, carried_ref, sums, starts, after_s):
    tiles, rows, _ = mixed_ref.shape
    modes = rate_ref.shape[1]
    steps = rows // SUB
    half = modes // 2
    index = lax.broadcasted_iota(jnp.int32, (SUB, LANES), 0).astype(F32)

    def tile(n, _):
        ct = begin + n
        rate = rate_ref[ct]
        behind = states[pl.ds(pl.multiple_of((tiles + ct) * modes, modes), modes), :]
        sums[n, 4 * modes : 5 * modes, :] = jnp.exp(-rate) * behind
        sums[n, 5 * modes : 6 * modes, :] = float(rows) * jnp.exp(-rate * float(rows + 1))
        for lo in range(0, modes, half):
            rate_rows = [spread(rate[m : m + 1, :]) for m in range(lo, lo + half)]
            decay = [jnp.exp(-r) for r in rate_rows]
            jumps = [jnp.exp(-r * float(steps)) for r in rate_rows]
            state = sub_starts(sub_ends(carried_ref, ct, decay, steps, True), jumps, True)
            for m in range(half):
                starts[n, 1, lo + m] = state[m]
            tally = None
            for i in range(steps - 1, -1, -1):
                c = carried_ref[ct, pl.ds(i, SUB, stride=steps), :]
                after = [d * s for d, s in zip(decay, state)]
                for m in range(half):
                    after_s[i, m] = after[m]
                tally = after if tally is None else [d * t + a for d, t, a in zip(decay, tally, after)]
                state = [a + c for a in after]
            sums[n, 2 * modes + lo : 2 * modes + lo + half, :] = jnp.concatenate(
                [
                    jnp.sum(t * (d * jnp.exp(-r * (index * float(steps)))), axis=0, keepdims=True)
                    for t, d, r in zip(tally, decay, rate_rows)
                ],
                axis=0,
            )
            state = sub_starts(sub_ends(mixed_ref, ct, decay, steps, False), jumps, False)
            for m in range(half):
                starts[n, 0, lo + m] = state[m]
            first = [jnp.zeros((SUB, LANES), F32)] * half
            second = [jnp.zeros((SUB, LANES), F32)] * half
            tally = None
            for i in range(steps):
                x = mixed_ref[ct, pl.ds(i, SUB, stride=steps), :]
                c = carried_ref[ct, pl.ds(i, SUB, stride=steps), :]
                state = [d * s + x for d, s in zip(decay, state)]
                first = [f + c * s for f, s in zip(first, state)]
                second = [f + after_s[i, m] * state[m] for m, f in enumerate(second)]
                tally = state if tally is None else [d * t + s for d, t, s in zip(decay, tally, state)]
            left = [jnp.exp(-r * ((SUB - 1 - index) * float(steps))) for r in rate_rows]
            for place, values in (
                (0, first),
                (modes, second),
                (3 * modes, [t * (d * e) for t, d, e in zip(tally, decay, left)]),
            ):
                sums[n, place + lo : place + lo + half, :] = jnp.concatenate(
                    [jnp.sum(v, axis=0, keepdims=True) for v in values], axis=0
                )
        return 0

    lax.fori_loop(0, sums.shape[0], tile, 0)


def across_kernel(full, unit, decays, states, edges_in, reach, near, middle, far, *refs):
    *locals_, edges, skip_grad, packed = refs
    tiles = skip_grad.shape[0]
    half = (states.shape[0] - tiles) // 2
    modes = half // tiles
    place = lax.axis_index("ctx") // unit
    skip = states[2 * half :, :]
    for ref in (near, middle, far):
        skip = skip + ref[half:, :]
    skip_grad[...] = skip / jnp.sqrt(jnp.float32(full))
    sums = []
    ct = 0
    for ref in locals_:
        firsts, seconds = [], []
        for n in range(ref.shape[0]):
            at = slice(ct * modes, (ct + 1) * modes)
            up = slice(half + ct * modes, half + (ct + 1) * modes)
            decay = decays[at, :]
            incoming = outgoing = jnp.zeros((modes, LANES), F32)
            for k, other in ((1, near), (2, middle), (3, far)):
                partner = place ^ k
                apart = jnp.abs(place - partner)
                term = other[at, :]
                term = jnp.where(apart >= 2, term * decay, term)
                term = jnp.where(apart >= 3, term * decay, term)
                incoming = incoming + jnp.where(partner < place, term, 0.0)
                outgoing = outgoing + jnp.where(partner > place, term, 0.0)
            incoming = edges_in[at, :] + reach[at, :] * incoming
            outgoing = edges_in[up, :] + reach[up, :] * outgoing
            edges[at, :] = incoming
            edges[up, :] = outgoing
            part = [ref[n, p * modes : (p + 1) * modes, :] for p in range(6)]
            firsts.append(part[0] + part[4] * incoming)
            seconds.append(part[1] + incoming * (part[2] + part[5] * outgoing) + outgoing * part[3])
            ct += 1
        both = jnp.concatenate([jnp.concatenate(v, axis=1) for v in (firsts, seconds)], axis=0)
        channels = both.shape[1]
        high, rest = split(both)
        middle_part, low = split(both - high.astype(F32))
        stacked = jnp.concatenate([high, middle_part, low], axis=0)
        summed = lax.dot_general(
            stacked,
            group_mask(channels // GROUP_CH, channels).astype(BF16),
            (((1,), (1,)), ((), ())),
            preferred_element_type=F32,
        )
        sums.append(summed[: 2 * modes] + summed[2 * modes : 4 * modes] + summed[4 * modes :])
    packed[...] = jnp.concatenate(
        [v[:modes] for v in sums] + [v[modes:] * (1.0 / full) for v in sums], axis=1
    )


def grads_kernel(
    full,
    begin,
    aliased,
    log_rates,
    residues,
    skip_weight,
    rate_ref,
    edges,
    mixed_ref,
    carried_ref,
    starts,
    key,
    values,
    upstream,
    *refs,
):
    query_grad, key_grad, value_grad, conv_s, back_s, scale_s = refs[aliased:]
    tiles, rows, _ = mixed_ref.shape
    modes = rate_ref.shape[1]
    channels = tiles * LANES
    filters = channels // GROUP_CH
    steps = rows // SUB
    half = modes // 2
    rates = jnp.exp(own_columns(log_rates[...], filters))
    scaled = own_columns(residues[...], filters) * jnp.sqrt(rates / full)
    scaled = per_channel(scaled, group_mask(filters, channels))
    for ct in range(tiles):
        scale_s[ct] = scaled[:, ct * LANES : (ct + 1) * LANES]
    index = lax.broadcasted_iota(jnp.int32, (SUB, LANES), 0).astype(F32) * float(steps)
    back_index = float(rows - steps) - index

    def tile(n, _):
        ct = begin + n
        rate = rate_ref[ct]
        scale = scale_s[ct]
        base = pl.multiple_of(ct * modes, modes)
        incoming = edges[pl.ds(base, modes), :]
        outgoing = edges[pl.ds(tiles * modes + base, modes), :]
        for lo in range(0, modes, half):
            rate_rows = [spread(rate[m : m + 1, :]) for m in range(lo, lo + half)]
            decay = [jnp.exp(-r) for r in rate_rows]
            scales = [spread(scale[m : m + 1, :]) for m in range(lo, lo + half)]
            for way, (x_ref, edge, result, away) in enumerate(
                ((mixed_ref, incoming, conv_s, index), (carried_ref, outgoing, back_s, back_index))
            ):
                state = [
                    starts[n, way, lo + m] + jnp.exp(-r * away) * edge[lo + m : lo + m + 1, :]
                    for m, r in enumerate(rate_rows)
                ]
                for i in range(steps - 1, -1, -1) if way else range(steps):
                    x = x_ref[ct, pl.ds(i, SUB, stride=steps), :]
                    state = [d * s + x for d, s in zip(decay, state)]
                    terms = [g * s for g, s in zip(scales, state)]
                    if lo > 0:
                        terms.append(result[pl.ds(i, SUB, stride=steps), :])
                    result[pl.ds(i, SUB, stride=steps), :] = functools.reduce(jnp.add, terms)
        lanes = pl.ds(pl.multiple_of(n * LANES, LANES), LANES)
        weight = skip_weight[pl.ds(ct, 1), :]
        query_grad[:, lanes] = (
            upstream[:, lanes].astype(F32) * (conv_s[...] + weight * mixed_ref[ct])
        ).astype(query_grad.dtype)
        mixed_grad = back_s[...] + weight * carried_ref[ct]
        key_grad[:, lanes] = (mixed_grad * values[:, lanes].astype(F32)).astype(key_grad.dtype)
        value_grad[:, lanes] = (mixed_grad * key[:, lanes].astype(F32)).astype(value_grad.dtype)
        return 0

    lax.fori_loop(0, starts.shape[0], tile, 0)


def final_kernel(full, log_rates, residues, mine, theirs, residue_grad, log_rate_grad):
    modes, total_filters = log_rates.shape
    filters = mine.shape[1] // 2
    group = lax.axis_index("grp")
    by_distance = [mine[:modes, :], theirs[:modes, :], mine[modes:, :], theirs[modes:, :]]
    totals = []
    for g in range(total_filters // filters):
        total = by_distance[0]
        for k in range(1, 4):
            total = jnp.where((group ^ k) == g, by_distance[k], total)
        totals.append(total)
    first_sum = jnp.concatenate([t[:, :filters] for t in totals], axis=1)
    second_sum = jnp.concatenate([t[:, filters:] for t in totals], axis=1)
    rates = jnp.exp(log_rates[...])
    root = jnp.sqrt(rates / full)
    scale_root = jnp.sqrt(jnp.float32(full))
    residue_grad[...] = root * first_sum / scale_root
    log_rate_grad[...] = residues[...] * root * (0.5 * first_sum - rates * second_sum) / scale_root


def flip(x, step, axes="ctx"):
    return lax.ppermute(x, axes, [(i, i ^ step) for i in range(lax.axis_size(axes))])


def after(x, *others):
    return lax.optimization_barrier((x, *others))[0]


def local(query_gate, key_gate, values, upstream, skip_weight, residues, log_rates):
    context = lax.axis_size("ctx")
    groups = lax.axis_size("grp")
    position = lax.axis_index("ctx")
    rows, channels = query_gate.shape
    total_filters, modes = residues.shape
    filters = channels // GROUP_CH
    tiles = channels // LANES
    full = rows * context
    half = tiles * modes
    chunk = 2 * half + tiles
    vmem = pl.BlockSpec(memory_space=pltpu.VMEM)
    anywhere = pl.BlockSpec(memory_space=pltpu.HBM)
    shape = jax.ShapeDtypeStruct
    params = pltpu.CompilerParams(vmem_limit_bytes=16 * 1024 * 1024)
    log_rates_t, residues_t = log_rates.T, residues.T
    assert groups == 4 and context >= 4 and context & (context - 1) == 0

    inputs = (log_rates_t, key_gate, values, upstream, query_gate)
    states, decays, rate, mixed, carried = pl.pallas_call(
        functools.partial(states_kernel, full),
        out_shape=(
            shape((chunk, LANES), F32),
            shape((chunk, LANES), F32),
            shape((tiles, modes, LANES), F32),
            shape((tiles, rows, LANES), F32),
            shape((tiles, rows, LANES), F32),
        ),
        in_specs=[anywhere] * 5,
        out_specs=(vmem,) * 5,
        scratch_shapes=[
            pltpu.VMEM((modes, total_filters), F32),
            pltpu.VMEM((rows, channels), BF16),
            pltpu.VMEM((rows, channels), BF16),
            pltpu.VMEM((rows, channels), BF16),
            pltpu.VMEM((rows, channels), BF16),
            pltpu.VMEM((tiles, 4, TILE_FILTERS * modes, rows), BF16),
            pltpu.SemaphoreType.DMA((5,)),
        ],
        compiler_params=params,
        name="states",
    )(*(pltpu.with_memory_space_constraint(x, pltpu.HBM) for x in inputs))
    own_states = states

    pieces = 2
    share = tiles // pieces
    work = rows * channels * modes // pieces

    def within(n, rate):
        return pl.pallas_call(
            functools.partial(local_kernel, n * share),
            out_shape=(shape((share, 6 * modes, LANES), F32), shape((share, 2, modes, SUB, LANES), F32)),
            in_specs=[vmem] * 4,
            out_specs=(vmem,) * 2,
            scratch_shapes=[pltpu.VMEM((rows // SUB, modes // 2, SUB, LANES), F32)],
            compiler_params=params,
            cost_estimate=pl.CostEstimate(
                flops=16 * work, transcendentals=0, bytes_accessed=8 * rows * channels // pieces
            ),
            name="within",
        )(rate, own_states, mixed, carried)

    is_forward = lax.broadcasted_iota(jnp.int32, states.shape, 0) < half
    edges = jnp.zeros((2 * half, LANES), F32)
    reach = jnp.ones((2 * half, LANES), F32)
    inside = []
    step = 1
    while 4 * step < context:
        upper = (position & step) != 0
        other = flip(states, step)
        if step == 1:
            inside.append(within(0, rate))
            other = after(other, *inside[0])
        takes = (is_forward == upper)[: 2 * half]
        edges = edges + jnp.where(takes, reach * other[: 2 * half], 0.0)
        reach = jnp.where(takes, reach * decays[: 2 * half], reach)
        states = jnp.where(is_forward == upper, states + decays * other, decays * states + other)
        decays = decays * decays
        step *= 2
    sends = [
        jnp.concatenate(
            [jnp.where((position & bit) == 0, states[:half], states[half : 2 * half]), states[2 * half :]],
            axis=0,
        )
        for bit in (step, 2 * step)
    ]
    others = [flip(sends[1], 3 * step), flip(sends[1], 2 * step), flip(sends[0], step)]
    for n in range(len(inside), pieces):
        inside.append(within(n, after(rate, states)))

    edges, skip_grad, packed = pl.pallas_call(
        functools.partial(across_kernel, full, step),
        out_shape=(
            shape((2 * half, LANES), F32),
            shape((tiles, LANES), F32),
            shape((modes, 2 * filters), F32),
        ),
        in_specs=[vmem] * (7 + pieces),
        out_specs=(vmem,) * 3,
        compiler_params=params,
        name="across",
    )(decays, states, edges, reach, others[2], others[1], others[0], *(v[0] for v in inside))

    def grads(n, rate, before):
        part = pl.BlockSpec((rows, share * LANES), lambda i: (0, n))
        whole = lambda x: pl.BlockSpec(x.shape, lambda i: (0,) * x.ndim)
        operands = (
            log_rates_t,
            residues_t,
            skip_weight.reshape(tiles, LANES),
            rate,
            edges,
            mixed,
            carried,
            inside[n][1],
        )
        return pl.pallas_call(
            functools.partial(grads_kernel, full, n * share, len(before)),
            grid=(1,),
            out_shape=(shape((rows, channels), BF16),) * 3,
            in_specs=[whole(x) for x in operands] + [part] * 3 + [anywhere] * len(before),
            out_specs=(part,) * 3,
            scratch_shapes=[
                pltpu.VMEM((rows, LANES), F32),
                pltpu.VMEM((rows, LANES), F32),
                pltpu.VMEM((tiles, modes, LANES), F32),
            ],
            input_output_aliases={len(operands) + 3 + k: k for k in range(len(before))},
            compiler_params=params,
            cost_estimate=pl.CostEstimate(
                flops=8 * work, transcendentals=0, bytes_accessed=20 * rows * channels // pieces
            ),
            name="grads",
        )(*operands, key_gate, values, upstream, *before)

    outputs = grads(0, rate, ())
    bit = context // 4
    waits = outputs
    while bit >= 2:
        parts = [flip(packed, k * bit) for k in (3, 2, 1)]
        parts[0] = after(parts[0], *waits)
        waits = ()
        packed = packed + (parts[0] + parts[1] + parts[2])
        bit //= 4
    if bit == 1:
        packed = packed + flip(packed, 2)
    everyone = ("ctx", "grp")
    both = flip(packed, groups + 2, everyone), flip(packed, groups, everyone), flip(packed, 2, everyone)
    outputs = grads(1, after(rate, packed), outputs)
    both = (after(both[0], *outputs), *both[1:])
    mine = jnp.concatenate([packed + both[1], both[2] + both[0]], axis=0)
    theirs = flip(mine, 1, "grp")
    query_grad, key_grad, value_grad = outputs

    residue_grad, log_rate_grad = pl.pallas_call(
        functools.partial(final_kernel, full),
        out_shape=(shape((modes, total_filters), F32),) * 2,
        in_specs=[vmem] * 4,
        out_specs=(vmem,) * 2,
        compiler_params=params,
        name="final",
    )(log_rates_t, residues_t, mine, theirs)
    return (
        query_grad,
        key_grad,
        value_grad,
        skip_grad.reshape(channels),
        residue_grad.T,
        log_rate_grad.T,
    )


def solution(mesh):
    placed = (
        P("ctx", "grp"),
        P("ctx", "grp"),
        P("ctx", "grp"),
        P("ctx", "grp"),
        P("grp"),
        P(),
        P(),
    )
    return jax.shard_map(
        local,
        mesh=mesh,
        in_specs=placed,
        out_specs=(P("ctx", "grp"), P("ctx", "grp"), P("ctx", "grp"), P("grp"), P(), P()),
        check_vma=False,
    )
```

```python
import functools

import jax
import jax.numpy as jnp
from jax import lax
from jax.experimental import pallas as pl
from jax.experimental.pallas import tpu as pltpu
from jax.sharding import PartitionSpec as P

GROUP_CH = 16
LANES = 128
SUB = 8
TILE_FILTERS = LANES // GROUP_CH
HIGHEST = lax.Precision.HIGHEST
F32 = jnp.float32
BF16 = jnp.bfloat16


def own_columns(table, filters):
    total = table.shape[1]
    start = lax.axis_index("grp") * filters
    return pltpu.roll(table, lax.rem(total - start, total), 1)[:, :filters]


def group_mask(filters, channels):
    row = lax.broadcasted_iota(jnp.int32, (filters, channels), 0)
    col = lax.broadcasted_iota(jnp.int32, (filters, channels), 1)
    return jnp.where(row == lax.div(col, GROUP_CH), 1.0, 0.0).astype(F32)


def per_channel(table, mask):
    return jnp.dot(table, mask, precision=HIGHEST, preferred_element_type=F32)


def split(x):
    high = x.astype(BF16)
    return high, (x - high.astype(F32)).astype(BF16)


def wide_dot(a_high, a_low, b_high, b_low):
    dot = functools.partial(jnp.dot, preferred_element_type=F32)
    return dot(a_high, b_high) + (dot(a_high, b_low) + dot(a_low, b_high))


def spread(row):
    return jnp.broadcast_to(row, (SUB, LANES))


def sub_ends(x_ref, ct, decay, steps, reverse):
    order = range(steps - 1, -1, -1) if reverse else range(steps)
    state = None
    for i in order:
        x = x_ref[ct, pl.ds(i, SUB, stride=steps), :]
        state = [x] * len(decay) if state is None else [d * s + x for d, s in zip(decay, state)]
    return state


def sub_starts(ends, jumps, reverse):
    index = lax.broadcasted_iota(jnp.int32, (SUB, LANES), 0)
    if reverse:
        index = SUB - 1 - index
    shift = lambda v, n: pltpu.roll(v, SUB - n if reverse else n, 0)
    out = []
    for end, jump in zip(ends, jumps):
        x = jnp.where(index == 0, 0.0, shift(end, 1))
        for n in (1, 2, 4):
            x = x + jnp.where(index >= n, jump, 0.0) * shift(x, n)
            jump = jump * jump
        out.append(x)
    return out


def fold_modes(products, modes):
    lane_filter = lax.div(lax.broadcasted_iota(jnp.int32, (modes, LANES), 1), GROUP_CH)
    parts = [
        jnp.where(lane_filter == f, products[f * modes : (f + 1) * modes, :], 0.0)
        for f in range(TILE_FILTERS)
    ]
    while len(parts) > 1:
        parts = [a + b for a, b in zip(parts[::2], parts[1::2])]
    return parts[0]


def states_kernel(
    full,
    log_rates_h,
    key_h,
    values_h,
    upstream_h,
    query_h,
    states,
    rate_out,
    mixed_out,
    carried_out,
    skip_out,
    rates_s,
    key,
    values,
    upstream,
    query,
    weight_s,
    sems,
):
    rows, channels = key.shape
    tiles = channels // LANES
    filters = channels // GROUP_CH
    modes = log_rates_h.shape[0]
    part = tiles // 2 * modes
    wide = TILE_FILTERS * modes
    copies = [
        pltpu.make_async_copy(src, dst, sems.at[n])
        for n, (src, dst) in enumerate(
            (
                (log_rates_h, rates_s),
                (key_h, key),
                (values_h, values),
                (upstream_h, upstream),
                (query_h, query),
            )
        )
    ]
    for copy in copies:
        copy.start()
    copies[0].wait()
    step_rates = own_columns(jnp.exp(rates_s[...]), filters) * (1.0 / full)
    channel_rates = per_channel(step_rates, group_mask(filters, channels))
    time = lax.broadcasted_iota(jnp.int32, (modes, rows), 1).astype(F32)
    back_time = float(rows - 1) - time
    for f in range(filters):
        rate = jnp.broadcast_to(step_rates[:, f : f + 1], (modes, rows))
        ct, row = f // TILE_FILTERS, (f % TILE_FILTERS) * modes
        for way, away in enumerate((back_time, time)):
            weight = jnp.exp(-rate * away)
            for n, high_low in enumerate((split(weight), split(weight * away))):
                at = slice(n * wide + row, n * wide + row + modes)
                weight_s[ct, 2 * way, at, :] = high_low[0]
                weight_s[ct, 2 * way + 1, at, :] = high_low[1]
    for ct in range(tiles):
        rate_out[ct] = channel_rates[:, ct * LANES : (ct + 1) * LANES]
    for copy in copies[1:]:
        copy.wait()
    for ct in range(tiles):
        lanes = slice(ct * LANES, (ct + 1) * LANES)
        mixed = key[:, lanes].astype(F32) * values[:, lanes].astype(F32)
        carried = upstream[:, lanes].astype(F32) * query[:, lanes].astype(F32)
        mixed_out[ct] = mixed
        carried_out[ct] = carried
        base = ct // (tiles // 2) * 4 * part + ct % (tiles // 2) * modes
        for way, x in enumerate((mixed, carried)):
            products = wide_dot(weight_s[ct, 2 * way], weight_s[ct, 2 * way + 1], *split(x))
            for n in range(2):
                at = base + (2 * way + n) * part
                states[at : at + modes, :] = fold_modes(products[n * wide : (n + 1) * wide], modes)
        skip_out[ct : ct + 1, :] = jnp.sum(mixed * carried, axis=0, keepdims=True)


def by_filter(firsts, seconds, first_filter, filters):
    modes = firsts[0].shape[0]
    both = jnp.concatenate([jnp.concatenate(v, axis=1) for v in (firsts, seconds)], axis=0)
    channels = both.shape[1]
    row = lax.broadcasted_iota(jnp.int32, (filters, channels), 0)
    col = lax.broadcasted_iota(jnp.int32, (filters, channels), 1)
    mask = jnp.where(row == first_filter + lax.div(col, GROUP_CH), 1.0, 0.0).astype(BF16)
    high, rest = split(both)
    middle, low = split(both - high.astype(F32))
    summed = lax.dot_general(
        jnp.concatenate([high, middle, low], axis=0),
        mask,
        (((1,), (1,)), ((), ())),
        preferred_element_type=F32,
    )
    summed = summed[: 2 * modes] + summed[2 * modes : 4 * modes] + summed[4 * modes :]
    return jnp.concatenate([summed[:modes], summed[modes:]], axis=1)


def within_kernel(rate_ref, mixed_ref, carried_ref, skip, sums, starts, after_s, first_s, second_s):
    tiles, rows, _ = mixed_ref.shape
    modes = rate_ref.shape[1]
    steps = rows // SUB
    half = modes // 2

    def tile(ct, _):
        rate = rate_ref[ct]
        for lo in range(0, modes, half):
            rate_rows = [spread(rate[m : m + 1, :]) for m in range(lo, lo + half)]
            decay = [jnp.exp(-r) for r in rate_rows]
            jumps = [jnp.exp(-r * float(steps)) for r in rate_rows]
            state = sub_starts(sub_ends(carried_ref, ct, decay, steps, True), jumps, True)
            for m in range(half):
                starts[ct, 1, lo + m] = state[m]
            for i in range(steps - 1, -1, -1):
                c = carried_ref[ct, pl.ds(i, SUB, stride=steps), :]
                state = [d * s for d, s in zip(decay, state)]
                for m in range(half):
                    after_s[i, m] = state[m]
                state = [a + c for a in state]
            state = sub_starts(sub_ends(mixed_ref, ct, decay, steps, False), jumps, False)
            for m in range(half):
                starts[ct, 0, lo + m] = state[m]
            first = [jnp.zeros((SUB, LANES), F32)] * half
            second = [jnp.zeros((SUB, LANES), F32)] * half
            for i in range(steps):
                x = mixed_ref[ct, pl.ds(i, SUB, stride=steps), :]
                c = carried_ref[ct, pl.ds(i, SUB, stride=steps), :]
                state = [d * s + x for d, s in zip(decay, state)]
                first = [f + c * s for f, s in zip(first, state)]
                second = [f + after_s[i, m] * state[m] for m, f in enumerate(second)]
            for ref, values in ((first_s, first), (second_s, second)):
                ref[ct, lo : lo + half, :] = jnp.concatenate(
                    [jnp.sum(v, axis=0, keepdims=True) for v in values], axis=0
                )
        return 0

    lax.fori_loop(0, tiles, tile, 0)
    packet = by_filter(
        [first_s[ct] for ct in range(tiles)],
        [second_s[ct] for ct in range(tiles)],
        0,
        tiles * TILE_FILTERS,
    )
    sums[:modes, :] = packet
    sums[modes:, :] = skip[...]


def spans_join(own, other, rate, upper, span):
    low = [jnp.where(upper, o, w) for w, o in zip(own, other)]
    high = [jnp.where(upper, w, o) for w, o in zip(own, other)]
    decay = jnp.exp(-rate)
    first = decay * (low[0] * high[2])
    second = decay * (low[1] * high[2] + low[0] * (high[2] + high[3]))
    far = jnp.exp(-rate * float(span))
    joined = (
        far * low[0] + high[0],
        far * (low[1] + float(span) * low[0]) + high[1],
        low[2] + far * high[2],
        low[3] + far * (high[3] + float(span) * high[2]),
    )
    return joined, first, second


def border_sums(first, second, tiles, modes):
    cut = lambda v: [v[n * modes : (n + 1) * modes, :] for n in range(tiles // 2)]
    begin = (lax.axis_index("ctx") & 1) * (tiles // 2 * TILE_FILTERS)
    return by_filter(cut(first), cut(second), begin, tiles * TILE_FILTERS)


def half_rates(rate_ref):
    tiles, modes, _ = rate_ref.shape
    begin = (lax.axis_index("ctx") & 1) * (tiles // 2)
    return jnp.concatenate([rate_ref[begin + n] for n in range(tiles // 2)], axis=0)


def join_kernel(rows, step, is_last_next, rate_ref, own_ref, other_ref, *refs):
    tiles, modes, _ = rate_ref.shape
    part = tiles // 2 * modes
    if step == 1:
        sums_ref, joined_ref, borders_ref, *send = refs
        begin = (lax.axis_index("ctx") & 1) * (4 * part)
        own = [own_ref[pl.ds(pl.multiple_of(begin + q * part, part), part), :] for q in range(4)]
        sums = sums_ref[...]
    else:
        old_borders, joined_ref, borders_ref, *send = refs
        own = [own_ref[q * part : (q + 1) * part, :] for q in range(4)]
        sums = own_ref[4 * part :, :] + other_ref[4 * part :, :]
    other = [other_ref[q * part : (q + 1) * part, :] for q in range(4)]
    position = lax.axis_index("ctx")
    upper = (position & step) != 0
    rate = half_rates(rate_ref)
    joined, first, second = spans_join(own, other, rate, upper, rows * step)
    for q in range(4):
        joined_ref[q * part : (q + 1) * part, :] = joined[q]
    sums = jnp.concatenate([sums[:modes] + border_sums(first, second, tiles, modes), sums[modes:]], axis=0)
    joined_ref[4 * part :, :] = sums
    if step == 1:
        borders_ref[...] = jnp.zeros_like(borders_ref)
    else:
        borders_ref[...] = add_borders(
            rows, step, rate, [old_borders[:part, :], old_borders[part:, :]], other[0], other[2]
        )
    if is_last_next:
        next_upper = (position & (2 * step)) != 0
        for q in range(2):
            send[0][q * part : (q + 1) * part, :] = jnp.where(next_upper, joined[2 + q], joined[q])
        send[0][2 * part :, :] = sums


def add_borders(rows, step, rate, borders, forward, backward):
    position = lax.axis_index("ctx")
    upper = (position & step) != 0
    before = ((position & (step - 1)) >> 1).astype(F32) * float(2 * rows)
    behind = float(rows * (step - 2)) - before
    return jnp.concatenate(
        [
            borders[0] + jnp.where(upper, jnp.exp(-rate * before) * forward, 0.0),
            borders[1] + jnp.where(upper, 0.0, jnp.exp(-rate * behind) * backward),
        ],
        axis=0,
    )


def last_join_kernel(
    rows, step, rate_ref, own_ref, other_ref, borders_ref, states_ref, partner_ref, mine_ref, back_ref
):
    tiles, modes, _ = rate_ref.shape
    part = tiles // 2 * modes
    position = lax.axis_index("ctx")
    upper = (position & step) != 0
    rate = half_rates(rate_ref)
    own = [own_ref[q * part : (q + 1) * part, :] for q in range(4)]
    other = [other_ref[q * part : (q + 1) * part, :] for q in range(2)]
    _, first, second = spans_join(own, other + other, rate, upper, rows * step)
    packet = border_sums(first, second, tiles, modes)
    borders = add_borders(
        rows, step, rate, [borders_ref[:part, :], borders_ref[part:, :]], other[0], other[0]
    )
    incoming, outgoing = borders[:part], borders[part:]
    far = jnp.exp(-rate * float(rows))
    begin = (position & 1) * (4 * part)
    pick = lambda q: states_ref[pl.ds(pl.multiple_of(begin + q * part, part), part), :]
    second_block = (position & 1) != 0
    through = far * incoming
    across = far * outgoing
    for ref, is_second, forward, backward in (
        (mine_ref, second_block, partner_ref[:part, :], partner_ref[2 * part : 3 * part, :]),
        (back_ref, jnp.logical_not(second_block), pick(0), pick(2)),
    ):
        ref[:part, :] = jnp.where(is_second, through + forward, incoming)
        ref[part : 2 * part, :] = jnp.where(is_second, outgoing, across + backward)
        sums = own_ref[4 * part :, :] + other_ref[2 * part :, :]
        ref[2 * part : 2 * part + modes, :] = sums[:modes] + packet
        ref[2 * part + modes :, :] = sums[modes:]


def block_kernel(
    full, log_rates, residues, skip_weight, rate_ref, mixed_ref, carried_ref, starts, scales, results
):
    tiles, rows, _ = mixed_ref.shape
    modes = rate_ref.shape[1]
    filters = tiles * TILE_FILTERS
    steps = rows // SUB
    half = modes // 2
    scaled = own_columns(residues[...], filters) * jnp.sqrt(
        jnp.exp(own_columns(log_rates[...], filters)) / full
    )
    scaled = per_channel(scaled, group_mask(filters, tiles * LANES))
    for n in range(tiles):
        scales[n] = scaled[:, n * LANES : (n + 1) * LANES]

    def tile(ct, _):
        rate = rate_ref[ct]
        scale = scales[ct]
        weight = spread(skip_weight[pl.ds(ct, 1), :])
        for lo in range(0, modes, half):
            decay = [jnp.exp(-spread(rate[m : m + 1, :])) for m in range(lo, lo + half)]
            gains = [spread(scale[m : m + 1, :]) for m in range(lo, lo + half)]
            for way, x_ref in enumerate((mixed_ref, carried_ref)):
                state = [starts[ct, way, lo + m] for m in range(half)]
                for i in range(steps - 1, -1, -1) if way else range(steps):
                    at = pl.ds(i, SUB, stride=steps)
                    x = x_ref[ct, at, :]
                    state = [d * s + x for d, s in zip(decay, state)]
                    terms = [g * s for g, s in zip(gains, state)]
                    terms.append(results[ct, way, at, :] if lo > 0 else weight * x)
                    while len(terms) > 1:
                        odd = terms[len(terms) // 2 * 2 :]
                        terms = [a + b for a, b in zip(terms[::2], terms[1::2])] + odd
                    results[ct, way, at, :] = terms[0]
        return 0

    lax.fori_loop(0, tiles, tile, 0)


def grads_kernel(full, mine, theirs, rate_ref, scale_ref, results, key, values, upstream, *refs):
    query_grad, key_grad, value_grad, skip_grad = refs
    tiles, modes, _ = scale_ref.shape
    rows = key.shape[0]
    share = tiles // 2
    part = share * modes
    skip_rows = slice(2 * part + modes, 2 * part + modes + tiles)
    skip_grad[...] = (mine[skip_rows, :] + theirs[skip_rows, :]) / jnp.sqrt(jnp.float32(full))
    second_half = (lax.axis_index("ctx") & 1) != 0
    lane = lax.broadcasted_iota(jnp.int32, (modes, LANES), 1)
    own_mode = lax.broadcasted_iota(jnp.int32, (modes, LANES), 0) == lax.rem(lane, modes)
    lane_filter = lax.div(lane, GROUP_CH)
    time = lax.broadcasted_iota(jnp.int32, (rows, LANES), 0).astype(F32)

    def piece(p):
        is_mine = second_half if p else jnp.logical_not(second_half)
        for n in range(share):
            ct = p * share + n
            rate = rate_ref[ct]
            rate_row = jnp.sum(jnp.where(own_mode, rate, 0.0), axis=0, keepdims=True)
            parts = []
            for offset, away in ((0, time + 1.0), (part, float(rows) - time)):
                at = slice(offset + n * modes, offset + (n + 1) * modes)
                edge = scale_ref[ct] * jnp.where(is_mine, mine[at, :], theirs[at, :])
                spaced = jnp.concatenate(
                    [jnp.where(lane_filter == f, edge, 0.0) for f in range(TILE_FILTERS)], axis=0
                )
                parts.append(wide_dot(*split(jnp.exp(-rate_row * away)), *split(spaced)))
            lanes = slice(n * LANES, (n + 1) * LANES)
            query_grad[:, lanes] = (
                upstream[:, lanes].astype(F32) * (results[ct, 0] + parts[0])
            ).astype(query_grad.dtype)
            mixed_grad = results[ct, 1] + parts[1]
            key_grad[:, lanes] = (mixed_grad * values[:, lanes].astype(F32)).astype(key_grad.dtype)
            value_grad[:, lanes] = (mixed_grad * key[:, lanes].astype(F32)).astype(value_grad.dtype)

    for p in range(2):
        pl.when(pl.program_id(0) == p)(functools.partial(piece, p))


def final_kernel(full, log_rates, residues, *refs):
    *by_distance, residue_grad, log_rate_grad = refs
    total_filters = log_rates.shape[1]
    filters = by_distance[0].shape[1] // 2
    group = lax.axis_index("grp")
    by_distance = [ref[...] for ref in by_distance]
    totals = []
    for g in range(total_filters // filters):
        total = by_distance[0]
        for k in range(1, len(by_distance)):
            total = jnp.where((group ^ k) == g, by_distance[k], total)
        totals.append(total)
    first_sum = jnp.concatenate([t[:, :filters] for t in totals], axis=1)
    second_sum = jnp.concatenate([t[:, filters:] for t in totals], axis=1) * (1.0 / full)
    rates = jnp.exp(log_rates[...])
    root = jnp.sqrt(rates / full)
    scale_root = jnp.sqrt(jnp.float32(full))
    residue_grad[...] = root * first_sum / scale_root
    log_rate_grad[...] = residues[...] * root * (0.5 * first_sum - rates * second_sum) / scale_root


def flip(x, step, axis="ctx"):
    return lax.ppermute(x, axis, [(i, i ^ step) for i in range(lax.axis_size(axis))])


def after(x, *others):
    return lax.optimization_barrier((x, *others))[0]


def local(query_gate, key_gate, values, upstream, skip_weight, residues, log_rates):
    context = lax.axis_size("ctx")
    groups = lax.axis_size("grp")
    position = lax.axis_index("ctx")
    rows, channels = query_gate.shape
    total_filters, modes = residues.shape
    filters = channels // GROUP_CH
    tiles = channels // LANES
    full = rows * context
    part = tiles // 2 * modes
    tail = modes + tiles
    assert context >= 4 and context & (context - 1) == 0 and groups & (groups - 1) == 0
    vmem = pl.BlockSpec(memory_space=pltpu.VMEM)
    in_hbm = pl.BlockSpec(memory_space=pltpu.HBM)
    shape = lambda *dims: jax.ShapeDtypeStruct(dims, F32)
    params = pltpu.CompilerParams(vmem_limit_bytes=16 * 1024 * 1024)
    log_rates_t, residues_t = log_rates.T, residues.T

    def call(name, kernel, out_shape, operands, scratch=(), flops=0):
        return pl.pallas_call(
            kernel,
            out_shape=out_shape,
            in_specs=[vmem] * len(operands),
            out_specs=(vmem,) * len(out_shape),
            scratch_shapes=[pltpu.VMEM(dims, F32) for dims in scratch],
            compiler_params=params,
            cost_estimate=pl.CostEstimate(flops=flops, transcendentals=0, bytes_accessed=flops // 4),
            name=name,
        )(*operands)

    inputs = (log_rates_t, key_gate, values, upstream, query_gate)
    states, rate, mixed, carried, skip = pl.pallas_call(
        functools.partial(states_kernel, full),
        out_shape=(
            shape(8 * part, LANES),
            shape(tiles, modes, LANES),
            shape(tiles, rows, LANES),
            shape(tiles, rows, LANES),
            shape(tiles, LANES),
        ),
        in_specs=[in_hbm] * 5,
        out_specs=(vmem,) * 5,
        scratch_shapes=[
            pltpu.VMEM((modes, total_filters), F32),
            pltpu.VMEM((rows, channels), BF16),
            pltpu.VMEM((rows, channels), BF16),
            pltpu.VMEM((rows, channels), BF16),
            pltpu.VMEM((rows, channels), BF16),
            pltpu.VMEM((tiles, 4, 2 * TILE_FILTERS * modes, rows), BF16),
            pltpu.SemaphoreType.DMA((5,)),
        ],
        compiler_params=params,
        name="states",
    )(*(pltpu.with_memory_space_constraint(x, pltpu.HBM) for x in inputs))
    work = rows * channels * modes

    other_half = lax.dynamic_slice_in_dim(states, (1 - (position & 1)) * (4 * part), 4 * part, 0)
    partner = flip(other_half, 1)
    sums, starts = call(
        "within",
        within_kernel,
        (shape(tail, LANES), shape(tiles, 2, modes, SUB, LANES)),
        (rate, mixed, carried, skip),
        ((rows // SUB, modes // 2, SUB, LANES), (tiles, modes, LANES), (tiles, modes, LANES)),
        12 * work,
    )
    scale = results = None
    step = 1
    own, other, extra = states, after(partner, sums), (sums,)
    while 2 * step < context:
        is_last_next = 4 * step >= context
        own, borders, *send = call(
            "join",
            functools.partial(join_kernel, rows, step, is_last_next),
            (shape(4 * part + tail, LANES), shape(2 * part, LANES))
            + ((shape(2 * part + tail, LANES),) if is_last_next else ()),
            (rate, own, other, *extra),
        )
        other = flip(send[0] if send else own, 2 * step)
        if step == 1:
            scale, results = call(
                "block",
                functools.partial(block_kernel, full),
                (shape(tiles, modes, LANES), shape(tiles, 2, rows, LANES)),
                (
                    log_rates_t,
                    residues_t,
                    skip_weight.reshape(tiles, LANES),
                    after(rate, own),
                    mixed,
                    carried,
                    starts,
                ),
                (),
                8 * work,
            )
            other = after(other, results)
        extra = (borders,)
        step *= 2
    mine, back = call(
        "last_join",
        functools.partial(last_join_kernel, rows, step),
        (shape(2 * part + tail, LANES),) * 2,
        (rate, own, other, borders, states, partner),
    )
    theirs = flip(back, 1)

    packed = mine[2 * part : 2 * part + modes] + theirs[2 * part : 2 * part + modes]
    gathered = [flip(packed, k, "grp") for k in range(1, groups)]
    columns = pl.BlockSpec((rows, channels // 2), lambda i: (0, i))
    outputs = pl.pallas_call(
        functools.partial(grads_kernel, full),
        grid=(2,),
        out_shape=(jax.ShapeDtypeStruct((rows, channels), BF16),) * 3 + (shape(tiles, LANES),),
        in_specs=[vmem] * 5 + [columns] * 3,
        out_specs=(columns,) * 3 + (pl.BlockSpec((tiles, LANES), lambda i: (0, 0)),),
        compiler_params=params,
        cost_estimate=pl.CostEstimate(
            flops=4 * work, transcendentals=0, bytes_accessed=20 * rows * channels
        ),
        name="grads",
    )(mine, theirs, rate, scale, results, key_gate, values, upstream)
    query_grad, key_grad, value_grad, skip_grad = outputs
    gathered[0] = after(gathered[0], *outputs)
    residue_grad, log_rate_grad = call(
        "final",
        functools.partial(final_kernel, full),
        (shape(modes, total_filters),) * 2,
        (log_rates_t, residues_t, packed, *gathered),
    )
    return (
        query_grad,
        key_grad,
        value_grad,
        skip_grad.reshape(channels),
        residue_grad.T,
        log_rate_grad.T,
    )


def solution(mesh):
    placed = (
        P("ctx", "grp"),
        P("ctx", "grp"),
        P("ctx", "grp"),
        P("ctx", "grp"),
        P("grp"),
        P(),
        P(),
    )
    return jax.shard_map(
        local,
        mesh=mesh,
        in_specs=placed,
        out_specs=(P("ctx", "grp"), P("ctx", "grp"), P("ctx", "grp"), P("grp"), P(), P()),
        check_vma=False,
    )
```

```python
import functools

import jax
import jax.numpy as jnp
from jax import lax
from jax.experimental import pallas as pl
from jax.experimental.pallas import tpu as pltpu
from jax.sharding import PartitionSpec as P

GROUP_CH = 16
LANES = 128
SUB = 8
TILE_FILTERS = LANES // GROUP_CH
HIGHEST = lax.Precision.HIGHEST
F32 = jnp.float32
BF16 = jnp.bfloat16


def own_columns(table, filters):
    total = table.shape[1]
    start = lax.axis_index("grp") * filters
    return pltpu.roll(table, lax.rem(total - start, total), 1)[:, :filters]


def group_mask(filters, channels):
    row = lax.broadcasted_iota(jnp.int32, (filters, channels), 0)
    col = lax.broadcasted_iota(jnp.int32, (filters, channels), 1)
    return jnp.where(row == lax.div(col, GROUP_CH), 1.0, 0.0).astype(F32)


def per_channel(table, mask):
    return jnp.dot(table, mask, precision=HIGHEST, preferred_element_type=F32)


def split(x):
    high = x.astype(BF16)
    return high, (x - high.astype(F32)).astype(BF16)


def wide_dot(a_high, a_low, b_high, b_low):
    return jnp.dot(
        jnp.concatenate([a_high, a_low, a_high], axis=1),
        jnp.concatenate([b_high, b_high, b_low], axis=0),
        preferred_element_type=F32,
    )


def spread(row):
    return jnp.broadcast_to(row, (SUB, LANES))


def sub_starts_back(ends, jumps):
    index = SUB - 1 - lax.broadcasted_iota(jnp.int32, (SUB, LANES), 0)
    out = []
    for end, jump in zip(ends, jumps):
        x = jnp.where(index == 0, 0.0, pltpu.roll(end, SUB - 1, 0))
        for n in (1, 2, 4):
            x = x + jnp.where(index >= n, jump, 0.0) * pltpu.roll(x, SUB - n, 0)
            jump = jump * jump
        out.append(x)
    return out


def fold_modes(products, modes):
    lane_filter = lax.div(lax.broadcasted_iota(jnp.int32, (modes, LANES), 1), GROUP_CH)
    parts = [
        jnp.where(lane_filter == f, products[f * modes : (f + 1) * modes, :], 0.0)
        for f in range(TILE_FILTERS)
    ]
    while len(parts) > 1:
        parts = [a + b for a, b in zip(parts[::2], parts[1::2])]
    return parts[0]


def states_kernel(
    full,
    log_rates_h,
    key_h,
    values_h,
    upstream_h,
    query_h,
    states,
    rate_out,
    mixed_out,
    carried_out,
    skip_out,
    rates_s,
    key,
    values,
    upstream,
    query,
    weight_s,
    sems,
):
    rows, channels = key.shape
    tiles = channels // LANES
    filters = channels // GROUP_CH
    modes = log_rates_h.shape[0]
    part = tiles // 2 * modes
    wide = TILE_FILTERS * modes
    copies = [
        pltpu.make_async_copy(src, dst, sems.at[n])
        for n, (src, dst) in enumerate(
            (
                (log_rates_h, rates_s),
                (key_h, key),
                (values_h, values),
                (upstream_h, upstream),
                (query_h, query),
            )
        )
    ]
    for copy in copies:
        copy.start()
    copies[0].wait()
    step_rates = own_columns(jnp.exp(rates_s[...]), filters) * (1.0 / full)
    channel_rates = per_channel(step_rates, group_mask(filters, channels))
    time = lax.broadcasted_iota(jnp.int32, (modes, rows), 1).astype(F32)
    back_time = float(rows - 1) - time
    for f in range(filters):
        rate = jnp.broadcast_to(step_rates[:, f : f + 1], (modes, rows))
        ct, row = f // TILE_FILTERS, (f % TILE_FILTERS) * modes
        for way, away in enumerate((back_time, time)):
            weight = jnp.exp(-rate * away)
            for n, high_low in enumerate((split(weight), split(weight * away))):
                at = slice(n * wide + row, n * wide + row + modes)
                weight_s[ct, 2 * way, at, :] = high_low[0]
                weight_s[ct, 2 * way + 1, at, :] = high_low[1]
    for ct in range(tiles):
        rate_out[ct] = channel_rates[:, ct * LANES : (ct + 1) * LANES]
    for copy in copies[1:]:
        copy.wait()
    for ct in range(tiles):
        lanes = slice(ct * LANES, (ct + 1) * LANES)
        mixed = key[:, lanes].astype(F32) * values[:, lanes].astype(F32)
        carried = upstream[:, lanes].astype(F32) * query[:, lanes].astype(F32)
        mixed_out[ct] = mixed
        carried_out[ct] = carried
        base = ct // (tiles // 2) * 4 * part + ct % (tiles // 2) * modes
        for way, x in enumerate((mixed, carried)):
            products = wide_dot(weight_s[ct, 2 * way], weight_s[ct, 2 * way + 1], *split(x))
            for n in range(2):
                at = base + (2 * way + n) * part
                states[at : at + modes, :] = fold_modes(products[n * wide : (n + 1) * wide], modes)
        skip_out[ct : ct + 1, :] = jnp.sum(mixed * carried, axis=0, keepdims=True)


def by_filter(firsts, seconds, first_filter, filters):
    modes = firsts[0].shape[0]
    both = jnp.concatenate([jnp.concatenate(v, axis=1) for v in (firsts, seconds)], axis=0)
    channels = both.shape[1]
    row = lax.broadcasted_iota(jnp.int32, (filters, channels), 0)
    col = lax.broadcasted_iota(jnp.int32, (filters, channels), 1)
    mask = jnp.where(row == first_filter + lax.div(col, GROUP_CH), 1.0, 0.0).astype(BF16)
    high, rest = split(both)
    middle, low = split(both - high.astype(F32))
    summed = lax.dot_general(
        jnp.concatenate([high, middle, low], axis=0),
        mask,
        (((1,), (1,)), ((), ())),
        preferred_element_type=F32,
    )
    summed = summed[: 2 * modes] + summed[2 * modes : 4 * modes] + summed[4 * modes :]
    return jnp.concatenate([summed[:modes], summed[modes:]], axis=1)


def sub_spans(x_ref, ct, decay, steps, reverse):
    order = range(steps - 1, -1, -1) if reverse else range(steps)
    state = slope = None
    for i in order:
        x = x_ref[ct, pl.ds(i, SUB, stride=steps), :]
        if state is None:
            state = [x] * len(decay)
            continue
        moved = [d * s for d, s in zip(decay, state)]
        slope = moved if slope is None else [d * t + a for d, t, a in zip(decay, slope, moved)]
        state = [a + x for a in moved]
    return state, slope


def sub_starts_both(ends, slopes, jumps, span):
    index = lax.broadcasted_iota(jnp.int32, (SUB, LANES), 0)
    starts, start_slopes = [], []
    for end, slope, jump in zip(ends, slopes, jumps):
        x = jnp.where(index == 0, 0.0, pltpu.roll(end, 1, 0))
        y = jnp.where(index == 0, 0.0, pltpu.roll(slope, 1, 0))
        for n in (1, 2, 4):
            hop = jnp.where(index >= n, jump, 0.0)
            x_far = pltpu.roll(x, n, 0)
            y = y + hop * (pltpu.roll(y, n, 0) + float(n * span) * x_far)
            x = x + hop * x_far
            jump = jump * jump
        starts.append(x)
        start_slopes.append(y)
    return starts, start_slopes


def within_kernel(rate_ref, mixed_ref, carried_ref, skip, sums, starts, first_s, second_s):
    tiles, rows, _ = mixed_ref.shape
    modes = rate_ref.shape[1]
    steps = rows // SUB
    half = modes // 2
    total = lambda v: jnp.sum(v, axis=0, keepdims=True)

    def tile(ct, _):
        rate = rate_ref[ct]
        firsts, seconds = [], []
        for lo in range(0, modes, half):
            rate_rows = [spread(rate[m : m + 1, :]) for m in range(lo, lo + half)]
            decay = [jnp.exp(-r) for r in rate_rows]
            jumps = [jnp.exp(-r * float(steps)) for r in rate_rows]
            ends, end_slopes = sub_spans(mixed_ref, ct, decay, steps, False)
            before, before_slopes = sub_starts_both(ends, end_slopes, jumps, steps)
            behind, behind_slopes = sub_spans(carried_ref, ct, decay, steps, True)
            for m in range(half):
                starts[ct, 0, lo + m] = before[m]
                starts[ct, 1, lo + m] = behind[m]
                reached = decay[m] * before[m]
                firsts.append(total(reached * behind[m]))
                seconds.append(
                    total(
                        (decay[m] * before_slopes[m]) * behind[m]
                        + reached * (behind[m] + behind_slopes[m])
                    )
                )
        x = [mixed_ref[ct, pl.ds(i, SUB, stride=steps), :] for i in range(steps)]
        c = [carried_ref[ct, pl.ds(i, SUB, stride=steps), :] for i in range(steps)]
        decay = jnp.exp(-rate)
        first = second = jnp.zeros((modes, LANES), F32)
        for lag in range(steps - 1, -1, -1):
            terms = [c[i + lag] * x[i] for i in range(steps - lag)]
            while len(terms) > 1:
                odd = terms[len(terms) // 2 * 2 :]
                terms = [a + b for a, b in zip(terms[::2], terms[1::2])] + odd
            moved = decay * first
            second = decay * second + moved
            first = moved + total(terms[0])
        first_s[ct] = first + jnp.concatenate(firsts, axis=0)
        second_s[ct] = second + jnp.concatenate(seconds, axis=0)
        return 0

    lax.fori_loop(0, tiles, tile, 0)
    packet = by_filter(
        [first_s[ct] for ct in range(tiles)],
        [second_s[ct] for ct in range(tiles)],
        0,
        tiles * TILE_FILTERS,
    )
    sums[:modes, :] = packet
    sums[modes:, :] = skip[...]


def spans_join(own, other, rate, upper, span):
    low = [jnp.where(upper, o, w) for w, o in zip(own, other)]
    high = [jnp.where(upper, w, o) for w, o in zip(own, other)]
    decay = jnp.exp(-rate)
    first = decay * (low[0] * high[2])
    second = decay * (low[1] * high[2] + low[0] * (high[2] + high[3]))
    far = jnp.exp(-rate * float(span))
    joined = (
        far * low[0] + high[0],
        far * (low[1] + float(span) * low[0]) + high[1],
        low[2] + far * high[2],
        low[3] + far * (high[3] + float(span) * high[2]),
    )
    return joined, first, second


def border_sums(first, second, tiles, modes):
    cut = lambda v: [v[n * modes : (n + 1) * modes, :] for n in range(tiles // 2)]
    begin = (lax.axis_index("ctx") & 1) * (tiles // 2 * TILE_FILTERS)
    return by_filter(cut(first), cut(second), begin, tiles * TILE_FILTERS)


def half_rates(rate_ref):
    tiles, modes, _ = rate_ref.shape
    begin = (lax.axis_index("ctx") & 1) * (tiles // 2)
    return jnp.concatenate([rate_ref[begin + n] for n in range(tiles // 2)], axis=0)


def join_kernel(rows, step, is_last_next, rate_ref, own_ref, other_ref, *refs):
    tiles, modes, _ = rate_ref.shape
    part = tiles // 2 * modes
    if step == 1:
        sums_ref, joined_ref, borders_ref, *send = refs
        begin = (lax.axis_index("ctx") & 1) * (4 * part)
        own = [own_ref[pl.ds(pl.multiple_of(begin + q * part, part), part), :] for q in range(4)]
        sums = sums_ref[...]
    else:
        old_borders, joined_ref, borders_ref, *send = refs
        own = [own_ref[q * part : (q + 1) * part, :] for q in range(4)]
        sums = own_ref[4 * part :, :] + other_ref[4 * part :, :]
    other = [other_ref[q * part : (q + 1) * part, :] for q in range(4)]
    position = lax.axis_index("ctx")
    upper = (position & step) != 0
    rate = half_rates(rate_ref)
    joined, first, second = spans_join(own, other, rate, upper, rows * step)
    for q in range(4):
        joined_ref[q * part : (q + 1) * part, :] = joined[q]
    sums = jnp.concatenate([sums[:modes] + border_sums(first, second, tiles, modes), sums[modes:]], axis=0)
    joined_ref[4 * part :, :] = sums
    if step == 1:
        borders_ref[...] = jnp.zeros_like(borders_ref)
    else:
        borders_ref[...] = add_borders(
            rows, step, rate, [old_borders[:part, :], old_borders[part:, :]], other[0], other[2]
        )
    if is_last_next:
        next_upper = (position & (2 * step)) != 0
        for q in range(2):
            send[0][q * part : (q + 1) * part, :] = jnp.where(next_upper, joined[2 + q], joined[q])
        send[0][2 * part :, :] = sums


def add_borders(rows, step, rate, borders, forward, backward):
    position = lax.axis_index("ctx")
    upper = (position & step) != 0
    before = ((position & (step - 1)) >> 1).astype(F32) * float(2 * rows)
    behind = float(rows * (step - 2)) - before
    return jnp.concatenate(
        [
            borders[0] + jnp.where(upper, jnp.exp(-rate * before) * forward, 0.0),
            borders[1] + jnp.where(upper, 0.0, jnp.exp(-rate * behind) * backward),
        ],
        axis=0,
    )


def last_join_kernel(
    rows, step, rate_ref, own_ref, other_ref, borders_ref, states_ref, partner_ref, mine_ref, back_ref, modal_ref
):
    tiles, modes, _ = rate_ref.shape
    part = tiles // 2 * modes
    position = lax.axis_index("ctx")
    upper = (position & step) != 0
    rate = half_rates(rate_ref)
    own = [own_ref[q * part : (q + 1) * part, :] for q in range(4)]
    other = [other_ref[q * part : (q + 1) * part, :] for q in range(2)]
    _, first, second = spans_join(own, other + other, rate, upper, rows * step)
    sums = own_ref[4 * part :, :] + other_ref[2 * part :, :]
    modal = sums[:modes] + border_sums(first, second, tiles, modes)
    modal_ref[...] = modal
    back_ref[2 * part : 2 * part + modes, :] = modal
    back_ref[2 * part + modes :, :] = sums[modes:]
    borders = add_borders(
        rows, step, rate, [borders_ref[:part, :], borders_ref[part:, :]], other[0], other[0]
    )
    incoming, outgoing = borders[:part], borders[part:]
    far = jnp.exp(-rate * float(rows))
    begin = (position & 1) * (4 * part)
    pick = lambda q: states_ref[pl.ds(pl.multiple_of(begin + q * part, part), part), :]
    second_block = (position & 1) != 0
    through = far * incoming
    across = far * outgoing
    for ref, is_second, forward, backward in (
        (mine_ref, second_block, partner_ref[:part, :], partner_ref[2 * part : 3 * part, :]),
        (back_ref, jnp.logical_not(second_block), pick(0), pick(2)),
    ):
        ref[:part, :] = jnp.where(is_second, through + forward, incoming)
        ref[part : 2 * part, :] = jnp.where(is_second, outgoing, across + backward)


def block_kernel(
    full, log_rates, residues, skip_weight, rate_ref, mixed_ref, carried_ref, starts, scales, results
):
    tiles, rows, _ = mixed_ref.shape
    modes = rate_ref.shape[1]
    filters = tiles * TILE_FILTERS
    steps = rows // SUB
    half = modes // 2
    scaled = own_columns(residues[...], filters) * jnp.sqrt(
        jnp.exp(own_columns(log_rates[...], filters)) / full
    )
    scaled = per_channel(scaled, group_mask(filters, tiles * LANES))
    for n in range(tiles):
        scales[n] = scaled[:, n * LANES : (n + 1) * LANES]

    def tile(ct, _):
        rate = rate_ref[ct]
        scale = scales[ct]
        weight = spread(skip_weight[pl.ds(ct, 1), :])
        for lo in range(0, modes, half):
            rate_rows = [spread(rate[m : m + 1, :]) for m in range(lo, lo + half)]
            decay = [jnp.exp(-r) for r in rate_rows]
            gains = [spread(scale[m : m + 1, :]) for m in range(lo, lo + half)]
            for way, x_ref in enumerate((mixed_ref, carried_ref)):
                state = [starts[ct, way, lo + m] for m in range(half)]
                if way:
                    state = sub_starts_back(state, [jnp.exp(-r * float(steps)) for r in rate_rows])
                for i in range(steps - 1, -1, -1) if way else range(steps):
                    at = pl.ds(i, SUB, stride=steps)
                    x = x_ref[ct, at, :]
                    state = [d * s + x for d, s in zip(decay, state)]
                    terms = [g * s for g, s in zip(gains, state)]
                    terms.append(results[ct, way, at, :] if lo > 0 else weight * x)
                    while len(terms) > 1:
                        odd = terms[len(terms) // 2 * 2 :]
                        terms = [a + b for a, b in zip(terms[::2], terms[1::2])] + odd
                    results[ct, way, at, :] = terms[0]
        return 0

    lax.fori_loop(0, tiles, tile, 0)


def grads_kernel(mine, theirs, rate_ref, scale_ref, results, key, values, upstream, *refs):
    query_grad, key_grad, value_grad = refs
    tiles, modes, _ = scale_ref.shape
    rows = key.shape[0]
    share = tiles // 2
    part = share * modes
    second_half = (lax.axis_index("ctx") & 1) != 0
    lane = lax.broadcasted_iota(jnp.int32, (modes, LANES), 1)
    own_mode = lax.broadcasted_iota(jnp.int32, (modes, LANES), 0) == lax.rem(lane, modes)
    lane_filter = lax.div(lane, GROUP_CH)
    time = lax.broadcasted_iota(jnp.int32, (rows, LANES), 0).astype(F32)

    def piece(p):
        is_mine = second_half if p else jnp.logical_not(second_half)
        for n in range(share):
            ct = p * share + n
            rate = rate_ref[ct]
            rate_row = jnp.sum(jnp.where(own_mode, rate, 0.0), axis=0, keepdims=True)
            parts = []
            for offset, away in ((0, time + 1.0), (part, float(rows) - time)):
                at = slice(offset + n * modes, offset + (n + 1) * modes)
                edge = scale_ref[ct] * jnp.where(is_mine, mine[at, :], theirs[at, :])
                spaced = jnp.concatenate(
                    [jnp.where(lane_filter == f, edge, 0.0) for f in range(TILE_FILTERS)], axis=0
                )
                parts.append(wide_dot(*split(jnp.exp(-rate_row * away)), *split(spaced)))
            lanes = slice(n * LANES, (n + 1) * LANES)
            query_grad[:, lanes] = (
                upstream[:, lanes].astype(F32) * (results[ct, 0] + parts[0])
            ).astype(query_grad.dtype)
            mixed_grad = results[ct, 1] + parts[1]
            key_grad[:, lanes] = (mixed_grad * values[:, lanes].astype(F32)).astype(key_grad.dtype)
            value_grad[:, lanes] = (mixed_grad * key[:, lanes].astype(F32)).astype(value_grad.dtype)

    for p in range(2):
        pl.when(pl.program_id(0) == p)(functools.partial(piece, p))


def final_kernel(
    full, log_rates, residues, back, theirs, here, there, residue_grad, log_rate_grad, skip_grad
):
    modes, total_filters = log_rates.shape
    filters = here.shape[1] // 2
    group = lax.axis_index("grp")
    skip_rows = slice(back.shape[0] - skip_grad.shape[0], back.shape[0])
    skip_grad[...] = (back[skip_rows, :] + theirs[skip_rows, :]) / jnp.sqrt(jnp.float32(full))
    by_distance = [here[:modes, :], there[:modes, :], here[modes:, :], there[modes:, :]]
    totals = []
    for g in range(total_filters // filters):
        total = by_distance[0]
        for k in range(1, len(by_distance)):
            total = jnp.where((group ^ k) == g, by_distance[k], total)
        totals.append(total)
    first_sum = jnp.concatenate([t[:, :filters] for t in totals], axis=1)
    second_sum = jnp.concatenate([t[:, filters:] for t in totals], axis=1) * (1.0 / full)
    rates = jnp.exp(log_rates[...])
    root = jnp.sqrt(rates / full)
    scale_root = jnp.sqrt(jnp.float32(full))
    residue_grad[...] = root * first_sum / scale_root
    log_rate_grad[...] = residues[...] * root * (0.5 * first_sum - rates * second_sum) / scale_root


def flip(x, step, axis="ctx"):
    return lax.ppermute(x, axis, [(i, i ^ step) for i in range(lax.axis_size(axis))])


def after(x, *others):
    return lax.optimization_barrier((x, *others))[0]


def local(query_gate, key_gate, values, upstream, skip_weight, residues, log_rates):
    context = lax.axis_size("ctx")
    groups = lax.axis_size("grp")
    position = lax.axis_index("ctx")
    rows, channels = query_gate.shape
    total_filters, modes = residues.shape
    filters = channels // GROUP_CH
    tiles = channels // LANES
    full = rows * context
    part = tiles // 2 * modes
    tail = modes + tiles
    assert context >= 4 and context & (context - 1) == 0 and groups == 4
    vmem = pl.BlockSpec(memory_space=pltpu.VMEM)
    in_hbm = pl.BlockSpec(memory_space=pltpu.HBM)
    shape = lambda *dims: jax.ShapeDtypeStruct(dims, F32)
    params = pltpu.CompilerParams(vmem_limit_bytes=16 * 1024 * 1024)
    log_rates_t, residues_t = log_rates.T, residues.T

    def call(name, kernel, out_shape, operands, scratch=(), flops=0):
        return pl.pallas_call(
            kernel,
            out_shape=out_shape,
            in_specs=[vmem] * len(operands),
            out_specs=(vmem,) * len(out_shape),
            scratch_shapes=[pltpu.VMEM(dims, F32) for dims in scratch],
            compiler_params=params,
            cost_estimate=pl.CostEstimate(flops=flops, transcendentals=0, bytes_accessed=flops // 4),
            name=name,
        )(*operands)

    inputs = (log_rates_t, key_gate, values, upstream, query_gate)
    states, rate, mixed, carried, skip = pl.pallas_call(
        functools.partial(states_kernel, full),
        out_shape=(
            shape(8 * part, LANES),
            shape(tiles, modes, LANES),
            shape(tiles, rows, LANES),
            shape(tiles, rows, LANES),
            shape(tiles, LANES),
        ),
        in_specs=[in_hbm] * 5,
        out_specs=(vmem,) * 5,
        scratch_shapes=[
            pltpu.VMEM((modes, total_filters), F32),
            pltpu.VMEM((rows, channels), BF16),
            pltpu.VMEM((rows, channels), BF16),
            pltpu.VMEM((rows, channels), BF16),
            pltpu.VMEM((rows, channels), BF16),
            pltpu.VMEM((tiles, 4, 2 * TILE_FILTERS * modes, rows), BF16),
            pltpu.SemaphoreType.DMA((5,)),
        ],
        compiler_params=params,
        name="states",
    )(*(pltpu.with_memory_space_constraint(x, pltpu.HBM) for x in inputs))
    work = rows * channels * modes

    other_half = lax.dynamic_slice_in_dim(states, (1 - (position & 1)) * (4 * part), 4 * part, 0)
    partner = flip(other_half, 1)
    sums, starts = call(
        "within",
        within_kernel,
        (shape(tail, LANES), shape(tiles, 2, modes, SUB, LANES)),
        (rate, mixed, carried, skip),
        ((tiles, modes, LANES), (tiles, modes, LANES)),
        12 * work,
    )
    scale = results = None
    step = 1
    own, other, extra = states, after(partner, sums), (sums,)
    while 2 * step < context:
        is_last_next = 4 * step >= context
        own, borders, *send = call(
            "join",
            functools.partial(join_kernel, rows, step, is_last_next),
            (shape(4 * part + tail, LANES), shape(2 * part, LANES))
            + ((shape(2 * part + tail, LANES),) if is_last_next else ()),
            (rate, own, other, *extra),
        )
        other = flip(send[0] if send else own, 2 * step)
        if step == 1:
            scale, results = call(
                "block",
                functools.partial(block_kernel, full),
                (shape(tiles, modes, LANES), shape(tiles, 2, rows, LANES)),
                (
                    log_rates_t,
                    residues_t,
                    skip_weight.reshape(tiles, LANES),
                    after(rate, own),
                    mixed,
                    carried,
                    starts,
                ),
                (),
                8 * work,
            )
            other = after(other, results)
        extra = (borders,)
        step *= 2
    mine, back, modal = call(
        "last_join",
        functools.partial(last_join_kernel, rows, step),
        (shape(2 * part, LANES), shape(2 * part + tail, LANES), shape(modes, LANES)),
        (rate, own, other, borders, states, partner),
    )

    everyone = ("ctx", "grp")
    theirs = flip(back, 1)
    across, level = flip(modal, groups + 2, everyone), flip(modal, 2, everyone)
    columns = pl.BlockSpec((rows, channels // 2), lambda i: (0, i))
    outputs = pl.pallas_call(
        grads_kernel,
        grid=(2,),
        out_shape=(jax.ShapeDtypeStruct((rows, channels), BF16),) * 3,
        in_specs=[vmem] * 5 + [columns] * 3,
        out_specs=(columns,) * 3,
        compiler_params=params,
        cost_estimate=pl.CostEstimate(
            flops=4 * work, transcendentals=0, bytes_accessed=20 * rows * channels
        ),
        name="grads",
    )(mine, theirs, rate, scale, results, key_gate, values, upstream)
    query_grad, key_grad, value_grad = outputs
    across, level = (after(x, *outputs) for x in (across, level))
    here = jnp.concatenate([modal + theirs[2 * part : 2 * part + modes], level + across], axis=0)
    there = flip(here, 1, "grp")
    residue_grad, log_rate_grad, skip_grad = call(
        "final",
        functools.partial(final_kernel, full),
        (shape(modes, total_filters),) * 2 + (shape(tiles, LANES),),
        (log_rates_t, residues_t, back, theirs, here, there),
    )
    return (
        query_grad,
        key_grad,
        value_grad,
        skip_grad.reshape(channels),
        residue_grad.T,
        log_rate_grad.T,
    )


def solution(mesh):
    placed = (
        P("ctx", "grp"),
        P("ctx", "grp"),
        P("ctx", "grp"),
        P("ctx", "grp"),
        P("grp"),
        P(),
        P(),
    )
    return jax.shard_map(
        local,
        mesh=mesh,
        in_specs=placed,
        out_specs=(P("ctx", "grp"), P("ctx", "grp"), P("ctx", "grp"), P("grp"), P(), P()),
        check_vma=False,
    )
```

```python
import functools

import jax
import jax.numpy as jnp
from jax import lax
from jax.experimental import pallas as pl
from jax.experimental.pallas import tpu as pltpu
from jax.sharding import PartitionSpec as P

GROUP_CH = 16
LANES = 128
SUB = 8
TILE_FILTERS = LANES // GROUP_CH
HIGHEST = lax.Precision.HIGHEST
F32 = jnp.float32
BF16 = jnp.bfloat16


def own_columns(table, filters):
    total = table.shape[1]
    start = lax.axis_index("grp") * filters
    return pltpu.roll(table, lax.rem(total - start, total), 1)[:, :filters]


def group_mask(filters, channels):
    row = lax.broadcasted_iota(jnp.int32, (filters, channels), 0)
    col = lax.broadcasted_iota(jnp.int32, (filters, channels), 1)
    return jnp.where(row == lax.div(col, GROUP_CH), 1.0, 0.0).astype(F32)


def per_channel(table, mask):
    return jnp.dot(table, mask, precision=HIGHEST, preferred_element_type=F32)


def split(x):
    high = x.astype(BF16)
    return high, (x - high.astype(F32)).astype(BF16)


def wide_dot(a_high, a_low, b_high, b_low):
    return jnp.dot(
        jnp.concatenate([a_high, a_low, a_high], axis=1),
        jnp.concatenate([b_high, b_high, b_low], axis=0),
        preferred_element_type=F32,
    )


def spread(row):
    return jnp.broadcast_to(row, (SUB, LANES))


def sub_starts_back(ends, jumps):
    index = SUB - 1 - lax.broadcasted_iota(jnp.int32, (SUB, LANES), 0)
    out = []
    for end, jump in zip(ends, jumps):
        x = jnp.where(index == 0, 0.0, pltpu.roll(end, SUB - 1, 0))
        for n in (1, 2, 4):
            x = x + jnp.where(index >= n, jump, 0.0) * pltpu.roll(x, SUB - n, 0)
            jump = jump * jump
        out.append(x)
    return out


def fold_modes(products, modes):
    lane_filter = lax.div(lax.broadcasted_iota(jnp.int32, (modes, LANES), 1), GROUP_CH)
    parts = [
        jnp.where(lane_filter == f, products[f * modes : (f + 1) * modes, :], 0.0)
        for f in range(TILE_FILTERS)
    ]
    while len(parts) > 1:
        parts = [a + b for a, b in zip(parts[::2], parts[1::2])]
    return parts[0]


def states_kernel(
    full,
    log_rates_h,
    key_h,
    values_h,
    upstream_h,
    query_h,
    states,
    rate_out,
    mixed_out,
    carried_out,
    skip_out,
    rates_s,
    key,
    values,
    upstream,
    query,
    weight_s,
    sems,
):
    rows, channels = key.shape
    tiles = channels // LANES
    filters = channels // GROUP_CH
    modes = log_rates_h.shape[0]
    part = tiles // 2 * modes
    copies = [
        pltpu.make_async_copy(src, dst, sems.at[n])
        for n, (src, dst) in enumerate(
            (
                (log_rates_h, rates_s),
                (key_h, key),
                (values_h, values),
                (upstream_h, upstream),
                (query_h, query),
            )
        )
    ]
    for copy in copies:
        copy.start()
    copies[0].wait()
    step_rates = own_columns(jnp.exp(rates_s[...]), filters) * (1.0 / full)
    channel_rates = per_channel(step_rates, group_mask(filters, channels))
    time = lax.broadcasted_iota(jnp.int32, (modes, rows), 1).astype(F32)
    back_time = float(rows - 1) - time
    for f in range(filters):
        rate = jnp.broadcast_to(step_rates[:, f : f + 1], (modes, rows))
        ct, row = f // TILE_FILTERS, (f % TILE_FILTERS) * modes
        for way, away in enumerate((back_time, time)):
            high, low = split(jnp.exp(-rate * away))
            weight_s[ct, 2 * way, row : row + modes, :] = high
            weight_s[ct, 2 * way + 1, row : row + modes, :] = low
    for ct in range(tiles):
        rate_out[ct] = channel_rates[:, ct * LANES : (ct + 1) * LANES]
    forward = lax.broadcasted_iota(jnp.int32, (rows, LANES), 0).astype(F32)
    backward = float(rows - 1) - forward
    for copy in copies[1:]:
        copy.wait()
    for ct in range(tiles):
        lanes = slice(ct * LANES, (ct + 1) * LANES)
        mixed = key[:, lanes].astype(F32) * values[:, lanes].astype(F32)
        carried = upstream[:, lanes].astype(F32) * query[:, lanes].astype(F32)
        mixed_out[ct] = mixed
        carried_out[ct] = carried
        base = ct // (tiles // 2) * 4 * part + ct % (tiles // 2) * modes
        for way, (x, away) in enumerate(((mixed, backward), (carried, forward))):
            both = jnp.concatenate([x, x * away], axis=1)
            products = wide_dot(weight_s[ct, 2 * way], weight_s[ct, 2 * way + 1], *split(both))
            for n in range(2):
                at = base + (2 * way + n) * part
                states[at : at + modes, :] = fold_modes(products[:, n * LANES : (n + 1) * LANES], modes)
        skip_out[ct : ct + 1, :] = jnp.sum(mixed * carried, axis=0, keepdims=True)


def by_filter(firsts, seconds, first_filter, filters):
    modes = firsts[0].shape[0]
    both = jnp.concatenate([jnp.concatenate(v, axis=1) for v in (firsts, seconds)], axis=0)
    channels = both.shape[1]
    row = lax.broadcasted_iota(jnp.int32, (filters, channels), 0)
    col = lax.broadcasted_iota(jnp.int32, (filters, channels), 1)
    mask = jnp.where(row == first_filter + lax.div(col, GROUP_CH), 1.0, 0.0).astype(BF16)
    high, rest = split(both)
    middle, low = split(both - high.astype(F32))
    summed = lax.dot_general(
        jnp.concatenate([high, middle, low], axis=0),
        mask,
        (((1,), (1,)), ((), ())),
        preferred_element_type=F32,
    )
    summed = summed[: 2 * modes] + summed[2 * modes : 4 * modes] + summed[4 * modes :]
    return jnp.concatenate([summed[:modes], summed[modes:]], axis=1)


def sub_spans(x_ref, decay, reverse):
    steps = x_ref.shape[0]
    state = slope = None
    for i in range(steps - 1, -1, -1) if reverse else range(steps):
        x = x_ref[i]
        if state is None:
            state = [x] * len(decay)
            continue
        moved = [d * s for d, s in zip(decay, state)]
        slope = moved if slope is None else [d * t + a for d, t, a in zip(decay, slope, moved)]
        state = [a + x for a in moved]
    return state, slope


def sub_starts_both(ends, slopes, jumps, span):
    index = lax.broadcasted_iota(jnp.int32, (SUB, LANES), 0)
    starts, start_slopes = [], []
    for end, slope, jump in zip(ends, slopes, jumps):
        x = jnp.where(index == 0, 0.0, pltpu.roll(end, 1, 0))
        y = jnp.where(index == 0, 0.0, pltpu.roll(slope, 1, 0))
        for n in (1, 2, 4):
            hop = jnp.where(index >= n, jump, 0.0)
            x_far = pltpu.roll(x, n, 0)
            y = y + hop * (pltpu.roll(y, n, 0) + float(n * span) * x_far)
            x = x + hop * x_far
            jump = jump * jump
        starts.append(x)
        start_slopes.append(y)
    return starts, start_slopes


def within_kernel(rate_ref, mixed_ref, carried_ref, skip, sums, starts, dealt, first_s, second_s):
    tiles, rows, _ = mixed_ref.shape
    modes = rate_ref.shape[1]
    steps = rows // SUB
    half = modes // 2
    total = lambda v: jnp.sum(v, axis=0, keepdims=True)

    def tile(ct, _):
        rate = rate_ref[ct]
        step_decay = jnp.exp(-rate)
        sub_decay = jnp.exp(-rate * float(steps))
        firsts, seconds = [], []
        for i in range(steps):
            for way, ref in enumerate((mixed_ref, carried_ref)):
                dealt[ct, way, i] = ref[ct, pl.ds(i, SUB, stride=steps), :]
        for lo in range(0, modes, half):
            decay = [spread(step_decay[m : m + 1, :]) for m in range(lo, lo + half)]
            jumps = [spread(sub_decay[m : m + 1, :]) for m in range(lo, lo + half)]
            ends, end_slopes = sub_spans(dealt.at[ct, 0], decay, False)
            before, before_slopes = sub_starts_both(ends, end_slopes, jumps, steps)
            behind, behind_slopes = sub_spans(dealt.at[ct, 1], decay, True)
            for m in range(half):
                starts[ct, 0, lo + m] = before[m]
                starts[ct, 1, lo + m] = behind[m]
                reached = decay[m] * before[m]
                firsts.append(total(reached * behind[m]))
                seconds.append(
                    total(
                        (decay[m] * before_slopes[m]) * behind[m]
                        + reached * (behind[m] + behind_slopes[m])
                    )
                )
        x = [dealt[ct, 0, i] for i in range(steps)]
        c = [dealt[ct, 1, i] for i in range(steps)]
        first = second = jnp.zeros((modes, LANES), F32)
        for lag in range(steps - 1, -1, -1):
            terms = [c[i + lag] * x[i] for i in range(steps - lag)]
            while len(terms) > 1:
                odd = terms[len(terms) // 2 * 2 :]
                terms = [a + b for a, b in zip(terms[::2], terms[1::2])] + odd
            moved = step_decay * first
            second = step_decay * second + moved
            first = moved + total(terms[0])
        first_s[ct] = first + jnp.concatenate(firsts, axis=0)
        second_s[ct] = second + jnp.concatenate(seconds, axis=0)
        return 0

    lax.fori_loop(0, tiles, tile, 0)
    packet = by_filter(
        [first_s[ct] for ct in range(tiles)],
        [second_s[ct] for ct in range(tiles)],
        0,
        tiles * TILE_FILTERS,
    )
    sums[:modes, :] = packet
    sums[modes:, :] = skip[...]


def spans_join(own, other, rate, upper, span):
    low = [jnp.where(upper, o, w) for w, o in zip(own, other)]
    high = [jnp.where(upper, w, o) for w, o in zip(own, other)]
    decay = jnp.exp(-rate)
    first = decay * (low[0] * high[2])
    second = decay * (low[1] * high[2] + low[0] * (high[2] + high[3]))
    far = jnp.exp(-rate * float(span))
    joined = (
        far * low[0] + high[0],
        far * (low[1] + float(span) * low[0]) + high[1],
        low[2] + far * high[2],
        low[3] + far * (high[3] + float(span) * high[2]),
    )
    return joined, first, second


def border_sums(first, second, tiles, modes):
    cut = lambda v: [v[n * modes : (n + 1) * modes, :] for n in range(tiles // 2)]
    begin = (lax.axis_index("ctx") & 1) * (tiles // 2 * TILE_FILTERS)
    return by_filter(cut(first), cut(second), begin, tiles * TILE_FILTERS)


def half_rates(rate_ref):
    tiles, modes, _ = rate_ref.shape
    begin = (lax.axis_index("ctx") & 1) * (tiles // 2)
    return jnp.concatenate([rate_ref[begin + n] for n in range(tiles // 2)], axis=0)


def join_kernel(rows, step, is_last_next, rate_ref, own_ref, other_ref, *refs):
    tiles, modes, _ = rate_ref.shape
    part = tiles // 2 * modes
    if step == 1:
        sums_ref, joined_ref, borders_ref, *send = refs
        begin = (lax.axis_index("ctx") & 1) * (4 * part)
        own = [own_ref[pl.ds(pl.multiple_of(begin + q * part, part), part), :] for q in range(4)]
        sums = sums_ref[...]
    else:
        old_borders, joined_ref, borders_ref, *send = refs
        own = [own_ref[q * part : (q + 1) * part, :] for q in range(4)]
        sums = own_ref[4 * part :, :] + other_ref[4 * part :, :]
    other = [other_ref[q * part : (q + 1) * part, :] for q in range(4)]
    position = lax.axis_index("ctx")
    upper = (position & step) != 0
    rate = half_rates(rate_ref)
    joined, first, second = spans_join(own, other, rate, upper, rows * step)
    for q in range(4):
        joined_ref[q * part : (q + 1) * part, :] = joined[q]
    sums = jnp.concatenate([sums[:modes] + border_sums(first, second, tiles, modes), sums[modes:]], axis=0)
    joined_ref[4 * part :, :] = sums
    if step == 1:
        borders_ref[...] = jnp.zeros_like(borders_ref)
    else:
        borders_ref[...] = add_borders(
            rows, step, rate, [old_borders[:part, :], old_borders[part:, :]], other[0], other[2]
        )
    if is_last_next:
        next_upper = (position & (2 * step)) != 0
        for q in range(2):
            send[0][q * part : (q + 1) * part, :] = jnp.where(next_upper, joined[2 + q], joined[q])
        send[0][2 * part :, :] = sums


def add_borders(rows, step, rate, borders, forward, backward):
    position = lax.axis_index("ctx")
    upper = (position & step) != 0
    before = ((position & (step - 1)) >> 1).astype(F32) * float(2 * rows)
    behind = float(rows * (step - 2)) - before
    return jnp.concatenate(
        [
            borders[0] + jnp.where(upper, jnp.exp(-rate * before) * forward, 0.0),
            borders[1] + jnp.where(upper, 0.0, jnp.exp(-rate * behind) * backward),
        ],
        axis=0,
    )


def last_join_kernel(
    rows, step, rate_ref, own_ref, other_ref, borders_ref, states_ref, partner_ref, mine_ref, back_ref, modal_ref
):
    tiles, modes, _ = rate_ref.shape
    part = tiles // 2 * modes
    position = lax.axis_index("ctx")
    upper = (position & step) != 0
    rate = half_rates(rate_ref)
    own = [own_ref[q * part : (q + 1) * part, :] for q in range(4)]
    other = [other_ref[q * part : (q + 1) * part, :] for q in range(2)]
    _, first, second = spans_join(own, other + other, rate, upper, rows * step)
    sums = own_ref[4 * part :, :] + other_ref[2 * part :, :]
    modal = sums[:modes] + border_sums(first, second, tiles, modes)
    modal_ref[...] = modal
    back_ref[2 * part : 2 * part + modes, :] = modal
    back_ref[2 * part + modes :, :] = sums[modes:]
    borders = add_borders(
        rows, step, rate, [borders_ref[:part, :], borders_ref[part:, :]], other[0], other[0]
    )
    incoming, outgoing = borders[:part], borders[part:]
    far = jnp.exp(-rate * float(rows))
    begin = (position & 1) * (4 * part)
    pick = lambda q: states_ref[pl.ds(pl.multiple_of(begin + q * part, part), part), :]
    second_block = (position & 1) != 0
    through = far * incoming
    across = far * outgoing
    for ref, is_second, forward, backward in (
        (mine_ref, second_block, partner_ref[:part, :], partner_ref[2 * part : 3 * part, :]),
        (back_ref, jnp.logical_not(second_block), pick(0), pick(2)),
    ):
        ref[:part, :] = jnp.where(is_second, through + forward, incoming)
        ref[part : 2 * part, :] = jnp.where(is_second, outgoing, across + backward)


def block_kernel(
    full, log_rates, residues, skip_weight, rate_ref, dealt, starts, scales, results, result_s
):
    tiles, modes, _ = rate_ref.shape
    filters = tiles * TILE_FILTERS
    steps = dealt.shape[2]
    half = modes // 2
    scaled = own_columns(residues[...], filters) * jnp.sqrt(
        jnp.exp(own_columns(log_rates[...], filters)) / full
    )
    scaled = per_channel(scaled, group_mask(filters, tiles * LANES))
    for n in range(tiles):
        scales[n] = scaled[:, n * LANES : (n + 1) * LANES]

    def tile(ct, _):
        step_decay = jnp.exp(-rate_ref[ct])
        sub_decay = jnp.exp(-rate_ref[ct] * float(steps))
        scale = scales[ct]
        weight = spread(skip_weight[pl.ds(ct, 1), :])
        for lo in range(0, modes, half):
            decay = [spread(step_decay[m : m + 1, :]) for m in range(lo, lo + half)]
            gains = [spread(scale[m : m + 1, :]) for m in range(lo, lo + half)]
            for way in range(2):
                state = [starts[ct, way, lo + m] for m in range(half)]
                if way:
                    state = sub_starts_back(
                        state, [spread(sub_decay[m : m + 1, :]) for m in range(lo, lo + half)]
                    )
                for i in range(steps - 1, -1, -1) if way else range(steps):
                    x = dealt[ct, way, i]
                    state = [d * s + x for d, s in zip(decay, state)]
                    terms = [g * s for g, s in zip(gains, state)]
                    terms.append(result_s[way, i] if lo > 0 else weight * x)
                    while len(terms) > 1:
                        odd = terms[len(terms) // 2 * 2 :]
                        terms = [a + b for a, b in zip(terms[::2], terms[1::2])] + odd
                    if lo > 0:
                        results[ct, way, pl.ds(i, SUB, stride=steps), :] = terms[0]
                    else:
                        result_s[way, i] = terms[0]
        return 0

    lax.fori_loop(0, tiles, tile, 0)


def grads_kernel(mine, theirs, rate_ref, scale_ref, results, key, values, upstream, *refs):
    query_grad, key_grad, value_grad = refs
    tiles, modes, _ = scale_ref.shape
    rows = key.shape[0]
    share = tiles // 2
    part = share * modes
    second_half = (lax.axis_index("ctx") & 1) != 0
    lane = lax.broadcasted_iota(jnp.int32, (modes, LANES), 1)
    own_mode = lax.broadcasted_iota(jnp.int32, (modes, LANES), 0) == lax.rem(lane, modes)
    lane_filter = lax.div(lane, GROUP_CH)
    time = lax.broadcasted_iota(jnp.int32, (rows, LANES), 0).astype(F32)

    def piece(p):
        is_mine = second_half if p else jnp.logical_not(second_half)
        for n in range(share):
            ct = p * share + n
            rate = rate_ref[ct]
            rate_row = jnp.sum(jnp.where(own_mode, rate, 0.0), axis=0, keepdims=True)
            parts = []
            for offset, away in ((0, time + 1.0), (part, float(rows) - time)):
                at = slice(offset + n * modes, offset + (n + 1) * modes)
                edge = scale_ref[ct] * jnp.where(is_mine, mine[at, :], theirs[at, :])
                spaced = jnp.concatenate(
                    [jnp.where(lane_filter == f, edge, 0.0) for f in range(TILE_FILTERS)], axis=0
                )
                parts.append(wide_dot(*split(jnp.exp(-rate_row * away)), *split(spaced)))
            lanes = slice(n * LANES, (n + 1) * LANES)
            query_grad[:, lanes] = (
                upstream[:, lanes].astype(F32) * (results[ct, 0] + parts[0])
            ).astype(query_grad.dtype)
            mixed_grad = results[ct, 1] + parts[1]
            key_grad[:, lanes] = (mixed_grad * values[:, lanes].astype(F32)).astype(key_grad.dtype)
            value_grad[:, lanes] = (mixed_grad * key[:, lanes].astype(F32)).astype(value_grad.dtype)

    for p in range(2):
        pl.when(pl.program_id(0) == p)(functools.partial(piece, p))


def final_kernel(
    full, log_rates, residues, back, theirs, here, there, residue_grad, log_rate_grad, skip_grad
):
    modes, total_filters = log_rates.shape
    filters = here.shape[1] // 2
    group = lax.axis_index("grp")
    skip_rows = slice(back.shape[0] - skip_grad.shape[0], back.shape[0])
    skip_grad[...] = (back[skip_rows, :] + theirs[skip_rows, :]) / jnp.sqrt(jnp.float32(full))
    by_distance = [here[:modes, :], there[:modes, :], here[modes:, :], there[modes:, :]]
    totals = []
    for g in range(total_filters // filters):
        total = by_distance[0]
        for k in range(1, len(by_distance)):
            total = jnp.where((group ^ k) == g, by_distance[k], total)
        totals.append(total)
    first_sum = jnp.concatenate([t[:, :filters] for t in totals], axis=1)
    second_sum = jnp.concatenate([t[:, filters:] for t in totals], axis=1) * (1.0 / full)
    rates = jnp.exp(log_rates[...])
    root = jnp.sqrt(rates / full)
    scale_root = jnp.sqrt(jnp.float32(full))
    residue_grad[...] = root * first_sum / scale_root
    log_rate_grad[...] = residues[...] * root * (0.5 * first_sum - rates * second_sum) / scale_root


def flip(x, step, axis="ctx"):
    return lax.ppermute(x, axis, [(i, i ^ step) for i in range(lax.axis_size(axis))])


def after(x, *others):
    return lax.optimization_barrier((x, *others))[0]


def local(query_gate, key_gate, values, upstream, skip_weight, residues, log_rates):
    context = lax.axis_size("ctx")
    groups = lax.axis_size("grp")
    position = lax.axis_index("ctx")
    rows, channels = query_gate.shape
    total_filters, modes = residues.shape
    filters = channels // GROUP_CH
    tiles = channels // LANES
    full = rows * context
    part = tiles // 2 * modes
    tail = modes + tiles
    assert context >= 4 and context & (context - 1) == 0 and groups == 4
    vmem = pl.BlockSpec(memory_space=pltpu.VMEM)
    in_hbm = pl.BlockSpec(memory_space=pltpu.HBM)
    shape = lambda *dims: jax.ShapeDtypeStruct(dims, F32)
    params = pltpu.CompilerParams(vmem_limit_bytes=16 * 1024 * 1024)
    log_rates_t, residues_t = log_rates.T, residues.T

    def call(name, kernel, out_shape, operands, scratch=(), flops=0):
        return pl.pallas_call(
            kernel,
            out_shape=out_shape,
            in_specs=[vmem] * len(operands),
            out_specs=(vmem,) * len(out_shape),
            scratch_shapes=[pltpu.VMEM(dims, F32) for dims in scratch],
            compiler_params=params,
            cost_estimate=pl.CostEstimate(flops=flops, transcendentals=0, bytes_accessed=flops // 4),
            name=name,
        )(*operands)

    inputs = (log_rates_t, key_gate, values, upstream, query_gate)
    states, rate, mixed, carried, skip = pl.pallas_call(
        functools.partial(states_kernel, full),
        out_shape=(
            shape(8 * part, LANES),
            shape(tiles, modes, LANES),
            shape(tiles, rows, LANES),
            shape(tiles, rows, LANES),
            shape(tiles, LANES),
        ),
        in_specs=[in_hbm] * 5,
        out_specs=(vmem,) * 5,
        scratch_shapes=[
            pltpu.VMEM((modes, total_filters), F32),
            pltpu.VMEM((rows, channels), BF16),
            pltpu.VMEM((rows, channels), BF16),
            pltpu.VMEM((rows, channels), BF16),
            pltpu.VMEM((rows, channels), BF16),
            pltpu.VMEM((tiles, 4, TILE_FILTERS * modes, rows), BF16),
            pltpu.SemaphoreType.DMA((5,)),
        ],
        compiler_params=params,
        name="states",
    )(*(pltpu.with_memory_space_constraint(x, pltpu.HBM) for x in inputs))
    work = rows * channels * modes

    other_half = lax.dynamic_slice_in_dim(states, (1 - (position & 1)) * (4 * part), 4 * part, 0)
    partner = flip(other_half, 1)
    sums, starts, dealt = call(
        "within",
        within_kernel,
        (
            shape(tail, LANES),
            shape(tiles, 2, modes, SUB, LANES),
            shape(tiles, 2, rows // SUB, SUB, LANES),
        ),
        (rate, mixed, carried, skip),
        ((tiles, modes, LANES), (tiles, modes, LANES)),
        12 * work,
    )
    scale = results = None
    step = 1
    own, other, extra = states, after(partner, sums), (sums,)
    while 2 * step < context:
        is_last_next = 4 * step >= context
        own, borders, *send = call(
            "join",
            functools.partial(join_kernel, rows, step, is_last_next),
            (shape(4 * part + tail, LANES), shape(2 * part, LANES))
            + ((shape(2 * part + tail, LANES),) if is_last_next else ()),
            (rate, own, other, *extra),
        )
        other = flip(send[0] if send else own, 2 * step)
        if step == 1:
            scale, results = call(
                "block",
                functools.partial(block_kernel, full),
                (shape(tiles, modes, LANES), shape(tiles, 2, rows, LANES)),
                (
                    log_rates_t,
                    residues_t,
                    skip_weight.reshape(tiles, LANES),
                    after(rate, own),
                    dealt,
                    starts,
                ),
                ((2, rows // SUB, SUB, LANES),),
                8 * work,
            )
            other = after(other, results)
        extra = (borders,)
        step *= 2
    mine, back, modal = call(
        "last_join",
        functools.partial(last_join_kernel, rows, step),
        (shape(2 * part, LANES), shape(2 * part + tail, LANES), shape(modes, LANES)),
        (rate, own, other, borders, states, partner),
    )

    everyone = ("ctx", "grp")
    theirs = flip(back, 1)
    across, level = flip(modal, groups + 2, everyone), flip(modal, 2, everyone)
    columns = pl.BlockSpec((rows, channels // 2), lambda i: (0, i))
    outputs = pl.pallas_call(
        grads_kernel,
        grid=(2,),
        out_shape=(jax.ShapeDtypeStruct((rows, channels), BF16),) * 3,
        in_specs=[vmem] * 5 + [columns] * 3,
        out_specs=(columns,) * 3,
        compiler_params=params,
        cost_estimate=pl.CostEstimate(
            flops=4 * work, transcendentals=0, bytes_accessed=20 * rows * channels
        ),
        name="grads",
    )(mine, theirs, rate, scale, results, key_gate, values, upstream)
    query_grad, key_grad, value_grad = outputs
    across, level = (after(x, *outputs) for x in (across, level))
    here = jnp.concatenate([modal + theirs[2 * part : 2 * part + modes], level + across], axis=0)
    there = flip(here, 1, "grp")
    residue_grad, log_rate_grad, skip_grad = call(
        "final",
        functools.partial(final_kernel, full),
        (shape(modes, total_filters),) * 2 + (shape(tiles, LANES),),
        (log_rates_t, residues_t, back, theirs, here, there),
    )
    return (
        query_grad,
        key_grad,
        value_grad,
        skip_grad.reshape(channels),
        residue_grad.T,
        log_rate_grad.T,
    )


def solution(mesh):
    placed = (
        P("ctx", "grp"),
        P("ctx", "grp"),
        P("ctx", "grp"),
        P("ctx", "grp"),
        P("grp"),
        P(),
        P(),
    )
    return jax.shard_map(
        local,
        mesh=mesh,
        in_specs=placed,
        out_specs=(P("ctx", "grp"), P("ctx", "grp"), P("ctx", "grp"), P("grp"), P(), P()),
        check_vma=False,
    )
```

```python
import functools

import jax
import jax.numpy as jnp
from jax import lax
from jax.experimental import pallas as pl
from jax.experimental.pallas import tpu as pltpu
from jax.sharding import PartitionSpec as P

GROUP_CH = 16
LANES = 128
SUB = 8
TILE_FILTERS = LANES // GROUP_CH
HIGHEST = lax.Precision.HIGHEST
F32 = jnp.float32
BF16 = jnp.bfloat16


def own_columns(table, filters):
    total = table.shape[1]
    start = lax.axis_index("grp") * filters
    return pltpu.roll(table, lax.rem(total - start, total), 1)[:, :filters]


def group_mask(filters, channels):
    row = lax.broadcasted_iota(jnp.int32, (filters, channels), 0)
    col = lax.broadcasted_iota(jnp.int32, (filters, channels), 1)
    return jnp.where(row == lax.div(col, GROUP_CH), 1.0, 0.0).astype(F32)


def per_channel(table, mask):
    return jnp.dot(table, mask, precision=HIGHEST, preferred_element_type=F32)


def split(x):
    high = x.astype(BF16)
    return high, (x - high.astype(F32)).astype(BF16)


def wide_dot(a_high, a_low, b_high, b_low):
    return jnp.dot(
        jnp.concatenate([a_high, a_low, a_high], axis=1),
        jnp.concatenate([b_high, b_high, b_low], axis=0),
        preferred_element_type=F32,
    )


def spread(row):
    return jnp.broadcast_to(row, (SUB, LANES))


def sub_starts_back(ends, jumps):
    index = SUB - 1 - lax.broadcasted_iota(jnp.int32, (SUB, LANES), 0)
    out = []
    for end, jump in zip(ends, jumps):
        x = jnp.where(index == 0, 0.0, pltpu.roll(end, SUB - 1, 0))
        for n in (1, 2, 4):
            x = x + jnp.where(index >= n, jump, 0.0) * pltpu.roll(x, SUB - n, 0)
            jump = jump * jump
        out.append(x)
    return out


def fold_modes(products, modes):
    lane_filter = lax.div(lax.broadcasted_iota(jnp.int32, (modes, LANES), 1), GROUP_CH)
    parts = [
        jnp.where(lane_filter == f, products[f * modes : (f + 1) * modes, :], 0.0)
        for f in range(TILE_FILTERS)
    ]
    while len(parts) > 1:
        parts = [a + b for a, b in zip(parts[::2], parts[1::2])]
    return parts[0]


def states_kernel(
    full,
    log_rates_h,
    key_h,
    values_h,
    upstream_h,
    query_h,
    states,
    rate_out,
    mixed_out,
    carried_out,
    skip_out,
    rates_s,
    key,
    values,
    upstream,
    query,
    weight_s,
    sems,
):
    rows, channels = key.shape
    tiles = channels // LANES
    filters = channels // GROUP_CH
    modes = log_rates_h.shape[0]
    part = tiles // 2 * modes
    copies = [
        pltpu.make_async_copy(src, dst, sems.at[n])
        for n, (src, dst) in enumerate(
            (
                (log_rates_h, rates_s),
                (key_h, key),
                (values_h, values),
                (upstream_h, upstream),
                (query_h, query),
            )
        )
    ]
    for copy in copies:
        copy.start()
    copies[0].wait()
    step_rates = own_columns(jnp.exp(rates_s[...]), filters) * (1.0 / full)
    channel_rates = per_channel(step_rates, group_mask(filters, channels))
    time = lax.broadcasted_iota(jnp.int32, (modes, rows), 1).astype(F32)
    back_time = float(rows - 1) - time
    for f in range(filters):
        rate = jnp.broadcast_to(step_rates[:, f : f + 1], (modes, rows))
        ct, row = f // TILE_FILTERS, (f % TILE_FILTERS) * modes
        for way, away in enumerate((back_time, time)):
            high, low = split(jnp.exp(-rate * away))
            weight_s[ct, 2 * way, row : row + modes, :] = high
            weight_s[ct, 2 * way + 1, row : row + modes, :] = low
    for ct in range(tiles):
        rate_out[ct] = channel_rates[:, ct * LANES : (ct + 1) * LANES]
    forward = lax.broadcasted_iota(jnp.int32, (rows, LANES), 0).astype(F32)
    backward = float(rows - 1) - forward
    for copy in copies[1:]:
        copy.wait()
    for ct in range(tiles):
        lanes = slice(ct * LANES, (ct + 1) * LANES)
        mixed = key[:, lanes].astype(F32) * values[:, lanes].astype(F32)
        carried = upstream[:, lanes].astype(F32) * query[:, lanes].astype(F32)
        mixed_out[ct] = mixed
        carried_out[ct] = carried
        base = ct // (tiles // 2) * 4 * part + ct % (tiles // 2) * modes
        for way, (x, away) in enumerate(((mixed, backward), (carried, forward))):
            both = jnp.concatenate([x, x * away], axis=1)
            products = wide_dot(weight_s[ct, 2 * way], weight_s[ct, 2 * way + 1], *split(both))
            for n in range(2):
                at = base + (2 * way + n) * part
                states[at : at + modes, :] = fold_modes(products[:, n * LANES : (n + 1) * LANES], modes)
        skip_out[ct : ct + 1, :] = jnp.sum(mixed * carried, axis=0, keepdims=True)


def by_filter(firsts, seconds, first_filter, filters):
    modes = firsts[0].shape[0]
    both = jnp.concatenate([jnp.concatenate(v, axis=1) for v in (firsts, seconds)], axis=0)
    channels = both.shape[1]
    row = lax.broadcasted_iota(jnp.int32, (filters, channels), 0)
    col = lax.broadcasted_iota(jnp.int32, (filters, channels), 1)
    mask = jnp.where(row == first_filter + lax.div(col, GROUP_CH), 1.0, 0.0).astype(BF16)
    high, rest = split(both)
    middle, low = split(both - high.astype(F32))
    summed = lax.dot_general(
        jnp.concatenate([high, middle, low], axis=0),
        mask,
        (((1,), (1,)), ((), ())),
        preferred_element_type=F32,
    )
    summed = summed[: 2 * modes] + summed[2 * modes : 4 * modes] + summed[4 * modes :]
    return jnp.concatenate([summed[:modes], summed[modes:]], axis=1)


def sub_spans(x_ref, decay, reverse):
    steps = x_ref.shape[0]
    state = slope = None
    for i in range(steps - 1, -1, -1) if reverse else range(steps):
        x = x_ref[i]
        if state is None:
            state = [x] * len(decay)
            continue
        moved = [d * s for d, s in zip(decay, state)]
        slope = moved if slope is None else [d * t + a for d, t, a in zip(decay, slope, moved)]
        state = [a + x for a in moved]
    return state, slope


def sub_starts_both(ends, slopes, jumps, span):
    index = lax.broadcasted_iota(jnp.int32, (SUB, LANES), 0)
    starts, start_slopes = [], []
    for end, slope, jump in zip(ends, slopes, jumps):
        x = jnp.where(index == 0, 0.0, pltpu.roll(end, 1, 0))
        y = jnp.where(index == 0, 0.0, pltpu.roll(slope, 1, 0))
        for n in (1, 2, 4):
            hop = jnp.where(index >= n, jump, 0.0)
            x_far = pltpu.roll(x, n, 0)
            y = y + hop * (pltpu.roll(y, n, 0) + float(n * span) * x_far)
            x = x + hop * x_far
            jump = jump * jump
        starts.append(x)
        start_slopes.append(y)
    return starts, start_slopes


def within_kernel(rate_ref, mixed_ref, carried_ref, skip, sums, starts, dealt, first_s, second_s):
    tiles, rows, _ = mixed_ref.shape
    modes = rate_ref.shape[1]
    steps = rows // SUB
    half = modes // 2
    total = lambda v: jnp.sum(v, axis=0, keepdims=True)

    def tile(ct, _):
        rate = rate_ref[ct]
        step_decay = jnp.exp(-rate)
        sub_decay = jnp.exp(-rate * float(steps))
        firsts, seconds = [], []
        for i in range(steps):
            for way, ref in enumerate((mixed_ref, carried_ref)):
                dealt[ct, way, i] = ref[ct, pl.ds(i, SUB, stride=steps), :]
        for lo in range(0, modes, half):
            decay = [spread(step_decay[m : m + 1, :]) for m in range(lo, lo + half)]
            jumps = [spread(sub_decay[m : m + 1, :]) for m in range(lo, lo + half)]
            ends, end_slopes = sub_spans(dealt.at[ct, 0], decay, False)
            before, before_slopes = sub_starts_both(ends, end_slopes, jumps, steps)
            behind, behind_slopes = sub_spans(dealt.at[ct, 1], decay, True)
            for m in range(half):
                starts[ct, 0, lo + m] = before[m]
                starts[ct, 1, lo + m] = behind[m]
                reached = decay[m] * before[m]
                firsts.append(total(reached * behind[m]))
                seconds.append(
                    total(
                        (decay[m] * before_slopes[m]) * behind[m]
                        + reached * (behind[m] + behind_slopes[m])
                    )
                )
        x = [dealt[ct, 0, i] for i in range(steps)]
        c = [dealt[ct, 1, i] for i in range(steps)]
        first = second = jnp.zeros((modes, LANES), F32)
        for lag in range(steps - 1, -1, -1):
            terms = [c[i + lag] * x[i] for i in range(steps - lag)]
            while len(terms) > 1:
                odd = terms[len(terms) // 2 * 2 :]
                terms = [a + b for a, b in zip(terms[::2], terms[1::2])] + odd
            moved = step_decay * first
            second = step_decay * second + moved
            first = moved + total(terms[0])
        first_s[ct] = first + jnp.concatenate(firsts, axis=0)
        second_s[ct] = second + jnp.concatenate(seconds, axis=0)
        return 0

    lax.fori_loop(0, tiles, tile, 0)
    packet = by_filter(
        [first_s[ct] for ct in range(tiles)],
        [second_s[ct] for ct in range(tiles)],
        0,
        tiles * TILE_FILTERS,
    )
    sums[:modes, :] = packet
    sums[modes:, :] = skip[...]


def spans_join(own, other, rate, upper, span):
    low = [jnp.where(upper, o, w) for w, o in zip(own, other)]
    high = [jnp.where(upper, w, o) for w, o in zip(own, other)]
    decay = jnp.exp(-rate)
    first = decay * (low[0] * high[2])
    second = decay * (low[1] * high[2] + low[0] * (high[2] + high[3]))
    far = jnp.exp(-rate * float(span))
    joined = (
        far * low[0] + high[0],
        far * (low[1] + float(span) * low[0]) + high[1],
        low[2] + far * high[2],
        low[3] + far * (high[3] + float(span) * high[2]),
    )
    return joined, first, second


def border_sums(first, second, tiles, modes):
    cut = lambda v: [v[n * modes : (n + 1) * modes, :] for n in range(tiles // 2)]
    begin = (lax.axis_index("ctx") & 1) * (tiles // 2 * TILE_FILTERS)
    return by_filter(cut(first), cut(second), begin, tiles * TILE_FILTERS)


def half_rates(rate_ref):
    tiles, modes, _ = rate_ref.shape
    begin = (lax.axis_index("ctx") & 1) * (tiles // 2)
    return jnp.concatenate([rate_ref[begin + n] for n in range(tiles // 2)], axis=0)


def join_kernel(rows, step, is_last_next, rate_ref, own_ref, other_ref, *refs):
    tiles, modes, _ = rate_ref.shape
    part = tiles // 2 * modes
    if step == 1:
        sums_ref, joined_ref, borders_ref, *send = refs
        begin = (lax.axis_index("ctx") & 1) * (4 * part)
        own = [own_ref[pl.ds(pl.multiple_of(begin + q * part, part), part), :] for q in range(4)]
        sums = sums_ref[...]
    else:
        old_borders, joined_ref, borders_ref, *send = refs
        own = [own_ref[q * part : (q + 1) * part, :] for q in range(4)]
        sums = own_ref[4 * part :, :] + other_ref[4 * part :, :]
    other = [other_ref[q * part : (q + 1) * part, :] for q in range(4)]
    position = lax.axis_index("ctx")
    upper = (position & step) != 0
    rate = half_rates(rate_ref)
    joined, first, second = spans_join(own, other, rate, upper, rows * step)
    for q in range(4):
        joined_ref[q * part : (q + 1) * part, :] = joined[q]
    sums = jnp.concatenate([sums[:modes] + border_sums(first, second, tiles, modes), sums[modes:]], axis=0)
    joined_ref[4 * part :, :] = sums
    if step == 1:
        borders_ref[...] = jnp.zeros_like(borders_ref)
    else:
        borders_ref[...] = add_borders(
            rows, step, rate, [old_borders[:part, :], old_borders[part:, :]], other[0], other[2]
        )
    if is_last_next:
        next_upper = (position & (2 * step)) != 0
        for q in range(2):
            send[0][q * part : (q + 1) * part, :] = jnp.where(next_upper, joined[2 + q], joined[q])
        send[0][2 * part :, :] = sums


def add_borders(rows, step, rate, borders, forward, backward):
    position = lax.axis_index("ctx")
    upper = (position & step) != 0
    before = ((position & (step - 1)) >> 1).astype(F32) * float(2 * rows)
    behind = float(rows * (step - 2)) - before
    return jnp.concatenate(
        [
            borders[0] + jnp.where(upper, jnp.exp(-rate * before) * forward, 0.0),
            borders[1] + jnp.where(upper, 0.0, jnp.exp(-rate * behind) * backward),
        ],
        axis=0,
    )


def last_join_kernel(
    rows, step, rate_ref, own_ref, other_ref, borders_ref, states_ref, partner_ref, mine_ref, back_ref, modal_ref
):
    tiles, modes, _ = rate_ref.shape
    part = tiles // 2 * modes
    position = lax.axis_index("ctx")
    upper = (position & step) != 0
    rate = half_rates(rate_ref)
    own = [own_ref[q * part : (q + 1) * part, :] for q in range(4)]
    other = [other_ref[q * part : (q + 1) * part, :] for q in range(2)]
    _, first, second = spans_join(own, other + other, rate, upper, rows * step)
    sums = own_ref[4 * part :, :] + other_ref[2 * part :, :]
    modal = sums[:modes] + border_sums(first, second, tiles, modes)
    modal_ref[...] = modal
    back_ref[2 * part : 2 * part + modes, :] = modal
    back_ref[2 * part + modes :, :] = sums[modes:]
    borders = add_borders(
        rows, step, rate, [borders_ref[:part, :], borders_ref[part:, :]], other[0], other[0]
    )
    incoming, outgoing = borders[:part], borders[part:]
    far = jnp.exp(-rate * float(rows))
    begin = (position & 1) * (4 * part)
    pick = lambda q: states_ref[pl.ds(pl.multiple_of(begin + q * part, part), part), :]
    second_block = (position & 1) != 0
    through = far * incoming
    across = far * outgoing
    for ref, is_second, forward, backward in (
        (mine_ref, second_block, partner_ref[:part, :], partner_ref[2 * part : 3 * part, :]),
        (back_ref, jnp.logical_not(second_block), pick(0), pick(2)),
    ):
        ref[:part, :] = jnp.where(is_second, through + forward, incoming)
        ref[part : 2 * part, :] = jnp.where(is_second, outgoing, across + backward)


def block_kernel(
    full, log_rates, residues, skip_weight, rate_ref, dealt, starts, scales, results, result_s
):
    tiles, modes, _ = rate_ref.shape
    filters = tiles * TILE_FILTERS
    steps = dealt.shape[2]
    half = modes // 2
    scaled = own_columns(residues[...], filters) * jnp.sqrt(
        jnp.exp(own_columns(log_rates[...], filters)) / full
    )
    scaled = per_channel(scaled, group_mask(filters, tiles * LANES))
    for n in range(tiles):
        scales[n] = scaled[:, n * LANES : (n + 1) * LANES]

    def tile(ct, _):
        step_decay = jnp.exp(-rate_ref[ct])
        sub_decay = jnp.exp(-rate_ref[ct] * float(steps))
        scale = scales[ct]
        weight = spread(skip_weight[pl.ds(ct, 1), :])
        for lo in range(0, modes, half):
            decay = [spread(step_decay[m : m + 1, :]) for m in range(lo, lo + half)]
            gains = [spread(scale[m : m + 1, :]) for m in range(lo, lo + half)]
            for way in range(2):
                state = [starts[ct, way, lo + m] for m in range(half)]
                if way:
                    state = sub_starts_back(
                        state, [spread(sub_decay[m : m + 1, :]) for m in range(lo, lo + half)]
                    )
                for i in range(steps - 1, -1, -1) if way else range(steps):
                    x = dealt[ct, way, i]
                    state = [d * s + x for d, s in zip(decay, state)]
                    terms = [g * s for g, s in zip(gains, state)]
                    terms.append(result_s[way, i] if lo > 0 else weight * x)
                    while len(terms) > 1:
                        odd = terms[len(terms) // 2 * 2 :]
                        terms = [a + b for a, b in zip(terms[::2], terms[1::2])] + odd
                    if lo > 0:
                        results[ct, way, pl.ds(i, SUB, stride=steps), :] = terms[0]
                    else:
                        result_s[way, i] = terms[0]
        return 0

    lax.fori_loop(0, tiles, tile, 0)


def reach_kernel(rate_ref, reach):
    tiles, modes, _ = rate_ref.shape
    rows = reach.shape[3]
    lane = lax.broadcasted_iota(jnp.int32, (modes, LANES), 1)
    own_mode = lax.broadcasted_iota(jnp.int32, (modes, LANES), 0) == lax.rem(lane, modes)
    time = lax.broadcasted_iota(jnp.int32, (rows, LANES), 0).astype(F32)
    for ct in range(tiles):
        rate_row = jnp.sum(jnp.where(own_mode, rate_ref[ct], 0.0), axis=0, keepdims=True)
        for way, away in enumerate((time + 1.0, float(rows) - time)):
            high, low = split(jnp.exp(-rate_row * away))
            reach[ct, way, 0] = high
            reach[ct, way, 1] = low


def grads_kernel(mine, theirs, reach, scale_ref, results, key, values, upstream, *refs):
    outs, made, sems = refs[:3], refs[3:6], refs[6]
    tiles, modes, _ = scale_ref.shape
    share = tiles // 2
    part = share * modes
    second_half = (lax.axis_index("ctx") & 1) != 0
    lane_filter = lax.div(lax.broadcasted_iota(jnp.int32, (modes, LANES), 1), GROUP_CH)
    copies = []
    for ct in range(tiles):
        is_mine = second_half if ct >= share else jnp.logical_not(second_half)
        parts = []
        for way in range(2):
            at = slice(way * part + ct % share * modes, way * part + (ct % share + 1) * modes)
            edge = scale_ref[ct] * jnp.where(is_mine, mine[at, :], theirs[at, :])
            spaced = jnp.concatenate(
                [jnp.where(lane_filter == f, edge, 0.0) for f in range(TILE_FILTERS)], axis=0
            )
            parts.append(wide_dot(reach[ct, way, 0], reach[ct, way, 1], *split(spaced)))
        lanes = slice(ct * LANES, (ct + 1) * LANES)
        mixed_grad = results[ct, 1] + parts[1]
        for made_ref, factor, grad in zip(
            made, (upstream, values, key), (results[ct, 0] + parts[0], mixed_grad, mixed_grad)
        ):
            made_ref[:, lanes] = (factor[:, lanes].astype(F32) * grad).astype(made_ref.dtype)
        if ct % 2 == 1:
            lanes = slice((ct - 1) * LANES, (ct + 1) * LANES)
            for n, (made_ref, out) in enumerate(zip(made, outs)):
                copies.append(
                    pltpu.make_async_copy(made_ref.at[:, lanes], out.at[:, lanes], sems.at[ct // 2, n])
                )
                copies[-1].start()
    for copy in copies:
        copy.wait()


def final_kernel(
    full, log_rates, residues, back, theirs, here, there, residue_grad, log_rate_grad, skip_grad
):
    modes, total_filters = log_rates.shape
    filters = here.shape[1] // 2
    group = lax.axis_index("grp")
    skip_rows = slice(back.shape[0] - skip_grad.shape[0], back.shape[0])
    skip_grad[...] = (back[skip_rows, :] + theirs[skip_rows, :]) / jnp.sqrt(jnp.float32(full))
    rows = [slice(n * modes, (n + 1) * modes) for n in range(3)]
    by_distance = [
        here[rows[0], :],
        there[rows[0], :],
        here[rows[1], :] + there[rows[2], :],
        here[rows[2], :] + there[rows[1], :],
    ]
    totals = []
    for g in range(total_filters // filters):
        total = by_distance[0]
        for k in range(1, len(by_distance)):
            total = jnp.where((group ^ k) == g, by_distance[k], total)
        totals.append(total)
    first_sum = jnp.concatenate([t[:, :filters] for t in totals], axis=1)
    second_sum = jnp.concatenate([t[:, filters:] for t in totals], axis=1) * (1.0 / full)
    rates = jnp.exp(log_rates[...])
    root = jnp.sqrt(rates / full)
    scale_root = jnp.sqrt(jnp.float32(full))
    residue_grad[...] = root * first_sum / scale_root
    log_rate_grad[...] = residues[...] * root * (0.5 * first_sum - rates * second_sum) / scale_root


def flip(x, step, axis="ctx"):
    return lax.ppermute(x, axis, [(i, i ^ step) for i in range(lax.axis_size(axis))])


def after(x, *others):
    return lax.optimization_barrier((x, *others))[0]


def local(query_gate, key_gate, values, upstream, skip_weight, residues, log_rates):
    context = lax.axis_size("ctx")
    groups = lax.axis_size("grp")
    position = lax.axis_index("ctx")
    rows, channels = query_gate.shape
    total_filters, modes = residues.shape
    filters = channels // GROUP_CH
    tiles = channels // LANES
    full = rows * context
    part = tiles // 2 * modes
    tail = modes + tiles
    assert context >= 4 and context & (context - 1) == 0 and groups == 4
    vmem = pl.BlockSpec(memory_space=pltpu.VMEM)
    in_hbm = pl.BlockSpec(memory_space=pltpu.HBM)
    shape = lambda *dims: jax.ShapeDtypeStruct(dims, F32)
    params = pltpu.CompilerParams(vmem_limit_bytes=16 * 1024 * 1024)
    log_rates_t, residues_t = log_rates.T, residues.T

    def call(name, kernel, out_shape, operands, scratch=(), flops=0):
        return pl.pallas_call(
            kernel,
            out_shape=out_shape,
            in_specs=[vmem] * len(operands),
            out_specs=(vmem,) * len(out_shape),
            scratch_shapes=[pltpu.VMEM(dims, F32) for dims in scratch],
            compiler_params=params,
            cost_estimate=pl.CostEstimate(flops=flops, transcendentals=0, bytes_accessed=flops // 4),
            name=name,
        )(*operands)

    inputs = (log_rates_t, key_gate, values, upstream, query_gate)
    states, rate, mixed, carried, skip = pl.pallas_call(
        functools.partial(states_kernel, full),
        out_shape=(
            shape(8 * part, LANES),
            shape(tiles, modes, LANES),
            shape(tiles, rows, LANES),
            shape(tiles, rows, LANES),
            shape(tiles, LANES),
        ),
        in_specs=[in_hbm] * 5,
        out_specs=(vmem,) * 5,
        scratch_shapes=[
            pltpu.VMEM((modes, total_filters), F32),
            pltpu.VMEM((rows, channels), BF16),
            pltpu.VMEM((rows, channels), BF16),
            pltpu.VMEM((rows, channels), BF16),
            pltpu.VMEM((rows, channels), BF16),
            pltpu.VMEM((tiles, 4, TILE_FILTERS * modes, rows), BF16),
            pltpu.SemaphoreType.DMA((5,)),
        ],
        compiler_params=params,
        name="states",
    )(*(pltpu.with_memory_space_constraint(x, pltpu.HBM) for x in inputs))
    work = rows * channels * modes

    other_half = lax.dynamic_slice_in_dim(states, (1 - (position & 1)) * (4 * part), 4 * part, 0)
    partner = flip(other_half, 1)
    sums, starts, dealt = call(
        "within",
        within_kernel,
        (
            shape(tail, LANES),
            shape(tiles, 2, modes, SUB, LANES),
            shape(tiles, 2, rows // SUB, SUB, LANES),
        ),
        (rate, mixed, carried, skip),
        ((tiles, modes, LANES), (tiles, modes, LANES)),
        12 * work,
    )
    scale = results = reach = None
    step = 1
    own, other, extra = states, after(partner, sums), (sums,)
    while 2 * step < context:
        is_last_next = 4 * step >= context
        own, borders, *send = call(
            "join",
            functools.partial(join_kernel, rows, step, is_last_next),
            (shape(4 * part + tail, LANES), shape(2 * part, LANES))
            + ((shape(2 * part + tail, LANES),) if is_last_next else ()),
            (rate, own, other, *extra),
        )
        other = flip(send[0] if send else own, 2 * step)
        if step == 1:
            scale, results = call(
                "block",
                functools.partial(block_kernel, full),
                (shape(tiles, modes, LANES), shape(tiles, 2, rows, LANES)),
                (
                    log_rates_t,
                    residues_t,
                    skip_weight.reshape(tiles, LANES),
                    after(rate, own),
                    dealt,
                    starts,
                ),
                ((2, rows // SUB, SUB, LANES),),
                8 * work,
            )
            other = after(other, results)
        if is_last_next:
            reach = pl.pallas_call(
                reach_kernel,
                out_shape=jax.ShapeDtypeStruct((tiles, 2, 2, rows, LANES), BF16),
                in_specs=[vmem],
                out_specs=vmem,
                compiler_params=params,
                name="reach",
            )(after(rate, own))
            other = after(other, reach)
        extra = (borders,)
        step *= 2
    mine, back, modal = call(
        "last_join",
        functools.partial(last_join_kernel, rows, step),
        (shape(2 * part, LANES), shape(2 * part + tail, LANES), shape(modes, LANES)),
        (rate, own, other, borders, states, partner),
    )

    duo = jnp.concatenate([modal, flip(modal, 1, "grp")], axis=0)
    theirs = flip(back, 1)
    far = lax.ppermute(
        duo,
        ("ctx", "grp"),
        [(i, i ^ (groups + 2 if i & 1 else 2)) for i in range(context * groups)],
    )
    grad = jax.ShapeDtypeStruct((rows, channels), BF16)
    outputs = pl.pallas_call(
        grads_kernel,
        out_shape=(grad,) * 3,
        in_specs=[vmem] * 8,
        out_specs=(in_hbm,) * 3,
        scratch_shapes=[pltpu.VMEM((rows, channels), BF16)] * 3
        + [pltpu.SemaphoreType.DMA((tiles // 2, 3))],
        compiler_params=params,
        cost_estimate=pl.CostEstimate(
            flops=4 * work, transcendentals=0, bytes_accessed=20 * rows * channels
        ),
        name="grads",
    )(mine, theirs, reach, scale, results, key_gate, values, upstream)
    query_grad, key_grad, value_grad = outputs
    here = jnp.concatenate([modal + theirs[2 * part : 2 * part + modes], far], axis=0)
    there = after(flip(here, 1, "grp"), *outputs)
    residue_grad, log_rate_grad, skip_grad = call(
        "final",
        functools.partial(final_kernel, full),
        (shape(modes, total_filters),) * 2 + (shape(tiles, LANES),),
        (log_rates_t, residues_t, back, theirs, here, there),
    )
    return (
        query_grad,
        key_grad,
        value_grad,
        skip_grad.reshape(channels),
        residue_grad.T,
        log_rate_grad.T,
    )


def solution(mesh):
    placed = (
        P("ctx", "grp"),
        P("ctx", "grp"),
        P("ctx", "grp"),
        P("ctx", "grp"),
        P("grp"),
        P(),
        P(),
    )
    return jax.shard_map(
        local,
        mesh=mesh,
        in_specs=placed,
        out_specs=(P("ctx", "grp"), P("ctx", "grp"), P("ctx", "grp"), P("grp"), P(), P()),
        check_vma=False,
    )
```

```python
import functools

import jax
import jax.numpy as jnp
from jax import lax
from jax.experimental import pallas as pl
from jax.experimental.pallas import tpu as pltpu
from jax.sharding import PartitionSpec as P

GROUP_CH = 16
LANES = 128
SUB = 8
TILE_FILTERS = LANES // GROUP_CH
HIGHEST = lax.Precision.HIGHEST
F32 = jnp.float32
BF16 = jnp.bfloat16


def own_columns(table, filters):
    total = table.shape[1]
    start = lax.axis_index("grp") * filters
    return pltpu.roll(table, lax.rem(total - start, total), 1)[:, :filters]


def group_mask(filters, channels):
    row = lax.broadcasted_iota(jnp.int32, (filters, channels), 0)
    col = lax.broadcasted_iota(jnp.int32, (filters, channels), 1)
    return jnp.where(row == lax.div(col, GROUP_CH), 1.0, 0.0).astype(F32)


def per_channel(table, mask):
    return jnp.dot(table, mask, precision=HIGHEST, preferred_element_type=F32)


def split(x):
    high = x.astype(BF16)
    return high, (x - high.astype(F32)).astype(BF16)


def wide_dot(a_high, a_low, b_high, b_low):
    return jnp.dot(
        jnp.concatenate([a_high, a_low, a_high], axis=1),
        jnp.concatenate([b_high, b_high, b_low], axis=0),
        preferred_element_type=F32,
    )


def spread(row):
    return jnp.broadcast_to(row, (SUB, LANES))


def sub_starts_back(ends, jumps):
    index = SUB - 1 - lax.broadcasted_iota(jnp.int32, (SUB, LANES), 0)
    out = []
    for end, jump in zip(ends, jumps):
        x = jnp.where(index == 0, 0.0, pltpu.roll(end, SUB - 1, 0))
        for n in (1, 2, 4):
            x = x + jnp.where(index >= n, jump, 0.0) * pltpu.roll(x, SUB - n, 0)
            jump = jump * jump
        out.append(x)
    return out


def fold_modes(products, modes):
    lane_filter = lax.div(lax.broadcasted_iota(jnp.int32, (modes, LANES), 1), GROUP_CH)
    parts = [
        jnp.where(lane_filter == f, products[f * modes : (f + 1) * modes, :], 0.0)
        for f in range(TILE_FILTERS)
    ]
    while len(parts) > 1:
        parts = [a + b for a, b in zip(parts[::2], parts[1::2])]
    return parts[0]


def states_kernel(
    full,
    log_rates_h,
    key_h,
    values_h,
    upstream_h,
    query_h,
    states,
    rate_out,
    mixed_out,
    carried_out,
    skip_out,
    rates_s,
    key,
    values,
    upstream,
    query,
    weight_s,
    sems,
):
    rows, channels = key.shape
    tiles = channels // LANES
    filters = channels // GROUP_CH
    modes = log_rates_h.shape[0]
    part = tiles // 2 * modes
    copies = [
        pltpu.make_async_copy(src, dst, sems.at[n])
        for n, (src, dst) in enumerate(
            (
                (log_rates_h, rates_s),
                (key_h, key),
                (values_h, values),
                (upstream_h, upstream),
                (query_h, query),
            )
        )
    ]
    for copy in copies:
        copy.start()
    copies[0].wait()
    step_rates = own_columns(jnp.exp(rates_s[...]), filters) * (1.0 / full)
    channel_rates = per_channel(step_rates, group_mask(filters, channels))
    time = lax.broadcasted_iota(jnp.int32, (modes, rows), 1).astype(F32)
    back_time = float(rows - 1) - time
    for f in range(filters):
        rate = jnp.broadcast_to(step_rates[:, f : f + 1], (modes, rows))
        ct, row = f // TILE_FILTERS, (f % TILE_FILTERS) * modes
        for way, away in enumerate((back_time, time)):
            high, low = split(jnp.exp(-rate * away))
            weight_s[ct, 2 * way, row : row + modes, :] = high
            weight_s[ct, 2 * way + 1, row : row + modes, :] = low
    for ct in range(tiles):
        rate_out[ct] = channel_rates[:, ct * LANES : (ct + 1) * LANES]
    forward = lax.broadcasted_iota(jnp.int32, (rows, LANES), 0).astype(F32)
    backward = float(rows - 1) - forward
    for copy in copies[1:]:
        copy.wait()
    for ct in range(tiles):
        lanes = slice(ct * LANES, (ct + 1) * LANES)
        mixed = key[:, lanes].astype(F32) * values[:, lanes].astype(F32)
        carried = upstream[:, lanes].astype(F32) * query[:, lanes].astype(F32)
        mixed_out[ct] = mixed
        carried_out[ct] = carried
        base = ct // (tiles // 2) * 4 * part + ct % (tiles // 2) * modes
        for way, (x, away) in enumerate(((mixed, backward), (carried, forward))):
            both = jnp.concatenate([x, x * away], axis=1)
            products = wide_dot(weight_s[ct, 2 * way], weight_s[ct, 2 * way + 1], *split(both))
            for n in range(2):
                at = base + (2 * way + n) * part
                states[at : at + modes, :] = fold_modes(products[:, n * LANES : (n + 1) * LANES], modes)
        skip_out[ct : ct + 1, :] = jnp.sum(mixed * carried, axis=0, keepdims=True)


def by_filter(firsts, seconds, first_filter, filters):
    modes = firsts[0].shape[0]
    both = jnp.concatenate([jnp.concatenate(v, axis=1) for v in (firsts, seconds)], axis=0)
    channels = both.shape[1]
    row = lax.broadcasted_iota(jnp.int32, (filters, channels), 0)
    col = lax.broadcasted_iota(jnp.int32, (filters, channels), 1)
    mask = jnp.where(row == first_filter + lax.div(col, GROUP_CH), 1.0, 0.0).astype(BF16)
    high, rest = split(both)
    middle, low = split(both - high.astype(F32))
    summed = lax.dot_general(
        jnp.concatenate([high, middle, low], axis=0),
        mask,
        (((1,), (1,)), ((), ())),
        preferred_element_type=F32,
    )
    summed = summed[: 2 * modes] + summed[2 * modes : 4 * modes] + summed[4 * modes :]
    return jnp.concatenate([summed[:modes], summed[modes:]], axis=1)


def sub_spans(x_ref, decay, reverse):
    steps = x_ref.shape[0]
    state = slope = None
    for i in range(steps - 1, -1, -1) if reverse else range(steps):
        x = x_ref[i]
        if state is None:
            state = [x] * len(decay)
            continue
        moved = [d * s for d, s in zip(decay, state)]
        slope = moved if slope is None else [d * t + a for d, t, a in zip(decay, slope, moved)]
        state = [a + x for a in moved]
    return state, slope


def sub_starts_both(ends, slopes, jumps, span):
    index = lax.broadcasted_iota(jnp.int32, (SUB, LANES), 0)
    starts, start_slopes = [], []
    for end, slope, jump in zip(ends, slopes, jumps):
        x = jnp.where(index == 0, 0.0, pltpu.roll(end, 1, 0))
        y = jnp.where(index == 0, 0.0, pltpu.roll(slope, 1, 0))
        for n in (1, 2, 4):
            hop = jnp.where(index >= n, jump, 0.0)
            x_far = pltpu.roll(x, n, 0)
            y = y + hop * (pltpu.roll(y, n, 0) + float(n * span) * x_far)
            x = x + hop * x_far
            jump = jump * jump
        starts.append(x)
        start_slopes.append(y)
    return starts, start_slopes


def within_kernel(rate_ref, mixed_ref, carried_ref, skip, sums, starts, dealt, first_s, second_s):
    tiles, rows, _ = mixed_ref.shape
    modes = rate_ref.shape[1]
    steps = rows // SUB
    half = modes // 2
    total = lambda v: jnp.sum(v, axis=0, keepdims=True)

    def tile(ct, _):
        rate = rate_ref[ct]
        step_decay = jnp.exp(-rate)
        sub_decay = jnp.exp(-rate * float(steps))
        firsts, seconds = [], []
        for i in range(steps):
            for way, ref in enumerate((mixed_ref, carried_ref)):
                dealt[ct, way, i] = ref[ct, pl.ds(i, SUB, stride=steps), :]
        for lo in range(0, modes, half):
            decay = [spread(step_decay[m : m + 1, :]) for m in range(lo, lo + half)]
            jumps = [spread(sub_decay[m : m + 1, :]) for m in range(lo, lo + half)]
            ends, end_slopes = sub_spans(dealt.at[ct, 0], decay, False)
            before, before_slopes = sub_starts_both(ends, end_slopes, jumps, steps)
            behind, behind_slopes = sub_spans(dealt.at[ct, 1], decay, True)
            for m in range(half):
                starts[ct, 0, lo + m] = before[m]
                starts[ct, 1, lo + m] = behind[m]
                reached = decay[m] * before[m]
                firsts.append(total(reached * behind[m]))
                seconds.append(
                    total(
                        (decay[m] * before_slopes[m]) * behind[m]
                        + reached * (behind[m] + behind_slopes[m])
                    )
                )
        x = [dealt[ct, 0, i] for i in range(steps)]
        c = [dealt[ct, 1, i] for i in range(steps)]
        first = second = jnp.zeros((modes, LANES), F32)
        for lag in range(steps - 1, -1, -1):
            terms = [c[i + lag] * x[i] for i in range(steps - lag)]
            while len(terms) > 1:
                odd = terms[len(terms) // 2 * 2 :]
                terms = [a + b for a, b in zip(terms[::2], terms[1::2])] + odd
            moved = step_decay * first
            second = step_decay * second + moved
            first = moved + total(terms[0])
        first_s[ct] = first + jnp.concatenate(firsts, axis=0)
        second_s[ct] = second + jnp.concatenate(seconds, axis=0)
        return 0

    lax.fori_loop(0, tiles, tile, 0)
    packet = by_filter(
        [first_s[ct] for ct in range(tiles)],
        [second_s[ct] for ct in range(tiles)],
        0,
        tiles * TILE_FILTERS,
    )
    sums[:modes, :] = packet
    sums[modes:, :] = skip[...]


def spans_join(own, other, rate, upper, span):
    low = [jnp.where(upper, o, w) for w, o in zip(own, other)]
    high = [jnp.where(upper, w, o) for w, o in zip(own, other)]
    decay = jnp.exp(-rate)
    first = decay * (low[0] * high[2])
    second = decay * (low[1] * high[2] + low[0] * (high[2] + high[3]))
    far = jnp.exp(-rate * float(span))
    joined = (
        far * low[0] + high[0],
        far * (low[1] + float(span) * low[0]) + high[1],
        low[2] + far * high[2],
        low[3] + far * (high[3] + float(span) * high[2]),
    )
    return joined, first, second


def border_sums(first, second, tiles, modes):
    cut = lambda v: [v[n * modes : (n + 1) * modes, :] for n in range(tiles // 2)]
    begin = (lax.axis_index("ctx") & 1) * (tiles // 2 * TILE_FILTERS)
    return by_filter(cut(first), cut(second), begin, tiles * TILE_FILTERS)


def half_rates(rate_ref):
    tiles, modes, _ = rate_ref.shape
    begin = (lax.axis_index("ctx") & 1) * (tiles // 2)
    return jnp.concatenate([rate_ref[begin + n] for n in range(tiles // 2)], axis=0)


def join_kernel(rows, step, is_last_next, rate_ref, own_ref, other_ref, *refs):
    tiles, modes, _ = rate_ref.shape
    part = tiles // 2 * modes
    if step == 1:
        sums_ref, joined_ref, borders_ref, *send = refs
        begin = (lax.axis_index("ctx") & 1) * (4 * part)
        own = [own_ref[pl.ds(pl.multiple_of(begin + q * part, part), part), :] for q in range(4)]
        sums = sums_ref[...]
    else:
        old_borders, joined_ref, borders_ref, *send = refs
        own = [own_ref[q * part : (q + 1) * part, :] for q in range(4)]
        sums = own_ref[4 * part :, :] + other_ref[4 * part :, :]
    other = [other_ref[q * part : (q + 1) * part, :] for q in range(4)]
    position = lax.axis_index("ctx")
    upper = (position & step) != 0
    rate = half_rates(rate_ref)
    joined, first, second = spans_join(own, other, rate, upper, rows * step)
    for q in range(4):
        joined_ref[q * part : (q + 1) * part, :] = joined[q]
    sums = jnp.concatenate([sums[:modes] + border_sums(first, second, tiles, modes), sums[modes:]], axis=0)
    joined_ref[4 * part :, :] = sums
    if step == 1:
        borders_ref[...] = jnp.zeros_like(borders_ref)
    else:
        borders_ref[...] = add_borders(
            rows, step, rate, [old_borders[:part, :], old_borders[part:, :]], other[0], other[2]
        )
    if is_last_next:
        next_upper = (position & (2 * step)) != 0
        for q in range(2):
            send[0][q * part : (q + 1) * part, :] = jnp.where(next_upper, joined[2 + q], joined[q])
        send[0][2 * part :, :] = sums


def add_borders(rows, step, rate, borders, forward, backward):
    position = lax.axis_index("ctx")
    upper = (position & step) != 0
    before = ((position & (step - 1)) >> 1).astype(F32) * float(2 * rows)
    behind = float(rows * (step - 2)) - before
    return jnp.concatenate(
        [
            borders[0] + jnp.where(upper, jnp.exp(-rate * before) * forward, 0.0),
            borders[1] + jnp.where(upper, 0.0, jnp.exp(-rate * behind) * backward),
        ],
        axis=0,
    )


def last_join_kernel(
    rows, step, rate_ref, own_ref, other_ref, borders_ref, states_ref, partner_ref, mine_ref, back_ref, modal_ref
):
    tiles, modes, _ = rate_ref.shape
    part = tiles // 2 * modes
    position = lax.axis_index("ctx")
    upper = (position & step) != 0
    rate = half_rates(rate_ref)
    own = [own_ref[q * part : (q + 1) * part, :] for q in range(4)]
    other = [other_ref[q * part : (q + 1) * part, :] for q in range(2)]
    _, first, second = spans_join(own, other + other, rate, upper, rows * step)
    sums = own_ref[4 * part :, :] + other_ref[2 * part :, :]
    modal = sums[:modes] + border_sums(first, second, tiles, modes)
    modal_ref[...] = modal
    back_ref[2 * part : 2 * part + modes, :] = modal
    back_ref[2 * part + modes :, :] = sums[modes:]
    borders = add_borders(
        rows, step, rate, [borders_ref[:part, :], borders_ref[part:, :]], other[0], other[0]
    )
    incoming, outgoing = borders[:part], borders[part:]
    far = jnp.exp(-rate * float(rows))
    begin = (position & 1) * (4 * part)
    pick = lambda q: states_ref[pl.ds(pl.multiple_of(begin + q * part, part), part), :]
    second_block = (position & 1) != 0
    through = far * incoming
    across = far * outgoing
    for ref, is_second, forward, backward in (
        (mine_ref, second_block, partner_ref[:part, :], partner_ref[2 * part : 3 * part, :]),
        (back_ref, jnp.logical_not(second_block), pick(0), pick(2)),
    ):
        ref[:part, :] = jnp.where(is_second, through + forward, incoming)
        ref[part : 2 * part, :] = jnp.where(is_second, outgoing, across + backward)


def block_kernel(
    full, log_rates, residues, skip_weight, rate_ref, dealt, starts, scales, results, result_s
):
    tiles, modes, _ = rate_ref.shape
    filters = tiles * TILE_FILTERS
    steps = dealt.shape[2]
    half = modes // 2
    scaled = own_columns(residues[...], filters) * jnp.sqrt(
        jnp.exp(own_columns(log_rates[...], filters)) / full
    )
    scaled = per_channel(scaled, group_mask(filters, tiles * LANES))
    for n in range(tiles):
        scales[n] = scaled[:, n * LANES : (n + 1) * LANES]

    def tile(ct, _):
        step_decay = jnp.exp(-rate_ref[ct])
        sub_decay = jnp.exp(-rate_ref[ct] * float(steps))
        scale = scales[ct]
        weight = spread(skip_weight[pl.ds(ct, 1), :])
        for lo in range(0, modes, half):
            decay = [spread(step_decay[m : m + 1, :]) for m in range(lo, lo + half)]
            gains = [spread(scale[m : m + 1, :]) for m in range(lo, lo + half)]
            for way in range(2):
                state = [starts[ct, way, lo + m] for m in range(half)]
                if way:
                    state = sub_starts_back(
                        state, [spread(sub_decay[m : m + 1, :]) for m in range(lo, lo + half)]
                    )
                for i in range(steps - 1, -1, -1) if way else range(steps):
                    x = dealt[ct, way, i]
                    state = [d * s + x for d, s in zip(decay, state)]
                    terms = [g * s for g, s in zip(gains, state)]
                    terms.append(result_s[way, i] if lo > 0 else weight * x)
                    while len(terms) > 1:
                        odd = terms[len(terms) // 2 * 2 :]
                        terms = [a + b for a, b in zip(terms[::2], terms[1::2])] + odd
                    if lo > 0:
                        results[ct, way, pl.ds(i, SUB, stride=steps), :] = terms[0]
                    else:
                        result_s[way, i] = terms[0]
        return 0

    lax.fori_loop(0, tiles, tile, 0)


def reach_kernel(full, rate_ref, log_rates, residues, reach, factors):
    rates = jnp.exp(log_rates[...])
    scale_root = jnp.sqrt(jnp.float32(full))
    factor = jnp.sqrt(rates / full) / scale_root
    factors[0] = factor
    factors[1] = residues[...] * factor * 0.5
    factors[2] = residues[...] * factor * (rates / full)
    tiles, modes, _ = rate_ref.shape
    rows = reach.shape[3]
    lane = lax.broadcasted_iota(jnp.int32, (modes, LANES), 1)
    own_mode = lax.broadcasted_iota(jnp.int32, (modes, LANES), 0) == lax.rem(lane, modes)
    time = lax.broadcasted_iota(jnp.int32, (rows, LANES), 0).astype(F32)
    for ct in range(tiles):
        rate_row = jnp.sum(jnp.where(own_mode, rate_ref[ct], 0.0), axis=0, keepdims=True)
        for way, away in enumerate((time + 1.0, float(rows) - time)):
            high, low = split(jnp.exp(-rate_row * away))
            reach[ct, way, 0] = high
            reach[ct, way, 1] = low


def grads_kernel(is_own, edges, reach, scale_ref, results, key, values, upstream, *refs):
    outs, made, sems = refs[-7:-4], refs[-4:-1], refs[-1]
    tiles, modes, _ = scale_ref.shape
    share = tiles // 2
    part = share * modes
    second_half = lax.axis_index("ctx") & 1
    begin = (second_half if is_own else 1 - second_half) * share
    lane_filter = lax.div(lax.broadcasted_iota(jnp.int32, (modes, LANES), 1), GROUP_CH)
    copies = []
    for n in range(share):
        ct = begin + n
        parts = []
        for way in range(2):
            at = slice(way * part + n * modes, way * part + (n + 1) * modes)
            edge = scale_ref[ct] * edges[at, :]
            spaced = jnp.concatenate(
                [jnp.where(lane_filter == f, edge, 0.0) for f in range(TILE_FILTERS)], axis=0
            )
            parts.append(wide_dot(reach[ct, way, 0], reach[ct, way, 1], *split(spaced)))
        there = pl.ds(pl.multiple_of(ct * LANES, LANES), LANES)
        here = slice(n * LANES, (n + 1) * LANES)
        mixed_grad = results[ct, 1] + parts[1]
        for made_ref, factor, grad in zip(
            made, (upstream, values, key), (results[ct, 0] + parts[0], mixed_grad, mixed_grad)
        ):
            made_ref[:, here] = (factor[:, there].astype(F32) * grad).astype(made_ref.dtype)
        if n % 2 == 1:
            here = slice((n - 1) * LANES, (n + 1) * LANES)
            there = pl.ds(pl.multiple_of((ct - 1) * LANES, LANES), 2 * LANES)
            for k, (made_ref, out) in enumerate(zip(made, outs)):
                copies.append(
                    pltpu.make_async_copy(made_ref.at[:, here], out.at[:, there], sems.at[n // 2, k])
                )
                copies[-1].start()
    for copy in copies:
        copy.wait()


def final_kernel(
    full, factors, back, theirs, here, there, residue_grad, log_rate_grad, skip_grad
):
    _, modes, total_filters = factors.shape
    filters = here.shape[1] // 2
    group = lax.axis_index("grp")
    skip_rows = slice(back.shape[0] - skip_grad.shape[0], back.shape[0])
    skip_grad[...] = (back[skip_rows, :] + theirs[skip_rows, :]) / jnp.sqrt(jnp.float32(full))
    rows = [slice(n * modes, (n + 1) * modes) for n in range(3)]
    by_distance = [
        here[rows[0], :],
        there[rows[0], :],
        here[rows[1], :] + there[rows[2], :],
        here[rows[2], :] + there[rows[1], :],
    ]
    totals = []
    for g in range(total_filters // filters):
        total = by_distance[0]
        for k in range(1, len(by_distance)):
            total = jnp.where((group ^ k) == g, by_distance[k], total)
        totals.append(total)
    first_sum = jnp.concatenate([t[:, :filters] for t in totals], axis=1)
    second_sum = jnp.concatenate([t[:, filters:] for t in totals], axis=1)
    residue_grad[...] = factors[0] * first_sum
    log_rate_grad[...] = factors[1] * first_sum - factors[2] * second_sum


def flip(x, step, axis="ctx"):
    return lax.ppermute(x, axis, [(i, i ^ step) for i in range(lax.axis_size(axis))])


def after(x, *others):
    return lax.optimization_barrier((x, *others))[0]


def local(query_gate, key_gate, values, upstream, skip_weight, residues, log_rates):
    context = lax.axis_size("ctx")
    groups = lax.axis_size("grp")
    position = lax.axis_index("ctx")
    rows, channels = query_gate.shape
    total_filters, modes = residues.shape
    filters = channels // GROUP_CH
    tiles = channels // LANES
    full = rows * context
    part = tiles // 2 * modes
    tail = modes + tiles
    assert context >= 4 and context & (context - 1) == 0 and groups == 4
    vmem = pl.BlockSpec(memory_space=pltpu.VMEM)
    in_hbm = pl.BlockSpec(memory_space=pltpu.HBM)
    shape = lambda *dims: jax.ShapeDtypeStruct(dims, F32)
    params = pltpu.CompilerParams(vmem_limit_bytes=16 * 1024 * 1024)
    log_rates_t, residues_t = log_rates.T, residues.T

    def call(name, kernel, out_shape, operands, scratch=(), flops=0):
        return pl.pallas_call(
            kernel,
            out_shape=out_shape,
            in_specs=[vmem] * len(operands),
            out_specs=(vmem,) * len(out_shape),
            scratch_shapes=[pltpu.VMEM(dims, F32) for dims in scratch],
            compiler_params=params,
            cost_estimate=pl.CostEstimate(flops=flops, transcendentals=0, bytes_accessed=flops // 4),
            name=name,
        )(*operands)

    inputs = (log_rates_t, key_gate, values, upstream, query_gate)
    states, rate, mixed, carried, skip = pl.pallas_call(
        functools.partial(states_kernel, full),
        out_shape=(
            shape(8 * part, LANES),
            shape(tiles, modes, LANES),
            shape(tiles, rows, LANES),
            shape(tiles, rows, LANES),
            shape(tiles, LANES),
        ),
        in_specs=[in_hbm] * 5,
        out_specs=(vmem,) * 5,
        scratch_shapes=[
            pltpu.VMEM((modes, total_filters), F32),
            pltpu.VMEM((rows, channels), BF16),
            pltpu.VMEM((rows, channels), BF16),
            pltpu.VMEM((rows, channels), BF16),
            pltpu.VMEM((rows, channels), BF16),
            pltpu.VMEM((tiles, 4, TILE_FILTERS * modes, rows), BF16),
            pltpu.SemaphoreType.DMA((5,)),
        ],
        compiler_params=params,
        name="states",
    )(*(pltpu.with_memory_space_constraint(x, pltpu.HBM) for x in inputs))
    work = rows * channels * modes

    other_half = lax.dynamic_slice_in_dim(states, (1 - (position & 1)) * (4 * part), 4 * part, 0)
    partner = flip(other_half, 1)
    sums, starts, dealt = call(
        "within",
        within_kernel,
        (
            shape(tail, LANES),
            shape(tiles, 2, modes, SUB, LANES),
            shape(tiles, 2, rows // SUB, SUB, LANES),
        ),
        (rate, mixed, carried, skip),
        ((tiles, modes, LANES), (tiles, modes, LANES)),
        12 * work,
    )
    scale = results = reach = factors = None
    step = 1
    own, other, extra = states, after(partner, sums), (sums,)
    while 2 * step < context:
        is_last_next = 4 * step >= context
        own, borders, *send = call(
            "join",
            functools.partial(join_kernel, rows, step, is_last_next),
            (shape(4 * part + tail, LANES), shape(2 * part, LANES))
            + ((shape(2 * part + tail, LANES),) if is_last_next else ()),
            (rate, own, other, *extra),
        )
        other = flip(send[0] if send else own, 2 * step)
        if step == 1:
            scale, results = call(
                "block",
                functools.partial(block_kernel, full),
                (shape(tiles, modes, LANES), shape(tiles, 2, rows, LANES)),
                (
                    log_rates_t,
                    residues_t,
                    skip_weight.reshape(tiles, LANES),
                    after(rate, own),
                    dealt,
                    starts,
                ),
                ((2, rows // SUB, SUB, LANES),),
                8 * work,
            )
            other = after(other, results)
        if is_last_next:
            reach, factors = pl.pallas_call(
                functools.partial(reach_kernel, full),
                out_shape=(
                    jax.ShapeDtypeStruct((tiles, 2, 2, rows, LANES), BF16),
                    shape(3, modes, total_filters),
                ),
                in_specs=[vmem] * 3,
                out_specs=(vmem,) * 2,
                compiler_params=params,
                name="reach",
            )(after(rate, own), log_rates_t, residues_t)
            other = after(other, reach)
        extra = (borders,)
        step *= 2
    mine, back, modal = call(
        "last_join",
        functools.partial(last_join_kernel, rows, step),
        (shape(2 * part, LANES), shape(2 * part + tail, LANES), shape(modes, LANES)),
        (rate, own, other, borders, states, partner),
    )

    duo = jnp.concatenate([modal, flip(modal, 1, "grp")], axis=0)
    theirs = flip(back, 1)
    far = lax.ppermute(
        duo,
        ("ctx", "grp"),
        [(i, i ^ (groups + 2 if i & 1 else 2)) for i in range(context * groups)],
    )
    grad = jax.ShapeDtypeStruct((rows, channels), BF16)

    def grads(name, is_own, edges, before):
        operands = (edges, reach, scale, results, key_gate, values, upstream)
        return pl.pallas_call(
            functools.partial(grads_kernel, is_own),
            out_shape=(grad,) * 3,
            in_specs=[vmem] * len(operands) + [in_hbm] * len(before),
            out_specs=(in_hbm,) * 3,
            scratch_shapes=[pltpu.VMEM((rows, channels // 2), BF16)] * 3
            + [pltpu.SemaphoreType.DMA((tiles // 4, 3))],
            input_output_aliases={len(operands) + k: k for k in range(len(before))},
            compiler_params=params,
            cost_estimate=pl.CostEstimate(
                flops=2 * work, transcendentals=0, bytes_accessed=10 * rows * channels
            ),
            name=name,
        )(*operands, *before)

    outputs = grads("grads_own", True, after(mine, duo), ())
    theirs = after(theirs, *outputs)
    outputs = grads("grads_other", False, theirs[: 2 * part], outputs)
    query_grad, key_grad, value_grad = outputs
    here = jnp.concatenate([modal + theirs[2 * part : 2 * part + modes], far], axis=0)
    there = after(flip(here, 1, "grp"), *outputs)
    residue_grad, log_rate_grad, skip_grad = call(
        "final",
        functools.partial(final_kernel, full),
        (shape(modes, total_filters),) * 2 + (shape(tiles, LANES),),
        (factors, back, theirs, here, there),
    )
    return (
        query_grad,
        key_grad,
        value_grad,
        skip_grad.reshape(channels),
        residue_grad.T,
        log_rate_grad.T,
    )


def solution(mesh):
    placed = (
        P("ctx", "grp"),
        P("ctx", "grp"),
        P("ctx", "grp"),
        P("ctx", "grp"),
        P("grp"),
        P(),
        P(),
    )
    return jax.shard_map(
        local,
        mesh=mesh,
        in_specs=placed,
        out_specs=(P("ctx", "grp"), P("ctx", "grp"), P("ctx", "grp"), P("grp"), P(), P()),
        check_vma=False,
    )
```

```python
import functools

import jax
import jax.numpy as jnp
from jax import lax
from jax.experimental import pallas as pl
from jax.experimental.pallas import tpu as pltpu
from jax.sharding import PartitionSpec as P

GROUP_CH = 16
LANES = 128
SUB = 8
TILE_FILTERS = LANES // GROUP_CH
F32 = jnp.float32
BF16 = jnp.bfloat16


def own_columns(table, filters):
    total = table.shape[1]
    start = lax.axis_index("grp") * filters
    return pltpu.roll(table, lax.rem(total - start, total), 1)[:, :filters]


def group_mask(filters, channels):
    row = lax.broadcasted_iota(jnp.int32, (filters, channels), 0)
    col = lax.broadcasted_iota(jnp.int32, (filters, channels), 1)
    return jnp.where(row == lax.div(col, GROUP_CH), 1.0, 0.0).astype(F32)


def per_channel(table, mask):
    modes = table.shape[0]
    high, _ = split(table)
    middle, low = split(table - high.astype(F32))
    terms = jnp.dot(
        jnp.concatenate([high, middle, low], axis=0), mask.astype(BF16), preferred_element_type=F32
    )
    return terms[:modes] + (terms[modes : 2 * modes] + terms[2 * modes :])


def split(x):
    high = x.astype(BF16)
    return high, (x - high.astype(F32)).astype(BF16)


def wide_dot(a_high, a_low, b_high, b_low):
    return jnp.dot(
        jnp.concatenate([a_high, a_low, a_high], axis=1),
        jnp.concatenate([b_high, b_high, b_low], axis=0),
        preferred_element_type=F32,
    )


def spread(row):
    return jnp.broadcast_to(row, (SUB, LANES))


def sub_starts_back(ends, jumps):
    index = SUB - 1 - lax.broadcasted_iota(jnp.int32, (SUB, LANES), 0)
    out = []
    for end, jump in zip(ends, jumps):
        x = jnp.where(index == 0, 0.0, pltpu.roll(end, SUB - 1, 0))
        for n in (1, 2, 4):
            x = x + jnp.where(index >= n, jump, 0.0) * pltpu.roll(x, SUB - n, 0)
            jump = jump * jump
        out.append(x)
    return out


def fold_modes(products, modes):
    lane_filter = lax.div(lax.broadcasted_iota(jnp.int32, (modes, LANES), 1), GROUP_CH)
    parts = [
        jnp.where(lane_filter == f, products[f * modes : (f + 1) * modes, :], 0.0)
        for f in range(TILE_FILTERS)
    ]
    while len(parts) > 1:
        parts = [a + b for a, b in zip(parts[::2], parts[1::2])]
    return parts[0]


def states_kernel(
    full,
    log_rates_h,
    key_h,
    values_h,
    upstream_h,
    query_h,
    states,
    rate_out,
    mixed_out,
    carried_out,
    skip_out,
    rates_s,
    key,
    values,
    upstream,
    query,
    weight_s,
    sems,
):
    rows, channels = key.shape
    tiles = channels // LANES
    filters = channels // GROUP_CH
    modes = log_rates_h.shape[0]
    part = tiles // 2 * modes
    copies = [
        pltpu.make_async_copy(src, dst, sems.at[n])
        for n, (src, dst) in enumerate(
            (
                (log_rates_h, rates_s),
                (key_h, key),
                (values_h, values),
                (upstream_h, upstream),
                (query_h, query),
            )
        )
    ]
    for copy in copies:
        copy.start()
    copies[0].wait()
    step_rates = own_columns(jnp.exp(rates_s[...]), filters) * (1.0 / full)
    channel_rates = per_channel(step_rates, group_mask(filters, channels))
    time = lax.broadcasted_iota(jnp.int32, (modes, rows), 1).astype(F32)
    back_time = float(rows - 1) - time
    for f in range(filters):
        rate = jnp.broadcast_to(step_rates[:, f : f + 1], (modes, rows))
        ct, row = f // TILE_FILTERS, (f % TILE_FILTERS) * modes
        for way, away in enumerate((back_time, time)):
            high, low = split(jnp.exp(-rate * away))
            weight_s[ct, 2 * way, row : row + modes, :] = high
            weight_s[ct, 2 * way + 1, row : row + modes, :] = low
    for ct in range(tiles):
        rate_out[ct] = channel_rates[:, ct * LANES : (ct + 1) * LANES]
    forward = lax.broadcasted_iota(jnp.int32, (rows, LANES), 0).astype(F32)
    backward = float(rows - 1) - forward
    for copy in copies[1:]:
        copy.wait()
    for ct in range(tiles):
        lanes = slice(ct * LANES, (ct + 1) * LANES)
        mixed = key[:, lanes].astype(F32) * values[:, lanes].astype(F32)
        carried = upstream[:, lanes].astype(F32) * query[:, lanes].astype(F32)
        mixed_out[ct] = mixed
        carried_out[ct] = carried
        base = ct // (tiles // 2) * 4 * part + ct % (tiles // 2) * modes
        for way, (x, away) in enumerate(((mixed, backward), (carried, forward))):
            both = jnp.concatenate([x, x * away], axis=1)
            products = wide_dot(weight_s[ct, 2 * way], weight_s[ct, 2 * way + 1], *split(both))
            for n in range(2):
                at = base + (2 * way + n) * part
                states[at : at + modes, :] = fold_modes(products[:, n * LANES : (n + 1) * LANES], modes)
        skip_out[ct : ct + 1, :] = jnp.sum(mixed * carried, axis=0, keepdims=True)


def by_filter(firsts, seconds, first_filter, filters):
    modes = firsts[0].shape[0]
    both = jnp.concatenate([jnp.concatenate(v, axis=1) for v in (firsts, seconds)], axis=0)
    channels = both.shape[1]
    row = lax.broadcasted_iota(jnp.int32, (filters, channels), 0)
    col = lax.broadcasted_iota(jnp.int32, (filters, channels), 1)
    mask = jnp.where(row == first_filter + lax.div(col, GROUP_CH), 1.0, 0.0).astype(BF16)
    high, rest = split(both)
    middle, low = split(both - high.astype(F32))
    summed = lax.dot_general(
        jnp.concatenate([high, middle, low], axis=0),
        mask,
        (((1,), (1,)), ((), ())),
        preferred_element_type=F32,
    )
    summed = summed[: 2 * modes] + summed[2 * modes : 4 * modes] + summed[4 * modes :]
    return jnp.concatenate([summed[:modes], summed[modes:]], axis=1)


def sub_spans(x_ref, decay, reverse):
    steps = x_ref.shape[0]
    state = slope = None
    for i in range(steps - 1, -1, -1) if reverse else range(steps):
        x = x_ref[i]
        if state is None:
            state = [x] * len(decay)
            continue
        moved = [d * s for d, s in zip(decay, state)]
        slope = moved if slope is None else [d * t + a for d, t, a in zip(decay, slope, moved)]
        state = [a + x for a in moved]
    return state, slope


def sub_starts_both(ends, slopes, jumps, span):
    index = lax.broadcasted_iota(jnp.int32, (SUB, LANES), 0)
    starts, start_slopes = [], []
    for end, slope, jump in zip(ends, slopes, jumps):
        x = jnp.where(index == 0, 0.0, pltpu.roll(end, 1, 0))
        y = jnp.where(index == 0, 0.0, pltpu.roll(slope, 1, 0))
        for n in (1, 2, 4):
            hop = jnp.where(index >= n, jump, 0.0)
            x_far = pltpu.roll(x, n, 0)
            y = y + hop * (pltpu.roll(y, n, 0) + float(n * span) * x_far)
            x = x + hop * x_far
            jump = jump * jump
        starts.append(x)
        start_slopes.append(y)
    return starts, start_slopes


def within_kernel(rate_ref, mixed_ref, carried_ref, skip, sums, starts, dealt, first_s, second_s):
    tiles, rows, _ = mixed_ref.shape
    modes = rate_ref.shape[1]
    steps = rows // SUB
    half = modes // 2
    total = lambda v: jnp.sum(v, axis=0, keepdims=True)

    def tile(ct, _):
        rate = rate_ref[ct]
        step_decay = jnp.exp(-rate)
        sub_decay = jnp.exp(-rate * float(steps))
        firsts, seconds = [], []
        for i in range(steps):
            for way, ref in enumerate((mixed_ref, carried_ref)):
                dealt[ct, way, i] = ref[ct, pl.ds(i, SUB, stride=steps), :]
        for lo in range(0, modes, half):
            decay = [spread(step_decay[m : m + 1, :]) for m in range(lo, lo + half)]
            jumps = [spread(sub_decay[m : m + 1, :]) for m in range(lo, lo + half)]
            ends, end_slopes = sub_spans(dealt.at[ct, 0], decay, False)
            before, before_slopes = sub_starts_both(ends, end_slopes, jumps, steps)
            behind, behind_slopes = sub_spans(dealt.at[ct, 1], decay, True)
            for m in range(half):
                starts[ct, 0, lo + m] = before[m]
                starts[ct, 1, lo + m] = behind[m]
                reached = decay[m] * before[m]
                firsts.append(total(reached * behind[m]))
                seconds.append(
                    total(
                        (decay[m] * before_slopes[m]) * behind[m]
                        + reached * (behind[m] + behind_slopes[m])
                    )
                )
        x = [dealt[ct, 0, i] for i in range(steps)]
        c = [dealt[ct, 1, i] for i in range(steps)]
        first = second = jnp.zeros((modes, LANES), F32)
        for lag in range(steps - 1, -1, -1):
            terms = [c[i + lag] * x[i] for i in range(steps - lag)]
            while len(terms) > 1:
                odd = terms[len(terms) // 2 * 2 :]
                terms = [a + b for a, b in zip(terms[::2], terms[1::2])] + odd
            moved = step_decay * first
            second = step_decay * second + moved
            first = moved + total(terms[0])
        first_s[ct] = first + jnp.concatenate(firsts, axis=0)
        second_s[ct] = second + jnp.concatenate(seconds, axis=0)
        return 0

    lax.fori_loop(0, tiles, tile, 0)
    packet = by_filter(
        [first_s[ct] for ct in range(tiles)],
        [second_s[ct] for ct in range(tiles)],
        0,
        tiles * TILE_FILTERS,
    )
    sums[:modes, :] = packet
    sums[modes:, :] = skip[...]


def spans_join(own, other, rate, upper, span):
    low = [jnp.where(upper, o, w) for w, o in zip(own, other)]
    high = [jnp.where(upper, w, o) for w, o in zip(own, other)]
    decay = jnp.exp(-rate)
    first = decay * (low[0] * high[2])
    second = decay * (low[1] * high[2] + low[0] * (high[2] + high[3]))
    far = jnp.exp(-rate * float(span))
    joined = (
        far * low[0] + high[0],
        far * (low[1] + float(span) * low[0]) + high[1],
        low[2] + far * high[2],
        low[3] + far * (high[3] + float(span) * high[2]),
    )
    return joined, first, second


def border_sums(first, second, tiles, modes):
    cut = lambda v: [v[n * modes : (n + 1) * modes, :] for n in range(tiles // 2)]
    begin = (lax.axis_index("ctx") & 1) * (tiles // 2 * TILE_FILTERS)
    return by_filter(cut(first), cut(second), begin, tiles * TILE_FILTERS)


def half_rates(rate_ref):
    tiles, modes, _ = rate_ref.shape
    begin = (lax.axis_index("ctx") & 1) * (tiles // 2)
    return jnp.concatenate([rate_ref[begin + n] for n in range(tiles // 2)], axis=0)


def join_kernel(rows, step, is_last_next, rate_ref, own_ref, other_ref, *refs):
    tiles, modes, _ = rate_ref.shape
    part = tiles // 2 * modes
    if step == 1:
        sums_ref, joined_ref, borders_ref, *send = refs
        begin = (lax.axis_index("ctx") & 1) * (4 * part)
        own = [own_ref[pl.ds(pl.multiple_of(begin + q * part, part), part), :] for q in range(4)]
        sums = sums_ref[...]
    else:
        old_borders, joined_ref, borders_ref, *send = refs
        own = [own_ref[q * part : (q + 1) * part, :] for q in range(4)]
        sums = own_ref[4 * part :, :] + other_ref[4 * part :, :]
    other = [other_ref[q * part : (q + 1) * part, :] for q in range(4)]
    position = lax.axis_index("ctx")
    upper = (position & step) != 0
    rate = half_rates(rate_ref)
    joined, first, second = spans_join(own, other, rate, upper, rows * step)
    for q in range(4):
        joined_ref[q * part : (q + 1) * part, :] = joined[q]
    sums = jnp.concatenate([sums[:modes] + border_sums(first, second, tiles, modes), sums[modes:]], axis=0)
    joined_ref[4 * part :, :] = sums
    if step == 1:
        borders_ref[...] = jnp.zeros_like(borders_ref)
    else:
        borders_ref[...] = add_borders(
            rows, step, rate, [old_borders[:part, :], old_borders[part:, :]], other[0], other[2]
        )
    if is_last_next:
        next_upper = (position & (2 * step)) != 0
        for q in range(2):
            send[0][q * part : (q + 1) * part, :] = jnp.where(next_upper, joined[2 + q], joined[q])
        send[0][2 * part :, :] = sums


def add_borders(rows, step, rate, borders, forward, backward):
    position = lax.axis_index("ctx")
    upper = (position & step) != 0
    before = ((position & (step - 1)) >> 1).astype(F32) * float(2 * rows)
    behind = float(rows * (step - 2)) - before
    return jnp.concatenate(
        [
            borders[0] + jnp.where(upper, jnp.exp(-rate * before) * forward, 0.0),
            borders[1] + jnp.where(upper, 0.0, jnp.exp(-rate * behind) * backward),
        ],
        axis=0,
    )


def last_join_kernel(
    rows, step, rate_ref, own_ref, other_ref, borders_ref, states_ref, partner_ref, mine_ref, back_ref, modal_ref
):
    tiles, modes, _ = rate_ref.shape
    part = tiles // 2 * modes
    position = lax.axis_index("ctx")
    upper = (position & step) != 0
    rate = half_rates(rate_ref)
    own = [own_ref[q * part : (q + 1) * part, :] for q in range(4)]
    other = [other_ref[q * part : (q + 1) * part, :] for q in range(2)]
    _, first, second = spans_join(own, other + other, rate, upper, rows * step)
    sums = own_ref[4 * part :, :] + other_ref[2 * part :, :]
    modal = sums[:modes] + border_sums(first, second, tiles, modes)
    modal_ref[...] = modal
    back_ref[2 * part : 2 * part + modes, :] = modal
    back_ref[2 * part + modes :, :] = sums[modes:]
    borders = add_borders(
        rows, step, rate, [borders_ref[:part, :], borders_ref[part:, :]], other[0], other[0]
    )
    incoming, outgoing = borders[:part], borders[part:]
    far = jnp.exp(-rate * float(rows))
    begin = (position & 1) * (4 * part)
    pick = lambda q: states_ref[pl.ds(pl.multiple_of(begin + q * part, part), part), :]
    second_block = (position & 1) != 0
    through = far * incoming
    across = far * outgoing
    for ref, is_second, forward, backward in (
        (mine_ref, second_block, partner_ref[:part, :], partner_ref[2 * part : 3 * part, :]),
        (back_ref, jnp.logical_not(second_block), pick(0), pick(2)),
    ):
        ref[:part, :] = jnp.where(is_second, through + forward, incoming)
        ref[part : 2 * part, :] = jnp.where(is_second, outgoing, across + backward)


def block_kernel(
    full, log_rates, residues, skip_weight, rate_ref, dealt, starts, scales, results, result_s
):
    tiles, modes, _ = rate_ref.shape
    filters = tiles * TILE_FILTERS
    steps = dealt.shape[2]
    half = modes // 2
    scaled = own_columns(residues[...], filters) * jnp.sqrt(
        jnp.exp(own_columns(log_rates[...], filters)) / full
    )
    scaled = per_channel(scaled, group_mask(filters, tiles * LANES))
    for n in range(tiles):
        scales[n] = scaled[:, n * LANES : (n + 1) * LANES]

    def tile(ct, _):
        step_decay = jnp.exp(-rate_ref[ct])
        sub_decay = jnp.exp(-rate_ref[ct] * float(steps))
        scale = scales[ct]
        weight = spread(skip_weight[pl.ds(ct, 1), :])
        for lo in range(0, modes, half):
            decay = [spread(step_decay[m : m + 1, :]) for m in range(lo, lo + half)]
            gains = [spread(scale[m : m + 1, :]) for m in range(lo, lo + half)]
            for way in range(2):
                state = [starts[ct, way, lo + m] for m in range(half)]
                if way:
                    state = sub_starts_back(
                        state, [spread(sub_decay[m : m + 1, :]) for m in range(lo, lo + half)]
                    )
                for i in range(steps - 1, -1, -1) if way else range(steps):
                    x = dealt[ct, way, i]
                    state = [d * s + x for d, s in zip(decay, state)]
                    terms = [g * s for g, s in zip(gains, state)]
                    terms.append(result_s[way, i] if lo > 0 else weight * x)
                    while len(terms) > 1:
                        odd = terms[len(terms) // 2 * 2 :]
                        terms = [a + b for a, b in zip(terms[::2], terms[1::2])] + odd
                    if lo > 0:
                        results[ct, way, pl.ds(i, SUB, stride=steps), :] = terms[0]
                    else:
                        result_s[way, i] = terms[0]
        return 0

    lax.fori_loop(0, tiles, tile, 0)


def reach_kernel(full, rate_ref, log_rates, residues, reach, factors):
    rates = jnp.exp(log_rates[...])
    scale_root = jnp.sqrt(jnp.float32(full))
    factor = jnp.sqrt(rates / full) / scale_root
    factors[0] = factor
    factors[1] = residues[...] * factor * 0.5
    factors[2] = residues[...] * factor * (rates / full)
    tiles, modes, _ = rate_ref.shape
    rows = reach.shape[3]
    lane = lax.broadcasted_iota(jnp.int32, (modes, LANES), 1)
    own_mode = lax.broadcasted_iota(jnp.int32, (modes, LANES), 0) == lax.rem(lane, modes)
    time = lax.broadcasted_iota(jnp.int32, (rows, LANES), 0).astype(F32)
    for ct in range(tiles):
        rate_row = jnp.sum(jnp.where(own_mode, rate_ref[ct], 0.0), axis=0, keepdims=True)
        for way, away in enumerate((time + 1.0, float(rows) - time)):
            high, low = split(jnp.exp(-rate_row * away))
            reach[ct, way, 0] = high
            reach[ct, way, 1] = low


def grads_kernel(is_own, edges, reach, scale_ref, results, key, values, upstream, *refs):
    outs, made, sems = refs[-7:-4], refs[-4:-1], refs[-1]
    tiles, modes, _ = scale_ref.shape
    share = tiles // 2
    part = share * modes
    second_half = lax.axis_index("ctx") & 1
    begin = (second_half if is_own else 1 - second_half) * share
    lane_filter = lax.div(lax.broadcasted_iota(jnp.int32, (modes, LANES), 1), GROUP_CH)
    copies = []
    for n in range(share):
        ct = begin + n
        parts = []
        for way in range(2):
            at = slice(way * part + n * modes, way * part + (n + 1) * modes)
            edge = scale_ref[ct] * edges[at, :]
            spaced = jnp.concatenate(
                [jnp.where(lane_filter == f, edge, 0.0) for f in range(TILE_FILTERS)], axis=0
            )
            parts.append(wide_dot(reach[ct, way, 0], reach[ct, way, 1], *split(spaced)))
        there = pl.ds(pl.multiple_of(ct * LANES, LANES), LANES)
        here = slice(n * LANES, (n + 1) * LANES)
        mixed_grad = results[ct, 1] + parts[1]
        for made_ref, factor, grad in zip(
            made, (upstream, values, key), (results[ct, 0] + parts[0], mixed_grad, mixed_grad)
        ):
            made_ref[:, here] = (factor[:, there].astype(F32) * grad).astype(made_ref.dtype)
        if n % 2 == 1:
            here = slice((n - 1) * LANES, (n + 1) * LANES)
            there = pl.ds(pl.multiple_of((ct - 1) * LANES, LANES), 2 * LANES)
            for k, (made_ref, out) in enumerate(zip(made, outs)):
                copies.append(
                    pltpu.make_async_copy(made_ref.at[:, here], out.at[:, there], sems.at[n // 2, k])
                )
                copies[-1].start()
    for copy in copies:
        copy.wait()


def final_kernel(
    full, factors, back, theirs, here, there, residue_grad, log_rate_grad, skip_grad
):
    _, modes, total_filters = factors.shape
    filters = here.shape[1] // 2
    group = lax.axis_index("grp")
    skip_rows = slice(back.shape[0] - skip_grad.shape[0], back.shape[0])
    skip_grad[...] = (back[skip_rows, :] + theirs[skip_rows, :]) / jnp.sqrt(jnp.float32(full))
    rows = [slice(n * modes, (n + 1) * modes) for n in range(3)]
    by_distance = [
        here[rows[0], :],
        there[rows[0], :],
        here[rows[1], :] + there[rows[2], :],
        here[rows[2], :] + there[rows[1], :],
    ]
    totals = []
    for g in range(total_filters // filters):
        total = by_distance[0]
        for k in range(1, len(by_distance)):
            total = jnp.where((group ^ k) == g, by_distance[k], total)
        totals.append(total)
    first_sum = jnp.concatenate([t[:, :filters] for t in totals], axis=1)
    second_sum = jnp.concatenate([t[:, filters:] for t in totals], axis=1)
    residue_grad[...] = factors[0] * first_sum
    log_rate_grad[...] = factors[1] * first_sum - factors[2] * second_sum


def flip(x, step, axis="ctx"):
    return lax.ppermute(x, axis, [(i, i ^ step) for i in range(lax.axis_size(axis))])


def after(x, *others):
    return lax.optimization_barrier((x, *others))[0]


def local(query_gate, key_gate, values, upstream, skip_weight, residues, log_rates):
    context = lax.axis_size("ctx")
    groups = lax.axis_size("grp")
    position = lax.axis_index("ctx")
    rows, channels = query_gate.shape
    total_filters, modes = residues.shape
    filters = channels // GROUP_CH
    tiles = channels // LANES
    full = rows * context
    part = tiles // 2 * modes
    tail = modes + tiles
    assert context >= 4 and context & (context - 1) == 0 and groups == 4
    vmem = pl.BlockSpec(memory_space=pltpu.VMEM)
    in_hbm = pl.BlockSpec(memory_space=pltpu.HBM)
    shape = lambda *dims: jax.ShapeDtypeStruct(dims, F32)
    params = pltpu.CompilerParams(vmem_limit_bytes=16 * 1024 * 1024)
    log_rates_t, residues_t = log_rates.T, residues.T

    def call(name, kernel, out_shape, operands, scratch=(), flops=0):
        return pl.pallas_call(
            kernel,
            out_shape=out_shape,
            in_specs=[vmem] * len(operands),
            out_specs=(vmem,) * len(out_shape),
            scratch_shapes=[pltpu.VMEM(dims, F32) for dims in scratch],
            compiler_params=params,
            cost_estimate=pl.CostEstimate(flops=flops, transcendentals=0, bytes_accessed=flops // 4),
            name=name,
        )(*operands)

    inputs = (log_rates_t, key_gate, values, upstream, query_gate)
    states, rate, mixed, carried, skip = pl.pallas_call(
        functools.partial(states_kernel, full),
        out_shape=(
            shape(8 * part, LANES),
            shape(tiles, modes, LANES),
            shape(tiles, rows, LANES),
            shape(tiles, rows, LANES),
            shape(tiles, LANES),
        ),
        in_specs=[in_hbm] * 5,
        out_specs=(vmem,) * 5,
        scratch_shapes=[
            pltpu.VMEM((modes, total_filters), F32),
            pltpu.VMEM((rows, channels), BF16),
            pltpu.VMEM((rows, channels), BF16),
            pltpu.VMEM((rows, channels), BF16),
            pltpu.VMEM((rows, channels), BF16),
            pltpu.VMEM((tiles, 4, TILE_FILTERS * modes, rows), BF16),
            pltpu.SemaphoreType.DMA((5,)),
        ],
        compiler_params=params,
        name="states",
    )(*(pltpu.with_memory_space_constraint(x, pltpu.HBM) for x in inputs))
    work = rows * channels * modes

    other_half = lax.dynamic_slice_in_dim(states, (1 - (position & 1)) * (4 * part), 4 * part, 0)
    partner = flip(other_half, 1)
    sums, starts, dealt = call(
        "within",
        within_kernel,
        (
            shape(tail, LANES),
            shape(tiles, 2, modes, SUB, LANES),
            shape(tiles, 2, rows // SUB, SUB, LANES),
        ),
        (rate, mixed, carried, skip),
        ((tiles, modes, LANES), (tiles, modes, LANES)),
        12 * work,
    )
    scale = results = reach = factors = None
    step = 1
    own, other, extra = states, after(partner, sums), (sums,)
    while 2 * step < context:
        is_last_next = 4 * step >= context
        own, borders, *send = call(
            "join",
            functools.partial(join_kernel, rows, step, is_last_next),
            (shape(4 * part + tail, LANES), shape(2 * part, LANES))
            + ((shape(2 * part + tail, LANES),) if is_last_next else ()),
            (rate, own, other, *extra),
        )
        other = flip(send[0] if send else own, 2 * step)
        if step == 1:
            scale, results = call(
                "block",
                functools.partial(block_kernel, full),
                (shape(tiles, modes, LANES), shape(tiles, 2, rows, LANES)),
                (
                    log_rates_t,
                    residues_t,
                    skip_weight.reshape(tiles, LANES),
                    after(rate, own),
                    dealt,
                    starts,
                ),
                ((2, rows // SUB, SUB, LANES),),
                8 * work,
            )
            other = after(other, results)
        if is_last_next:
            reach, factors = pl.pallas_call(
                functools.partial(reach_kernel, full),
                out_shape=(
                    jax.ShapeDtypeStruct((tiles, 2, 2, rows, LANES), BF16),
                    shape(3, modes, total_filters),
                ),
                in_specs=[vmem] * 3,
                out_specs=(vmem,) * 2,
                compiler_params=params,
                name="reach",
            )(after(rate, own), log_rates_t, residues_t)
            other = after(other, reach)
        extra = (borders,)
        step *= 2
    mine, back, modal = call(
        "last_join",
        functools.partial(last_join_kernel, rows, step),
        (shape(2 * part, LANES), shape(2 * part + tail, LANES), shape(modes, LANES)),
        (rate, own, other, borders, states, partner),
    )

    duo = jnp.concatenate([modal, flip(modal, 1, "grp")], axis=0)
    theirs = flip(back, 1)
    far = lax.ppermute(
        duo,
        ("ctx", "grp"),
        [(i, i ^ (groups + 2 if i & 1 else 2)) for i in range(context * groups)],
    )
    grad = jax.ShapeDtypeStruct((rows, channels), BF16)

    def grads(name, is_own, edges, before):
        operands = (edges, reach, scale, results, key_gate, values, upstream)
        return pl.pallas_call(
            functools.partial(grads_kernel, is_own),
            out_shape=(grad,) * 3,
            in_specs=[vmem] * len(operands) + [in_hbm] * len(before),
            out_specs=(in_hbm,) * 3,
            scratch_shapes=[pltpu.VMEM((rows, channels // 2), BF16)] * 3
            + [pltpu.SemaphoreType.DMA((tiles // 4, 3))],
            input_output_aliases={len(operands) + k: k for k in range(len(before))},
            compiler_params=params,
            cost_estimate=pl.CostEstimate(
                flops=2 * work, transcendentals=0, bytes_accessed=10 * rows * channels
            ),
            name=name,
        )(*operands, *before)

    outputs = grads("grads_own", True, after(mine, duo), ())
    theirs = after(theirs, *outputs)
    outputs = grads("grads_other", False, theirs[: 2 * part], outputs)
    query_grad, key_grad, value_grad = outputs
    here = jnp.concatenate([modal + theirs[2 * part : 2 * part + modes], far], axis=0)
    there = after(flip(here, 1, "grp"), *outputs)
    residue_grad, log_rate_grad, skip_grad = call(
        "final",
        functools.partial(final_kernel, full),
        (shape(modes, total_filters),) * 2 + (shape(tiles, LANES),),
        (factors, back, theirs, here, there),
    )
    return (
        query_grad,
        key_grad,
        value_grad,
        skip_grad.reshape(channels),
        residue_grad.T,
        log_rate_grad.T,
    )


def solution(mesh):
    placed = (
        P("ctx", "grp"),
        P("ctx", "grp"),
        P("ctx", "grp"),
        P("ctx", "grp"),
        P("grp"),
        P(),
        P(),
    )
    return jax.shard_map(
        local,
        mesh=mesh,
        in_specs=placed,
        out_specs=(P("ctx", "grp"), P("ctx", "grp"), P("ctx", "grp"), P("grp"), P(), P()),
        check_vma=False,
    )
```
